256 devices in a mesh: tm: 4 (over x_hi, core), row: 64 (over y, z, x_lo).
Axes of the slice: x: 4 (x_hi: 2, x_lo: 2; x = x_hi * 2 + x_lo), y: 4, z: 8, core: 2. Of those that a mesh axis runs over, the one named last changes fastest.
Arguments:
- event_counts: int32 [4, 4096, 4096], P('tm', 'row'), may hold values from 0 to 8
- latent_mean: float32 [4, 4096, 4096], P('tm', 'row'), may hold values from -3 to 3
- latent_var: float32 [4, 4096, 4096], P('tm', 'row'), may hold values from 0.05 to 0.6
- eigen_basis: bfloat16 [4096, 4096], P('row', 'tm'), may hold values from -0.09375 to 0.09375
- spectrum: float32 [4096], replicated, may hold values from 0.2 to 2
- correlation: float32 [1], replicated, may hold values from 0.3 to 0.9
- whitened: float32 [4, 64, 16, 4, 4096], P(None, 'row', None, None, 'tm'), may hold values from -6 to 6
Outputs:
- gradient: float32 [4, 64, 16, 4, 4096], P(None, 'row', None, None, 'tm')
The draws below stay inside these ranges and needn't reach their ends.
All inputs are finite; a program needn't handle non-finite values.
Results may differ from the reference program's by a relative error of at most 0.0045.
Values may be sent and summed in bfloat16 or wider, within the bound.
No kernel may reach another device: no remote copies, remote signals or barrier semaphores. Data moves between devices by JAX's collectives and lax.ppermute only.
A program may use at most 64 MiB of HBM per device.

```python
import math
import jax
import jax.numpy as jnp
from jax import lax

N = 4096
TS = 4
QB = 16
N_TM = 4
N_ROW = 64


def set_ends(values, rng, smallest, top_value):
    index_at = [jax.random.randint(jax.random.fold_in(rng, axis), (), 0, length) for axis, length in enumerate(values.shape)]
    longest = values.shape.index(max(values.shape))
    next_to = index_at[:longest] + [(index_at[longest] + 1) % values.shape[longest]] + index_at[longest + 1:]
    return values.at[tuple(index_at)].set(smallest).at[tuple(next_to)].set(top_value)


def shard_levels(rng, extent, split, least, largest):
    def one(dim, shards_of):
        draws = jax.random.uniform(jax.random.fold_in(jax.random.fold_in(rng, 6), dim), (shards_of,), jnp.float32, least / len(split), largest / len(split))
        return jnp.repeat(jnp.exp(draws), extent[dim] // shards_of).reshape((-1,) + (1,) * (len(extent) - dim - 1))

    level = one(*split[0])
    for cut in split[1:]:
        level = level * one(*cut)
    return level


def bell_draw(stream_key, dims, width, reach, shards=(), kind=jnp.bfloat16):
    factor_of = shard_levels(stream_key, dims, shards, -0.22, 0.18) if shards else 1.0
    array = jax.random.normal(stream_key, dims, jnp.float32) * width * factor_of
    return jnp.minimum(jnp.maximum(array, -reach), reach).astype(kind)


def setup_inputs(seed: int = 0) -> dict:
    key_list = jax.random.split(jax.random.key(seed), 8)
    event_counts = set_ends(jax.random.randint(key_list[0], (TS, N, N), 0, 9), jax.random.fold_in(key_list[0], 1), 0, 8).astype(jnp.int32)
    latent_mean = bell_draw(key_list[1], (TS, N, N), 0.7, 3.0, ((0, 4), (1, 64)), jnp.float32)
    latent_var = jnp.clip(jnp.exp(math.log(0.6) - 2.4849067 * jax.random.uniform(key_list[2], (TS, N, N), jnp.float32) ** shard_levels(key_list[2], (TS, N, N), ((0, 4), (1, 64)), -0.2, 0.2)), 0.05, 0.6)
    eigen_basis = bell_draw(key_list[3], (N, N), N ** -0.5, 0.09375, ((0, 64), (1, 4)))
    spectrum = jnp.clip(jnp.exp(jax.random.uniform(key_list[4], (N,), jnp.float32, math.log(0.2), math.log(2.0))), 0.2, 2.0)
    correlation = jnp.clip(jax.random.uniform(key_list[5], (1,), jnp.float32, 0.3, 0.9), 0.3, 0.9)
    whitened = bell_draw(key_list[6], (N_TM, N_ROW, QB, TS, N), 1.0, 6.0, ((1, 64), (4, 4)), jnp.float32)
    return dict(event_counts=event_counts, latent_mean=latent_mean, latent_var=latent_var, eigen_basis=eigen_basis, spectrum=spectrum, correlation=correlation, whitened=whitened)


HERMITE_NODES = (-2.0201828704560856, -0.9585724646138185, 0.0, 0.9585724646138185, 2.0201828704560856)
HERMITE_WEIGHTS = (0.019953242059045913, 0.3936193231522412, 0.9453087204829419, 0.3936193231522412, 0.019953242059045913)

def moments(event_counts, latent_mean, latent_var):
    spread = jnp.sqrt(2.0 * latent_var)
    normal = 1.0 / math.sqrt(math.pi)
    points = [latent_mean + spread * abscissa for abscissa in HERMITE_NODES]
    rate_points = [jnp.exp(value) for value in points]
    mean_rate = sum((weight * normal * value for weight, value in zip(HERMITE_WEIGHTS, rate_points)))
    covariance = sum((weight * normal * (node_value - latent_mean) * (value - mean_rate) for weight, node_value, value in zip(HERMITE_WEIGHTS, points, rate_points)))
    rate_var = sum((weight * normal * (value - mean_rate) * (value - mean_rate) for weight, value in zip(HERMITE_WEIGHTS, rate_points)))
    slope_gain = covariance / latent_var
    noise_var = rate_var - slope_gain * covariance + mean_rate
    return slope_gain * (event_counts.astype(latent_mean.dtype) - mean_rate) / noise_var

def time_factor(correlation, total):
    later = jnp.arange(total)[:, None]
    earlier = jnp.arange(total)[None, :]
    distance = jnp.maximum(later - earlier, 0).astype(correlation.dtype)
    lower = jnp.where(later >= earlier, jnp.power(correlation, distance), jnp.zeros_like(distance))
    column_scale = jnp.where(earlier == 0, jnp.ones_like(distance), jnp.sqrt(1.0 - correlation * correlation) * jnp.ones_like(distance))
    return lower * column_scale

def reference(event_counts, latent_mean, latent_var, eigen_basis, spectrum, correlation, whitened):
    pseudo = moments(event_counts, latent_mean, latent_var).astype(jnp.bfloat16)
    factor = time_factor(correlation[0], TS)
    flat = pseudo.reshape(TS, N * N).astype(factor.dtype)
    mixed_field = jnp.dot(factor.T, flat, precision=lax.Precision.HIGHEST).reshape(TS, N, N).astype(jnp.bfloat16)

    def transform(field):
        partial_y = jnp.dot(field, eigen_basis, preferred_element_type=jnp.float32).astype(jnp.bfloat16)
        return jnp.dot(partial_y.T, eigen_basis, preferred_element_type=jnp.float32)
    mode_values = lax.map(transform, mixed_field)
    root_scale = jnp.sqrt(spectrum)
    scaled = root_scale[None, :, None] * root_scale[None, None, :] * mode_values
    gradient = jnp.transpose(scaled, (1, 0, 2)) - whitened.reshape(N, TS, N)
    return gradient.reshape(N_TM, N_ROW, QB, TS, N)
```

```python
import math

import jax
import jax.numpy as jnp
from jax import lax
from jax.experimental import pallas as pl
from jax.experimental.pallas import tpu as pltpu
from jax.sharding import Mesh
from jax.sharding import PartitionSpec as P

TM = ("hi", "core")
ROW = ("y", "z", "lo")
RING = ("hi", "lo")

HERMITE_NODES = (
    -2.0201828704560856,
    -0.9585724646138185,
    0.0,
    0.9585724646138185,
    2.0201828704560856,
)
HERMITE_WEIGHTS = (
    0.019953242059045913,
    0.3936193231522412,
    0.9453087204829419,
    0.3936193231522412,
    0.019953242059045913,
)
VMEM = pl.BlockSpec(memory_space=pltpu.VMEM)
SMEM = pl.BlockSpec(memory_space=pltpu.SMEM)


def moments(event_counts, latent_mean, latent_var):
    spread = jnp.sqrt(2.0 * latent_var)
    normal = 1.0 / math.sqrt(math.pi)
    points = [latent_mean + spread * abscissa for abscissa in HERMITE_NODES]
    rate_points = [jnp.exp(value) for value in points]
    mean_rate = sum(
        (weight * normal * value for weight, value in zip(HERMITE_WEIGHTS, rate_points))
    )
    covariance = sum(
        (
            weight * normal * (node_value - latent_mean) * (value - mean_rate)
            for weight, node_value, value in zip(HERMITE_WEIGHTS, points, rate_points)
        )
    )
    rate_var = sum(
        (
            weight * normal * (value - mean_rate) * (value - mean_rate)
            for weight, value in zip(HERMITE_WEIGHTS, rate_points)
        )
    )
    slope_gain = covariance / latent_var
    noise_var = rate_var - slope_gain * covariance + mean_rate
    return slope_gain * (event_counts.astype(latent_mean.dtype) - mean_rate) / noise_var


def time_factor(correlation, total):
    later = jnp.arange(total)[:, None]
    earlier = jnp.arange(total)[None, :]
    distance = jnp.maximum(later - earlier, 0).astype(correlation.dtype)
    lower = jnp.where(later >= earlier, jnp.power(correlation, distance), jnp.zeros_like(distance))
    column_scale = jnp.where(
        earlier == 0,
        jnp.ones_like(distance),
        jnp.sqrt(1.0 - correlation * correlation) * jnp.ones_like(distance),
    )
    return lower * column_scale


def shifted(array, axis, step):
    size = lax.axis_size(axis)
    return lax.ppermute(array, axis, [(k, (k + step) % size) for k in range(size)])


def copies_along(array, axis):
    size = lax.axis_size(axis)
    return lax.all_to_all(
        jnp.broadcast_to(array[None], (size, *array.shape)), axis, 0, 0, tiled=True
    )


def split_kernel(basis_ref, halves_ref):
    source = lax.broadcasted_iota(jnp.int32, (256, 128), 0)
    target = lax.broadcasted_iota(jnp.int32, (256, 128), 1)
    for half in range(2):
        chosen = (source == (target // 8) * 16 + half * 8 + target % 8).astype(jnp.bfloat16)
        for block in range(basis_ref.shape[1] // 256):
            moved = jnp.dot(
                basis_ref[:, block * 256 : block * 256 + 256],
                chosen,
                preferred_element_type=jnp.float32,
            )
            halves_ref[half, :, block * 128 : block * 128 + 128] = moved.astype(jnp.bfloat16)


def split_columns(basis):
    rows, columns = basis.shape
    return pl.pallas_call(
        split_kernel,
        out_shape=jax.ShapeDtypeStruct((2, rows, columns // 2), basis.dtype),
        in_specs=[VMEM],
        out_specs=VMEM,
        name="split_columns",
    )(basis)


def first_kernel(
    mix_ref, place_ref, a0, a1, a2, a3, b0, b1, b2, b3, zy_ref, yz_ref, out_ref, acc_ref, tmp_ref
):
    blocks = (a0, a1, a2, a3, b0, b1, b2, b3)
    rows = a0.shape[0]
    ny, nz = yz_ref.shape[:2]
    depth = a0.shape[1] // ny
    half = zy_ref.shape[-1]
    for y in range(ny):
        field = jnp.concatenate([ref[:, y * depth : (y + 1) * depth] for ref in blocks], axis=0)
        for part in range(2):
            pieces = [zy_ref[z, y] if part == 0 else yz_ref[y, z] for z in range(nz)]
            product = jnp.dot(
                field, jnp.concatenate(pieces, axis=0), preferred_element_type=jnp.float32
            )
            span = slice(part * half, part * half + half)
            if y == 0:
                acc_ref[:, span] = product
            else:
                acc_ref[:, span] += product
    place = place_ref[0]
    for a in range(4):
        for group in range(2):
            mixed = sum(
                mix_ref[group * 4 + t, a]
                * acc_ref[(group * 4 + t) * rows : (group * 4 + t + 1) * rows, :]
                for t in range(4)
            )
            at = place if group == 0 else 1 - place
            tmp_ref[pl.ds(pl.multiple_of(at * rows, rows), rows), :] = mixed
        out_ref[:, a * 2 * rows : (a + 1) * 2 * rows] = tmp_ref[...].T.astype(jnp.bfloat16)


def first_product(mix, place, fields, zy, yz):
    rows, depth = fields[0].shape
    width = zy.shape[-1] + yz.shape[-1]
    return pl.pallas_call(
        first_kernel,
        out_shape=jax.ShapeDtypeStruct((width, 8 * rows), jnp.bfloat16),
        in_specs=[SMEM, SMEM] + [VMEM] * 10,
        out_specs=VMEM,
        scratch_shapes=[
            pltpu.VMEM((8 * rows, width), jnp.float32),
            pltpu.VMEM((2 * rows, width), jnp.float32),
        ],
        cost_estimate=pl.CostEstimate(
            flops=2 * 8 * rows * depth * width, bytes_accessed=8 << 20, transcendentals=0
        ),
        name="first_product",
    )(mix, place, *fields, zy, yz)


def last_kernel(
    place_ref, t0, t1, t2, t3, zy_ref, yz_ref, rest_ref, sx_ref, sy_ref, white_ref, out_ref, acc_ref
):
    fields = (t0, t1, t2, t3)
    ny, nz = yz_ref.shape[:2]
    times, rows, total = t0.shape
    depth = total // ny
    half = zy_ref.shape[-1]
    for y in range(ny):
        field = jnp.concatenate(
            [ref[a, :, y * depth : (y + 1) * depth] for a in range(times) for ref in fields], axis=0
        )
        for part in range(3):
            pieces = [
                (zy_ref[z, y], yz_ref[y, z], rest_ref[z, y])[part] for z in range(nz)
            ]
            product = jnp.dot(
                field, jnp.concatenate(pieces, axis=0), preferred_element_type=jnp.float32
            )
            span = slice(part * half, part * half + product.shape[-1])
            if y == 0:
                acc_ref[:, span] = product
            else:
                acc_ref[:, span] += product
    lo, time = place_ref[0], place_ref[1]
    source = lax.broadcasted_iota(jnp.int32, (256, 256), 0)
    target = lax.broadcasted_iota(jnp.int32, (256, 256), 1)
    within = lax.rem(source, 128)
    which = jnp.where(source < 128, lo, 1 - lo)
    chosen = (target == (within // 8) * 16 + which * 8 + lax.rem(within, 8)).astype(jnp.float32)
    width = out_ref.shape[-1]
    for block in range(width // 256):
        pair = jnp.concatenate(
            [
                acc_ref[:, block * 128 : block * 128 + 128],
                acc_ref[:, width // 2 + block * 128 : width // 2 + block * 128 + 128],
            ],
            axis=1,
        )
        natural = jnp.dot(pair, chosen, precision=lax.Precision.HIGHEST)
        span = slice(block * 256, block * 256 + 256)
        for a in range(times):
            for b in range(4):
                first = (a * 4 + b) * rows
                own = pl.ds(pl.multiple_of(lax.bitwise_xor(time, b) * rows, rows), rows)
                scale = sy_ref[b * rows : (b + 1) * rows, :1] * sx_ref[:, span]
                out_ref[own, a, span] = (
                    scale * natural[first : first + rows] - white_ref[own, a, span]
                )


def last_product(place, fields, zy, yz, rest, sx, sy, white):
    times, rows, total = fields[0].shape
    width = white.shape[-1]
    return pl.pallas_call(
        last_kernel,
        out_shape=jax.ShapeDtypeStruct(white.shape, jnp.float32),
        in_specs=[SMEM] + [VMEM] * 10,
        out_specs=VMEM,
        scratch_shapes=[pltpu.VMEM((4 * times * rows, width), jnp.float32)],
        cost_estimate=pl.CostEstimate(
            flops=2 * 4 * times * rows * total * width, bytes_accessed=12 << 20, transcendentals=0
        ),
        name="last_product",
    )(place, *fields, zy, yz, rest, sx, sy, white)


def local(event_counts, latent_mean, latent_var, eigen_basis, spectrum, correlation, whitened):
    hi, core = lax.axis_index("hi"), lax.axis_index("core")
    y, z, lo = (lax.axis_index(axis) for axis in ROW)
    time = hi * 2 + core
    ny, nz = lax.axis_size("y"), lax.axis_size("z")

    halves = split_columns(eigen_basis)
    other = shifted(halves, "lo", 1)
    stacked = jnp.where(lo == 0, jnp.stack([halves, other]), jnp.stack([other, halves]))
    mine = jnp.where(lo == 0, stacked[:, 0], stacked[:, 1])
    rest = jnp.where(lo == 0, stacked[:, 1], stacked[:, 0])
    mine = mine.reshape(-1, mine.shape[-1])
    rest = rest.reshape(-1, rest.shape[-1])
    quarter = mine.shape[-1] // 2

    yz = copies_along(lax.all_gather(mine[:, quarter:], "z"), "y")
    zy = lax.all_gather(copies_along(mine[:, :quarter], "y"), "z")
    rest_y = copies_along(rest, "y")
    rest_y, zy = lax.optimization_barrier((rest_y, zy))
    rest = lax.all_gather(rest_y, "z")

    pseudo = moments(event_counts, latent_mean, latent_var).astype(jnp.bfloat16)[0]
    around = [pseudo] + [shifted(pseudo, RING, step) for step in (2, 1, 3)]
    own, far, before, after = [(block, shifted(block, "core", 1)) for block in around]
    fields = (*own, *far, *before, *after)
    flips = jnp.array([0, 1, 2, 3], jnp.int32)
    before_flip, after_flip = 2 * (1 - lo), 2 * lo
    crossed = jnp.stack([before_flip, before_flip + 1, after_flip, after_flip + 1])
    slices = lax.bitwise_xor(time, jnp.concatenate([flips, crossed]))
    factor = time_factor(correlation[0], 4)
    mix = jnp.take(factor, slices, axis=0)
    place = jnp.stack([lo, time]).astype(jnp.int32)
    partial_y = first_product(mix, place, fields, zy, yz)

    modes, width = partial_y.shape
    row_devices = lax.axis_size(ROW)
    sent = partial_y.reshape(row_devices, modes // row_devices, width)
    got = lax.all_to_all(sent, ROW, 0, 0, tiled=True)
    got = got.reshape(ny * nz, 2, modes // row_devices, 4, width // 4)
    got = got.transpose(3, 1, 2, 0, 4).reshape(4, 2 * (modes // row_devices), -1)
    across = shifted(got, "hi", 1)
    bands = (got, shifted(got, "core", 1), across, shifted(across, "core", 1))

    root = jnp.sqrt(spectrum)
    sx = lax.dynamic_slice_in_dim(root, time * 1024, 1024, 0)[None]
    row = (y * nz + z) * 2 + lo
    by_row = lax.dynamic_slice_in_dim(root.reshape(4, row_devices, -1), row, 1, 1)[:, 0]
    sy = jnp.take(by_row, lax.bitwise_xor(time, flips), axis=0).reshape(-1, 1)
    sy = jnp.broadcast_to(sy, (sy.shape[0], 128))
    white = whitened.reshape(-1, *whitened.shape[3:])
    gradient = last_product(place, bands, zy, yz, rest, sx, sy, white)
    return gradient.reshape(whitened.shape)


def solution(mesh):
    finer = Mesh(mesh.devices.reshape(2, 2, 4, 8, 2), ("hi", "core", "y", "z", "lo"))
    placed = (
        P(TM, ROW, None),
        P(TM, ROW, None),
        P(TM, ROW, None),
        P(ROW, TM),
        P(),
        P(),
        P(None, ROW, None, None, TM),
    )
    return jax.shard_map(
        local,
        mesh=finer,
        in_specs=placed,
        out_specs=P(None, ROW, None, None, TM),
        check_vma=False,
    )
```

```python
import math

import jax
import jax.numpy as jnp
from jax import lax
from jax.experimental import pallas as pl
from jax.experimental.pallas import tpu as pltpu
from jax.sharding import Mesh
from jax.sharding import PartitionSpec as P

TM = ("hi", "core")
ROW = ("y", "z", "lo")
RING = ("hi", "lo")

HERMITE_NODES = (
    -2.0201828704560856,
    -0.9585724646138185,
    0.0,
    0.9585724646138185,
    2.0201828704560856,
)
HERMITE_WEIGHTS = (
    0.019953242059045913,
    0.3936193231522412,
    0.9453087204829419,
    0.3936193231522412,
    0.019953242059045913,
)
VMEM = pl.BlockSpec(memory_space=pltpu.VMEM)
SMEM = pl.BlockSpec(memory_space=pltpu.SMEM)


def moments(event_counts, latent_mean, latent_var):
    spread = jnp.sqrt(2.0 * latent_var)
    normal = 1.0 / math.sqrt(math.pi)
    points = [latent_mean + spread * abscissa for abscissa in HERMITE_NODES]
    rate_points = [jnp.exp(value) for value in points]
    mean_rate = sum(
        (weight * normal * value for weight, value in zip(HERMITE_WEIGHTS, rate_points))
    )
    covariance = sum(
        (
            weight * normal * (node_value - latent_mean) * (value - mean_rate)
            for weight, node_value, value in zip(HERMITE_WEIGHTS, points, rate_points)
        )
    )
    rate_var = sum(
        (
            weight * normal * (value - mean_rate) * (value - mean_rate)
            for weight, value in zip(HERMITE_WEIGHTS, rate_points)
        )
    )
    slope_gain = covariance / latent_var
    noise_var = rate_var - slope_gain * covariance + mean_rate
    return slope_gain * (event_counts.astype(latent_mean.dtype) - mean_rate) / noise_var


def time_factor(correlation, total):
    later = jnp.arange(total)[:, None]
    earlier = jnp.arange(total)[None, :]
    distance = jnp.maximum(later - earlier, 0).astype(correlation.dtype)
    lower = jnp.where(later >= earlier, jnp.power(correlation, distance), jnp.zeros_like(distance))
    column_scale = jnp.where(
        earlier == 0,
        jnp.ones_like(distance),
        jnp.sqrt(1.0 - correlation * correlation) * jnp.ones_like(distance),
    )
    return lower * column_scale


def shifted(array, axis, step):
    size = lax.axis_size(axis)
    return lax.ppermute(array, axis, [(k, (k + step) % size) for k in range(size)])


def split_kernel(first_ref, basis_ref, halves_ref):
    source = lax.broadcasted_iota(jnp.int32, (256, 128), 0)
    target = lax.broadcasted_iota(jnp.int32, (256, 128), 1)
    for place in range(2):
        half = first_ref[0] if place == 0 else 1 - first_ref[0]
        match = source == (target // 8) * 16 + half * 8 + lax.rem(target, 8)
        chosen = match.astype(jnp.float32).astype(jnp.bfloat16)
        for block in range(basis_ref.shape[1] // 256):
            moved = jnp.dot(
                basis_ref[:, block * 256 : block * 256 + 256],
                chosen,
                preferred_element_type=jnp.float32,
            ).astype(jnp.bfloat16)
            for copy in range(halves_ref.shape[0]):
                halves_ref[copy, place, :, block * 128 : block * 128 + 128] = moved


def split_columns(first, basis, copies):
    rows, columns = basis.shape
    return pl.pallas_call(
        split_kernel,
        out_shape=jax.ShapeDtypeStruct((copies, 2, rows, columns // 2), basis.dtype),
        in_specs=[SMEM, VMEM],
        out_specs=VMEM,
        name="split_columns",
    )(first, basis)


def depth_of(ref, y):
    if len(ref.shape) == 4:
        pieces = [ref[z, y] for z in range(ref.shape[0])]
    else:
        pieces = [ref[y, lo, z] for z in range(ref.shape[2]) for lo in range(2)]
    return jnp.concatenate(pieces, axis=0)


def first_kernel(
    mix_ref, place_ref, a0, a1, a2, a3, b0, b1, b2, b3, zy_ref, yz_ref, out_ref, acc_ref, tmp_ref
):
    blocks = (a0, a1, a2, a3, b0, b1, b2, b3)
    rows = a0.shape[0]
    ny, nz = yz_ref.shape[0], yz_ref.shape[2]
    depth = a0.shape[1] // ny
    half = zy_ref.shape[-1]
    for y in range(ny):
        field = jnp.concatenate([ref[:, y * depth : (y + 1) * depth] for ref in blocks], axis=0)
        for part in range(2):
            basis = depth_of((zy_ref, yz_ref)[part], y)
            product = jnp.dot(field, basis, preferred_element_type=jnp.float32)
            span = slice(part * half, part * half + half)
            if y == 0:
                acc_ref[:, span] = product
            else:
                acc_ref[:, span] += product
    place = place_ref[0]
    for a in range(4):
        for group in range(2):
            mixed = sum(
                mix_ref[group * 4 + t, a]
                * acc_ref[(group * 4 + t) * rows : (group * 4 + t + 1) * rows, :]
                for t in range(4)
            )
            at = place if group == 0 else 1 - place
            tmp_ref[pl.ds(pl.multiple_of(at * rows, rows), rows), :] = mixed
        out_ref[:, a * 2 * rows : (a + 1) * 2 * rows] = tmp_ref[...].T.astype(jnp.bfloat16)


def first_product(mix, place, fields, zy, yz):
    rows, depth = fields[0].shape
    width = zy.shape[-1] + yz.shape[-1]
    return pl.pallas_call(
        first_kernel,
        out_shape=jax.ShapeDtypeStruct((width, 8 * rows), jnp.bfloat16),
        in_specs=[SMEM, SMEM] + [VMEM] * 10,
        out_specs=VMEM,
        scratch_shapes=[
            pltpu.VMEM((8 * rows, width), jnp.float32),
            pltpu.VMEM((2 * rows, width), jnp.float32),
        ],
        cost_estimate=pl.CostEstimate(
            flops=2 * 8 * rows * depth * width, bytes_accessed=8 << 20, transcendentals=0
        ),
        name="first_product",
    )(mix, place, *fields, zy, yz)


def last_kernel(
    place_ref, t0, t1, t2, t3, zy0, yz0, zy1, yz1, sx_ref, sy_ref, white_ref, out_ref, acc_ref
):
    fields = (t0, t1, t2, t3)
    ny, nz = yz0.shape[0], yz0.shape[2]
    times, rows, total = t0.shape
    depth = total // ny
    half = zy0.shape[-1]
    for y in range(ny):
        field = jnp.concatenate(
            [ref[a, :, y * depth : (y + 1) * depth] for a in range(times) for ref in fields], axis=0
        )
        for part, ref in enumerate((zy0, yz0, zy1, yz1)):
            product = jnp.dot(field, depth_of(ref, y), preferred_element_type=jnp.float32)
            span = slice(part * half, part * half + half)
            if y == 0:
                acc_ref[:, span] = product
            else:
                acc_ref[:, span] += product
    lo, time = place_ref[0], place_ref[1]
    source = lax.broadcasted_iota(jnp.int32, (256, 256), 0)
    target = lax.broadcasted_iota(jnp.int32, (256, 256), 1)
    within = lax.rem(source, 128)
    which = jnp.where(source < 128, lo, 1 - lo)
    chosen = (target == (within // 8) * 16 + which * 8 + lax.rem(within, 8)).astype(jnp.float32)
    width = out_ref.shape[-1]
    for block in range(width // 256):
        pair = jnp.concatenate(
            [
                acc_ref[:, block * 128 : block * 128 + 128],
                acc_ref[:, width // 2 + block * 128 : width // 2 + block * 128 + 128],
            ],
            axis=1,
        )
        natural = jnp.dot(pair, chosen, precision=lax.Precision.HIGHEST)
        span = slice(block * 256, block * 256 + 256)
        for a in range(times):
            for b in range(4):
                first = (a * 4 + b) * rows
                own = pl.ds(pl.multiple_of(lax.bitwise_xor(time, b) * rows, rows), rows)
                scale = sy_ref[b * rows : (b + 1) * rows, :1] * sx_ref[:, span]
                out_ref[own, a, span] = (
                    scale * natural[first : first + rows] - white_ref[own, a, span]
                )


def last_product(place, fields, basis, sx, sy, white):
    times, rows, total = fields[0].shape
    width = white.shape[-1]
    return pl.pallas_call(
        last_kernel,
        out_shape=jax.ShapeDtypeStruct(white.shape, jnp.float32),
        in_specs=[SMEM] + [VMEM] * 11,
        out_specs=VMEM,
        scratch_shapes=[pltpu.VMEM((4 * times * rows, width), jnp.float32)],
        cost_estimate=pl.CostEstimate(
            flops=2 * 4 * times * rows * total * width, bytes_accessed=12 << 20, transcendentals=0
        ),
        name="last_product",
    )(place, *fields, *basis, sx, sy, white)


def local(event_counts, latent_mean, latent_var, eigen_basis, spectrum, correlation, whitened):
    hi, core = lax.axis_index("hi"), lax.axis_index("core")
    y, z, lo = (lax.axis_index(axis) for axis in ROW)
    time = hi * 2 + core
    ny, nz = lax.axis_size("y"), lax.axis_size("z")

    rows, columns = eigen_basis.shape
    part = columns // 4
    raw = lax.all_gather(eigen_basis, "z").reshape(nz * rows, columns)
    left = jnp.broadcast_to(eigen_basis[None, :, : 2 * part], (2 * ny, rows, 2 * part))
    left = lax.all_to_all(left, ("y", "lo"), 0, 0, tiled=True).reshape(-1, 2 * part)
    pseudo = moments(event_counts, latent_mean, latent_var).astype(jnp.bfloat16)[0]
    left, pseudo = lax.optimization_barrier((left, pseudo))
    first = lo[None].astype(jnp.int32)
    left = split_columns(first, left, 1).reshape(2, ny, 2 * rows, part)
    left, raw = lax.optimization_barrier((left, raw))
    right = split_columns(jnp.zeros((1,), jnp.int32), raw[:, 2 * part :], ny)
    yz = lax.all_to_all(right.reshape(2 * ny, nz * rows, part), ("y", "lo"), 0, 0, tiled=True)
    yz = yz.reshape(ny, 2, nz, rows, part)
    zy = lax.all_gather(left[0], "z")
    around = [pseudo] + [shifted(pseudo, RING, step) for step in (2, 1, 3)]
    left_rest, zy, around = lax.optimization_barrier((left[1], zy, around))
    zy_rest = lax.all_gather(left_rest, "z")
    yz_rest = shifted(yz, "lo", 1)

    own, far, before, after = [(block, shifted(block, "core", 1)) for block in around]
    fields = (*own, *far, *before, *after)
    flips = jnp.array([0, 1, 2, 3], jnp.int32)
    before_flip, after_flip = 2 * (1 - lo), 2 * lo
    crossed = jnp.stack([before_flip, before_flip + 1, after_flip, after_flip + 1])
    slices = lax.bitwise_xor(time, jnp.concatenate([flips, crossed]))
    factor = time_factor(correlation[0], 4)
    mix = jnp.take(factor, slices, axis=0)
    place = jnp.stack([lo, time]).astype(jnp.int32)
    partial_y = first_product(mix, place, fields, zy, yz)

    modes, width = partial_y.shape
    row_devices = lax.axis_size(ROW)
    sent = partial_y.reshape(row_devices, modes // row_devices, width)
    got = lax.all_to_all(sent, ROW, 0, 0, tiled=True)
    got = got.reshape(ny * nz, 2, modes // row_devices, 4, width // 4)
    got = got.transpose(3, 1, 2, 0, 4).reshape(4, 2 * (modes // row_devices), -1)
    across = shifted(got, "hi", 1)
    bands = (got, shifted(got, "core", 1), across, shifted(across, "core", 1))

    root = jnp.sqrt(spectrum)
    sx = lax.dynamic_slice_in_dim(root, time * 1024, 1024, 0)[None]
    row = (y * nz + z) * 2 + lo
    by_row = lax.dynamic_slice_in_dim(root.reshape(4, row_devices, -1), row, 1, 1)[:, 0]
    sy = jnp.take(by_row, lax.bitwise_xor(time, flips), axis=0).reshape(-1, 1)
    sy = jnp.broadcast_to(sy, (sy.shape[0], 128))
    white = whitened.reshape(-1, *whitened.shape[3:])
    gradient = last_product(place, bands, (zy, yz, zy_rest, yz_rest), sx, sy, white)
    return gradient.reshape(whitened.shape)


def solution(mesh):
    finer = Mesh(mesh.devices.reshape(2, 2, 4, 8, 2), ("hi", "core", "y", "z", "lo"))
    placed = (
        P(TM, ROW, None),
        P(TM, ROW, None),
        P(TM, ROW, None),
        P(ROW, TM),
        P(),
        P(),
        P(None, ROW, None, None, TM),
    )
    return jax.shard_map(
        local,
        mesh=finer,
        in_specs=placed,
        out_specs=P(None, ROW, None, None, TM),
        check_vma=False,
    )
```

```python
import math

import jax
import jax.numpy as jnp
from jax import lax
from jax.experimental import pallas as pl
from jax.experimental.pallas import tpu as pltpu
from jax.sharding import Mesh
from jax.sharding import PartitionSpec as P

TM = ("hi", "core")
ROW = ("y", "z", "lo")
RING = ("hi", "lo")

HERMITE_NODES = (
    -2.0201828704560856,
    -0.9585724646138185,
    0.0,
    0.9585724646138185,
    2.0201828704560856,
)
HERMITE_WEIGHTS = (
    0.019953242059045913,
    0.3936193231522412,
    0.9453087204829419,
    0.3936193231522412,
    0.019953242059045913,
)
VMEM = pl.BlockSpec(memory_space=pltpu.VMEM)
SMEM = pl.BlockSpec(memory_space=pltpu.SMEM)


def moments(event_counts, latent_mean, latent_var):
    spread = jnp.sqrt(2.0 * latent_var)
    normal = 1.0 / math.sqrt(math.pi)
    points = [latent_mean + spread * abscissa for abscissa in HERMITE_NODES]
    rate_points = [jnp.exp(value) for value in points]
    mean_rate = sum(
        (weight * normal * value for weight, value in zip(HERMITE_WEIGHTS, rate_points))
    )
    covariance = sum(
        (
            weight * normal * (node_value - latent_mean) * (value - mean_rate)
            for weight, node_value, value in zip(HERMITE_WEIGHTS, points, rate_points)
        )
    )
    rate_var = sum(
        (
            weight * normal * (value - mean_rate) * (value - mean_rate)
            for weight, value in zip(HERMITE_WEIGHTS, rate_points)
        )
    )
    slope_gain = covariance / latent_var
    noise_var = rate_var - slope_gain * covariance + mean_rate
    return slope_gain * (event_counts.astype(latent_mean.dtype) - mean_rate) / noise_var


def time_factor(correlation, total):
    later = jnp.arange(total)[:, None]
    earlier = jnp.arange(total)[None, :]
    distance = jnp.maximum(later - earlier, 0).astype(correlation.dtype)
    lower = jnp.where(later >= earlier, jnp.power(correlation, distance), jnp.zeros_like(distance))
    column_scale = jnp.where(
        earlier == 0,
        jnp.ones_like(distance),
        jnp.sqrt(1.0 - correlation * correlation) * jnp.ones_like(distance),
    )
    return lower * column_scale


def shifted(array, axis, step):
    size = lax.axis_size(axis)
    return lax.ppermute(array, axis, [(k, (k + step) % size) for k in range(size)])


def copies_along(array, axis):
    size = lax.axis_size(axis)
    return lax.all_to_all(
        jnp.broadcast_to(array[None], (size, *array.shape)), axis, 0, 0, tiled=True
    )


def split_kernel(first_ref, basis_ref, kept_ref, sent_ref):
    source = lax.broadcasted_iota(jnp.int32, (256, 128), 0)
    target = lax.broadcasted_iota(jnp.int32, (256, 128), 1)
    for half, ref in ((first_ref[0], kept_ref), (1 - first_ref[0], sent_ref)):
        match = source == (target // 8) * 16 + half * 8 + lax.rem(target, 8)
        chosen = match.astype(jnp.float32).astype(jnp.bfloat16)
        for block in range(basis_ref.shape[1] // 256):
            moved = jnp.dot(
                basis_ref[:, block * 256 : block * 256 + 256],
                chosen,
                preferred_element_type=jnp.float32,
            )
            ref[:, block * 128 : block * 128 + 128] = moved.astype(jnp.bfloat16)


def split_columns(place, basis):
    rows, columns = basis.shape
    half = jax.ShapeDtypeStruct((rows, columns // 2), basis.dtype)
    return pl.pallas_call(
        split_kernel,
        out_shape=(half, half),
        in_specs=[SMEM, VMEM],
        out_specs=(VMEM, VMEM),
        name="split_columns",
    )(place, basis)


def first_kernel(mix_ref, place_ref, *refs):
    blocks, z_refs, y_refs = refs[:8], refs[8:17], refs[17:22]
    out_ref, zy_ref, yz_ref, acc_ref, tmp_ref = refs[22:]
    rows, total = blocks[0].shape
    ny, nz = yz_ref.shape[:2]
    lo, y_here, z_here = place_ref[0], place_ref[2], place_ref[3]

    y_steps = (0, ny - 1, 1, 2)
    for ref, step in zip(z_refs, (0, nz - 1, 1, nz - 2, 2, nz - 3, 3, 4, 4)):
        at = lax.rem(z_here + step, nz)
        first = 2 if ref is z_refs[8] else 0
        for k in range(ref.shape[0]):
            zy_ref[at, lax.rem(y_here + y_steps[first + k], ny)] = ref[k]
    for ref, step in zip(y_refs, (0, ny - 1, 1, 2, 2)):
        at = lax.rem(y_here + step, ny)
        first = nz // 2 if ref is y_refs[4] else 0
        for k in range(ref.shape[0]):
            yz_ref[at, first + k] = ref[k]

    depth = total // ny
    half = zy_ref.shape[-1]
    for y in range(ny):
        field = jnp.concatenate([ref[:, y * depth : (y + 1) * depth] for ref in blocks], axis=0)
        for part in range(2):
            product = jnp.dot(
                field, basis_at(zy_ref, yz_ref, part, y), preferred_element_type=jnp.float32
            )
            span = slice(part * half, part * half + half)
            if y == 0:
                acc_ref[:, span] = product
            else:
                acc_ref[:, span] += product
    for a in range(4):
        for group in range(2):
            mixed = sum(
                mix_ref[group * 4 + t, a]
                * acc_ref[(group * 4 + t) * rows : (group * 4 + t + 1) * rows, :]
                for t in range(4)
            )
            at = lo if group == 0 else 1 - lo
            tmp_ref[pl.ds(pl.multiple_of(at * rows, rows), rows), :] = mixed
        out_ref[:, a * 2 * rows : (a + 1) * 2 * rows] = tmp_ref[...].T.astype(jnp.bfloat16)


def basis_at(zy_ref, yz_ref, part, y):
    if part == 0:
        pieces = [zy_ref[z, y] for z in range(zy_ref.shape[0])]
    else:
        pieces = [yz_ref[y, z] for z in range(yz_ref.shape[1])]
    return jnp.concatenate(pieces, axis=0)


def first_product(mix, place, fields, by_z, by_y):
    rows, depth = fields[0].shape
    ny, (nz, deep, half) = lax.axis_size("y"), by_y[0].shape
    width = 2 * half
    return pl.pallas_call(
        first_kernel,
        out_shape=(
            jax.ShapeDtypeStruct((width, 8 * rows), jnp.bfloat16),
            jax.ShapeDtypeStruct((nz, ny, deep, half), jnp.bfloat16),
            jax.ShapeDtypeStruct((ny, nz, deep, half), jnp.bfloat16),
        ),
        in_specs=[SMEM, SMEM] + [VMEM] * 22,
        out_specs=(VMEM, VMEM, VMEM),
        scratch_shapes=[
            pltpu.VMEM((8 * rows, width), jnp.float32),
            pltpu.VMEM((2 * rows, width), jnp.float32),
        ],
        cost_estimate=pl.CostEstimate(
            flops=2 * 8 * rows * depth * width, bytes_accessed=8 << 20, transcendentals=0
        ),
        name="first_product",
    )(mix, place, *fields, *by_z, *by_y)


def last_kernel(place_ref, slice_ref, *refs):
    fields = refs[:8]
    zy_ref, yz_ref, kept_ref, sent_ref, acc_ref, tmp_ref = refs[8:]
    ny = yz_ref.shape[0]
    times, rows, total = fields[0].shape
    depth = total // ny
    half = zy_ref.shape[-1]
    for y in range(ny):
        field = jnp.concatenate(
            [ref[a, :, y * depth : (y + 1) * depth] for a in range(times) for ref in fields], axis=0
        )
        for part in range(2):
            product = jnp.dot(
                field, basis_at(zy_ref, yz_ref, part, y), preferred_element_type=jnp.float32
            )
            span = slice(part * half, part * half + half)
            if y == 0:
                acc_ref[:, span] = product
            else:
                acc_ref[:, span] += product
    lo = place_ref[0]
    group = rows // 2
    for a in range(times):
        for b in range(8):
            half_of = lo if b < 4 else 1 - lo
            to = pl.multiple_of((slice_ref[b] * 2 + half_of) * group, group)
            base = (a * 8 + b) * rows
            mine = pl.multiple_of(base + lo * group, group)
            theirs = pl.multiple_of(base + (1 - lo) * group, group)
            kept_ref[a, pl.ds(to, group), :] = acc_ref[pl.ds(mine, group), :]
            tmp_ref[pl.ds(to, group), :] = acc_ref[pl.ds(theirs, group), :]
        sent_ref[a] = tmp_ref[...].astype(jnp.bfloat16)


def last_product(place, slices, fields, zy, yz):
    times, rows, total = fields[0].shape
    width = zy.shape[-1] + yz.shape[-1]
    own = (times, 4 * rows, width)
    return pl.pallas_call(
        last_kernel,
        out_shape=(
            jax.ShapeDtypeStruct(own, jnp.float32),
            jax.ShapeDtypeStruct(own, jnp.bfloat16),
        ),
        in_specs=[SMEM, SMEM] + [VMEM] * 10,
        out_specs=(VMEM, VMEM),
        scratch_shapes=[
            pltpu.VMEM((8 * times * rows, width), jnp.float32),
            pltpu.VMEM((4 * rows, width), jnp.float32),
        ],
        cost_estimate=pl.CostEstimate(
            flops=2 * 8 * times * rows * total * width, bytes_accessed=8 << 20, transcendentals=0
        ),
        name="last_product",
    )(place, slices, *fields, zy, yz)


def gradient_kernel(place_ref, kept_ref, got_ref, sx_ref, sy_ref, white_ref, out_ref):
    lo = place_ref[0]
    source = lax.broadcasted_iota(jnp.int32, (256, 256), 0)
    target = lax.broadcasted_iota(jnp.int32, (256, 256), 1)
    within = lax.rem(source, 128)
    which = jnp.where(source < 128, lo, 1 - lo)
    chosen = (target == (within // 8) * 16 + which * 8 + lax.rem(within, 8)).astype(jnp.float32)
    times, rows, half = kept_ref.shape
    for block in range(half // 128):
        here = slice(block * 128, block * 128 + 128)
        span = slice(block * 256, block * 256 + 256)
        pair = jnp.concatenate(
            [
                jnp.concatenate(
                    [kept_ref[a, :, here], got_ref[a, :, here].astype(jnp.float32)], axis=1
                )
                for a in range(times)
            ],
            axis=0,
        )
        natural = jnp.dot(pair, chosen, precision=lax.Precision.HIGHEST)
        for a in range(times):
            scale = sy_ref[:, :1] * sx_ref[:, span]
            out_ref[:, a, span] = (
                scale * natural[a * rows : (a + 1) * rows] - white_ref[:, a, span]
            )


def whitened_gradient(place, kept, got, sx, sy, white):
    return pl.pallas_call(
        gradient_kernel,
        out_shape=jax.ShapeDtypeStruct(white.shape, jnp.float32),
        in_specs=[SMEM] + [VMEM] * 5,
        out_specs=VMEM,
        name="whitened_gradient",
    )(place, kept, got, sx, sy, white)


def around_x(block):
    blocks = [block] + [shifted(block, RING, step) for step in (2, 1, 3)]
    return tuple(copy for b in blocks for copy in (b, shifted(b, "core", 1)))


def local(event_counts, latent_mean, latent_var, eigen_basis, spectrum, correlation, whitened):
    hi, core = lax.axis_index("hi"), lax.axis_index("core")
    y, z, lo = (lax.axis_index(axis) for axis in ROW)
    time = hi * 2 + core
    ny, nz = lax.axis_size("y"), lax.axis_size("z")
    place = jnp.stack([lo, time, y, z]).astype(jnp.int32)

    kept, sent = split_columns(place, eigen_basis)
    other = shifted(sent, "lo", 1)
    mine = jnp.where(lo == 0, jnp.concatenate([kept, other]), jnp.concatenate([other, kept]))
    half = mine.shape[-1] // 2
    z_block, y_block = mine[:, :half], mine[:, half:]

    pseudo = moments(event_counts, latent_mean, latent_var).astype(jnp.bfloat16)[0]
    z_block, y_block, pseudo = lax.optimization_barrier((z_block, y_block, pseudo))

    y_block = copies_along(y_block, "z")
    z_block = jnp.stack([z_block] + [shifted(z_block, "y", step) for step in (1, 3, 2)])
    fields = around_x(pseudo)

    right = left = z_block
    by_z = [z_block]
    for _ in range(3):
        right, left = shifted(right, "z", 1), shifted(left, "z", nz - 1)
        by_z += [right, left]
    by_z += [shifted(right[:2], "z", 1), shifted(left[2:], "z", nz - 1)]
    right, left = shifted(y_block, "y", 1), shifted(y_block, "y", ny - 1)
    by_y = [y_block, right, left]
    by_y += [shifted(right[: nz // 2], "y", 1), shifted(left[nz // 2 :], "y", ny - 1)]

    flips = jnp.array([0, 1, 2, 3], jnp.int32)
    before_flip, after_flip = 2 * (1 - lo), 2 * lo
    crossed = jnp.stack([before_flip, before_flip + 1, after_flip, after_flip + 1])
    slices = lax.bitwise_xor(time, jnp.concatenate([flips, crossed])).astype(jnp.int32)
    factor = time_factor(correlation[0], 4)
    mix = jnp.take(factor, slices, axis=0)
    partial_y, zy, yz = first_product(mix, place, fields, by_z, by_y)

    modes, width = partial_y.shape
    sent = partial_y.reshape(ny * nz, modes // (ny * nz), width)
    got = lax.all_to_all(sent, ("y", "z"), 0, 0, tiled=True)
    got = got.reshape(ny * nz, modes // (ny * nz), 4, width // 4)
    got = got.transpose(2, 1, 0, 3).reshape(4, modes // (ny * nz), -1)
    kept, sent = last_product(place, slices, around_x(got), zy, yz)
    got = shifted(sent, "lo", 1)

    root = jnp.sqrt(spectrum)
    sx = lax.dynamic_slice_in_dim(root, time * 1024, 1024, 0)[None]
    row = (y * nz + z) * 2 + lo
    sy = lax.dynamic_slice_in_dim(root.reshape(4, lax.axis_size(ROW), -1), row, 1, 1).reshape(-1, 1)
    sy = jnp.broadcast_to(sy, (sy.shape[0], 128))
    white = whitened.reshape(-1, *whitened.shape[3:])
    gradient = whitened_gradient(place, kept, got, sx, sy, white)
    return gradient.reshape(whitened.shape)


def solution(mesh):
    finer = Mesh(mesh.devices.reshape(2, 2, 4, 8, 2), ("hi", "core", "y", "z", "lo"))
    placed = (
        P(TM, ROW, None),
        P(TM, ROW, None),
        P(TM, ROW, None),
        P(ROW, TM),
        P(),
        P(),
        P(None, ROW, None, None, TM),
    )
    return jax.shard_map(
        local,
        mesh=finer,
        in_specs=placed,
        out_specs=P(None, ROW, None, None, TM),
        check_vma=False,
    )
```

```python
import math

import jax
import jax.numpy as jnp
from jax import lax
from jax.experimental import pallas as pl
from jax.experimental.pallas import tpu as pltpu
from jax.sharding import Mesh
from jax.sharding import PartitionSpec as P

TM = ("hi", "core")
ROW = ("y", "z", "lo")
RING = ("hi", "lo")

HERMITE_NODES = (
    -2.0201828704560856,
    -0.9585724646138185,
    0.0,
    0.9585724646138185,
    2.0201828704560856,
)
HERMITE_WEIGHTS = (
    0.019953242059045913,
    0.3936193231522412,
    0.9453087204829419,
    0.3936193231522412,
    0.019953242059045913,
)
VMEM = pl.BlockSpec(memory_space=pltpu.VMEM)
SMEM = pl.BlockSpec(memory_space=pltpu.SMEM)


def moments(event_counts, latent_mean, latent_var):
    spread = jnp.sqrt(2.0 * latent_var)
    normal = 1.0 / math.sqrt(math.pi)
    points = [latent_mean + spread * abscissa for abscissa in HERMITE_NODES]
    rate_points = [jnp.exp(value) for value in points]
    mean_rate = sum(
        (weight * normal * value for weight, value in zip(HERMITE_WEIGHTS, rate_points))
    )
    covariance = sum(
        (
            weight * normal * (node_value - latent_mean) * (value - mean_rate)
            for weight, node_value, value in zip(HERMITE_WEIGHTS, points, rate_points)
        )
    )
    rate_var = sum(
        (
            weight * normal * (value - mean_rate) * (value - mean_rate)
            for weight, value in zip(HERMITE_WEIGHTS, rate_points)
        )
    )
    slope_gain = covariance / latent_var
    noise_var = rate_var - slope_gain * covariance + mean_rate
    return slope_gain * (event_counts.astype(latent_mean.dtype) - mean_rate) / noise_var


def time_factor(correlation, total):
    later = jnp.arange(total)[:, None]
    earlier = jnp.arange(total)[None, :]
    distance = jnp.maximum(later - earlier, 0).astype(correlation.dtype)
    lower = jnp.where(later >= earlier, jnp.power(correlation, distance), jnp.zeros_like(distance))
    column_scale = jnp.where(
        earlier == 0,
        jnp.ones_like(distance),
        jnp.sqrt(1.0 - correlation * correlation) * jnp.ones_like(distance),
    )
    return lower * column_scale


def shifted(array, axis, step):
    size = lax.axis_size(axis)
    return lax.ppermute(array, axis, [(k, (k + step) % size) for k in range(size)])


def split_kernel(first_ref, basis_ref, kept_ref, sent_ref):
    source = lax.broadcasted_iota(jnp.int32, (256, 128), 0)
    target = lax.broadcasted_iota(jnp.int32, (256, 128), 1)
    for half, ref in ((first_ref[0], kept_ref), (1 - first_ref[0], sent_ref)):
        match = source == (target // 8) * 16 + half * 8 + lax.rem(target, 8)
        chosen = match.astype(jnp.float32).astype(jnp.bfloat16)
        for block in range(basis_ref.shape[1] // 256):
            moved = jnp.dot(
                basis_ref[:, block * 256 : block * 256 + 256],
                chosen,
                preferred_element_type=jnp.float32,
            )
            ref[:, block * 128 : block * 128 + 128] = moved.astype(jnp.bfloat16)


def split_columns(place, basis):
    rows, columns = basis.shape
    half = jax.ShapeDtypeStruct((rows, columns // 2), basis.dtype)
    return pl.pallas_call(
        split_kernel,
        out_shape=(half, half),
        in_specs=[SMEM, VMEM],
        out_specs=(VMEM, VMEM),
        name="split_columns",
    )(place, basis)


def columns_at(ref, index):
    return pl.ds(pl.multiple_of(index * 128, 128), 128)


def product_of(place_ref, load, steps, pieces, acc_ref):
    y_here, z_here = place_ref[2], place_ref[3]
    for (step, parts), ref in zip(steps, pieces):
        at = lax.rem(z_here + step, 8)
        where = [columns_at(ref, lax.rem(y_here + part, 4) * 8 + at) for part in parts]
        field = jnp.concatenate([load(span) for span in where], axis=1)
        basis = jnp.concatenate([ref[k] for k in range(len(parts))], axis=0)
        acc_ref[...] += jnp.dot(field, basis, preferred_element_type=jnp.float32)


NEAR = tuple((step, (0, 3, 1, 2)) for step in (0, 7, 1, 6, 2, 5, 3))
FAR = ((4, (0, 3)), (4, (1, 2)))


def near_kernel(place_ref, *refs):
    blocks, pieces, acc_ref = refs[:8], refs[8:-1], refs[-1]
    acc_ref[...] = jnp.zeros_like(acc_ref)

    def load(span):
        return jnp.concatenate([ref[:, span] for ref in blocks], axis=0)

    product_of(place_ref, load, NEAR, pieces, acc_ref)


def near_product(place, fields, pieces):
    rows = sum(field.shape[0] for field in fields)
    width = pieces[0].shape[-1]
    return pl.pallas_call(
        near_kernel,
        out_shape=jax.ShapeDtypeStruct((rows, width), jnp.float32),
        in_specs=[SMEM] + [VMEM] * 15,
        out_specs=VMEM,
        cost_estimate=pl.CostEstimate(
            flops=2 * rows * 3584 * width, bytes_accessed=8 << 20, transcendentals=0
        ),
        name="near_product",
    )(place, *fields, *pieces)


def first_kernel(mix_ref, place_ref, *refs):
    blocks, pieces, near_ref, out_ref, acc_ref, tmp_ref = refs[:8], refs[8:10], *refs[10:]
    rows = blocks[0].shape[0]
    lo = place_ref[0]
    acc_ref[...] = near_ref[...]

    def load(span):
        return jnp.concatenate([ref[:, span] for ref in blocks], axis=0)

    product_of(place_ref, load, FAR, pieces, acc_ref)
    for a in range(4):
        for group in range(2):
            mixed = sum(
                mix_ref[group * 4 + t, a]
                * acc_ref[(group * 4 + t) * rows : (group * 4 + t + 1) * rows, :]
                for t in range(4)
            )
            at = lo if group == 0 else 1 - lo
            tmp_ref[pl.ds(pl.multiple_of(at * rows, rows), rows), :] = mixed
        out_ref[:, a * 2 * rows : (a + 1) * 2 * rows] = tmp_ref[...].T.astype(jnp.bfloat16)


def first_product(mix, place, fields, pieces, near):
    rows = fields[0].shape[0]
    width = near.shape[-1]
    return pl.pallas_call(
        first_kernel,
        out_shape=jax.ShapeDtypeStruct((width, 8 * rows), jnp.bfloat16),
        in_specs=[SMEM, SMEM] + [VMEM] * 11,
        out_specs=VMEM,
        scratch_shapes=[
            pltpu.VMEM((8 * rows, width), jnp.float32),
            pltpu.VMEM((2 * rows, width), jnp.float32),
        ],
        cost_estimate=pl.CostEstimate(
            flops=2 * 8 * rows * 512 * width, bytes_accessed=4 << 20, transcendentals=0
        ),
        name="first_product",
    )(mix, place, *fields, *pieces, near)


def load_bands(fields, span):
    times = fields[0].shape[0]
    return jnp.concatenate([ref[a, :, span] for a in range(times) for ref in fields], axis=0)


def band_kernel(place_ref, *refs):
    fields, pieces, acc_ref = refs[:-10], refs[-10:-1], refs[-1]
    acc_ref[...] = jnp.zeros_like(acc_ref)
    product_of(place_ref, lambda span: load_bands(fields, span), NEAR + FAR, pieces, acc_ref)


def band_product(place, fields, pieces):
    times, rows, total = fields[0].shape
    width = pieces[0].shape[-1]
    count = len(fields) * times * rows
    return pl.pallas_call(
        band_kernel,
        out_shape=jax.ShapeDtypeStruct((count, width), jnp.float32),
        in_specs=[SMEM] + [VMEM] * (len(fields) + 9),
        out_specs=VMEM,
        cost_estimate=pl.CostEstimate(
            flops=2 * count * total * width, bytes_accessed=6 << 20, transcendentals=0
        ),
        name="band_product",
    )(place, *fields, *pieces)


def last_kernel(place_ref, slice_ref, *refs):
    fields, pieces, done = refs[:2], refs[2:11], refs[11:13]
    kept_ref, sent_ref, acc_ref, tmp_ref = refs[13:]
    times, rows, _ = fields[0].shape
    acc_ref[...] = jnp.zeros_like(acc_ref)
    product_of(place_ref, lambda span: load_bands(fields, span), NEAR + FAR, pieces, acc_ref)
    lo = place_ref[0]
    group = rows // 2
    sources = [(done[0], 2, 0), (acc_ref, 2, 0), (done[1], 4, 0), (done[1], 4, 2)]
    for a in range(times):
        for b in range(8):
            ref, count, first = sources[b // 2]
            half_of = lo if b < 4 else 1 - lo
            to = pl.multiple_of((slice_ref[b] * 2 + half_of) * group, group)
            base = (a * count + first + b % 2) * rows
            mine = pl.multiple_of(base + lo * group, group)
            theirs = pl.multiple_of(base + (1 - lo) * group, group)
            kept_ref[a, pl.ds(to, group), :] = ref[pl.ds(mine, group), :]
            tmp_ref[pl.ds(to, group), :] = ref[pl.ds(theirs, group), :]
        sent_ref[a] = tmp_ref[...].astype(jnp.bfloat16)


def last_product(place, slices, fields, pieces, done):
    times, rows, total = fields[0].shape
    width = pieces[0].shape[-1]
    own = (times, 4 * rows, width)
    return pl.pallas_call(
        last_kernel,
        out_shape=(
            jax.ShapeDtypeStruct(own, jnp.float32),
            jax.ShapeDtypeStruct(own, jnp.bfloat16),
        ),
        in_specs=[SMEM, SMEM] + [VMEM] * 13,
        out_specs=(VMEM, VMEM),
        scratch_shapes=[
            pltpu.VMEM((2 * times * rows, width), jnp.float32),
            pltpu.VMEM((4 * rows, width), jnp.float32),
        ],
        cost_estimate=pl.CostEstimate(
            flops=4 * times * rows * total * width, bytes_accessed=6 << 20, transcendentals=0
        ),
        name="last_product",
    )(place, slices, *fields, *pieces, *done)


def gradient_kernel(place_ref, kept_ref, got_ref, sx_ref, sy_ref, white_ref, out_ref):
    lo = place_ref[0]
    source = lax.broadcasted_iota(jnp.int32, (256, 256), 0)
    target = lax.broadcasted_iota(jnp.int32, (256, 256), 1)
    within = lax.rem(source, 128)
    which = jnp.where(source < 128, lo, 1 - lo)
    chosen = (target == (within // 8) * 16 + which * 8 + lax.rem(within, 8)).astype(jnp.float32)
    times, rows, half = kept_ref.shape
    for block in range(half // 128):
        here = slice(block * 128, block * 128 + 128)
        span = slice(block * 256, block * 256 + 256)
        pair = jnp.concatenate(
            [
                jnp.concatenate(
                    [kept_ref[a, :, here], got_ref[a, :, here].astype(jnp.float32)], axis=1
                )
                for a in range(times)
            ],
            axis=0,
        )
        natural = jnp.dot(pair, chosen, precision=lax.Precision.HIGHEST)
        for a in range(times):
            scale = sy_ref[:, :1] * sx_ref[:, span]
            out_ref[:, a, span] = (
                scale * natural[a * rows : (a + 1) * rows] - white_ref[:, a, span]
            )


def whitened_gradient(place, kept, got, sx, sy, white):
    return pl.pallas_call(
        gradient_kernel,
        out_shape=jax.ShapeDtypeStruct(white.shape, jnp.float32),
        in_specs=[SMEM] + [VMEM] * 5,
        out_specs=VMEM,
        name="whitened_gradient",
    )(place, kept, got, sx, sy, white)


def with_core(block):
    return block, shifted(block, "core", 1)


def local(event_counts, latent_mean, latent_var, eigen_basis, spectrum, correlation, whitened):
    hi, core = lax.axis_index("hi"), lax.axis_index("core")
    y, z, lo = (lax.axis_index(axis) for axis in ROW)
    time = hi * 2 + core
    ny, nz = lax.axis_size("y"), lax.axis_size("z")
    place = jnp.stack([lo, time, y, z]).astype(jnp.int32)

    kept, sent = split_columns(place, eigen_basis)
    other = shifted(sent, "lo", 1)
    mine = jnp.where(lo == 0, jnp.concatenate([kept, other]), jnp.concatenate([other, kept]))
    pseudo = moments(event_counts, latent_mean, latent_var).astype(jnp.bfloat16)[0]
    mine, pseudo = lax.optimization_barrier((mine, pseudo))
    far, before, after = [shifted(pseudo, RING, step) for step in (2, 1, 3)]
    block = jnp.stack([mine] + [shifted(mine, "y", step) for step in (1, 3, 2)])
    own = with_core(pseudo)

    flips = jnp.array([0, 1, 2, 3], jnp.int32)
    before_flip, after_flip = 2 * (1 - lo), 2 * lo
    crossed = jnp.stack([before_flip, before_flip + 1, after_flip, after_flip + 1])
    slices = lax.bitwise_xor(time, jnp.concatenate([flips, crossed])).astype(jnp.int32)
    factor = time_factor(correlation[0], 4)
    mix = jnp.take(factor, slices, axis=0)
    root = jnp.sqrt(spectrum)
    sx = lax.dynamic_slice_in_dim(root, time * 1024, 1024, 0)[None]
    row = (y * nz + z) * 2 + lo
    sy = lax.dynamic_slice_in_dim(root.reshape(4, lax.axis_size(ROW), -1), row, 1, 1).reshape(-1, 1)
    sy = jnp.broadcast_to(sy, (sy.shape[0], 128))

    right, left = shifted(block, "z", 1), shifted(block, "z", nz - 1)
    pieces = [block, right, left]
    right, left, before, after = lax.optimization_barrier((right, left, before, after))
    before, after = with_core(before), with_core(after)
    right, left = shifted(right, "z", 1), shifted(left, "z", nz - 1)
    pieces += [right, left]
    right, left, far, own, mix, sx, sy = lax.optimization_barrier(
        (right, left, far, own, mix, sx, sy)
    )
    far = with_core(far)
    right, left = shifted(right, "z", 1), shifted(left, "z", nz - 1)
    pieces += [right, left]
    right, left, far, before, after = lax.optimization_barrier((right, left, far, before, after))
    last = [shifted(right[:2], "z", 1), shifted(left[2:], "z", nz - 1)]

    fields = (*own, *far, *before, *after)
    near = near_product(place, fields, pieces)
    partial_y = first_product(mix, place, fields, last, near)
    pieces += last

    modes, width = partial_y.shape
    sent = partial_y.reshape(ny * nz, modes // (ny * nz), width)
    got = lax.all_to_all(sent, ("y", "z"), 0, 0, tiled=True)
    got = got.reshape(ny * nz, modes // (ny * nz), 4, width // 4)
    got = got.transpose(2, 1, 0, 3).reshape(4, modes // (ny * nz), -1)
    far, before, after = [shifted(got, RING, step) for step in (2, 1, 3)]
    done = (
        band_product(place, with_core(got), pieces),
        band_product(place, (*with_core(before), *with_core(after)), pieces),
    )
    kept, sent = last_product(place, slices, with_core(far), pieces, done)
    got = shifted(sent, "lo", 1)

    white = whitened.reshape(-1, *whitened.shape[3:])
    gradient = whitened_gradient(place, kept, got, sx, sy, white)
    return gradient.reshape(whitened.shape)


def solution(mesh):
    finer = Mesh(mesh.devices.reshape(2, 2, 4, 8, 2), ("hi", "core", "y", "z", "lo"))
    placed = (
        P(TM, ROW, None),
        P(TM, ROW, None),
        P(TM, ROW, None),
        P(ROW, TM),
        P(),
        P(),
        P(None, ROW, None, None, TM),
    )
    return jax.shard_map(
        local,
        mesh=finer,
        in_specs=placed,
        out_specs=P(None, ROW, None, None, TM),
        check_vma=False,
    )
```

```python
import math

import jax
import jax.numpy as jnp
from jax import lax
from jax.experimental import pallas as pl
from jax.experimental.pallas import tpu as pltpu
from jax.sharding import Mesh
from jax.sharding import PartitionSpec as P

TM = ("hi", "core")
ROW = ("y", "z", "lo")
RING = ("hi", "lo")

HERMITE_NODES = (
    -2.0201828704560856,
    -0.9585724646138185,
    0.0,
    0.9585724646138185,
    2.0201828704560856,
)
HERMITE_WEIGHTS = (
    0.019953242059045913,
    0.3936193231522412,
    0.9453087204829419,
    0.3936193231522412,
    0.019953242059045913,
)
GRANT = 20 << 20
VMEM = pl.BlockSpec(memory_space=pltpu.VMEM)
SMEM = pl.BlockSpec(memory_space=pltpu.SMEM)


def moments(event_counts, latent_mean, latent_var):
    spread = jnp.sqrt(2.0 * latent_var)
    normal = 1.0 / math.sqrt(math.pi)
    points = [latent_mean + spread * abscissa for abscissa in HERMITE_NODES]
    rate_points = [jnp.exp(value) for value in points]
    mean_rate = sum(
        (weight * normal * value for weight, value in zip(HERMITE_WEIGHTS, rate_points))
    )
    covariance = sum(
        (
            weight * normal * (node_value - latent_mean) * (value - mean_rate)
            for weight, node_value, value in zip(HERMITE_WEIGHTS, points, rate_points)
        )
    )
    rate_var = sum(
        (
            weight * normal * (value - mean_rate) * (value - mean_rate)
            for weight, value in zip(HERMITE_WEIGHTS, rate_points)
        )
    )
    slope_gain = covariance / latent_var
    noise_var = rate_var - slope_gain * covariance + mean_rate
    return slope_gain * (event_counts.astype(latent_mean.dtype) - mean_rate) / noise_var


def time_factor(correlation, total):
    later = jnp.arange(total)[:, None]
    earlier = jnp.arange(total)[None, :]
    distance = jnp.maximum(later - earlier, 0).astype(correlation.dtype)
    lower = jnp.where(later >= earlier, jnp.power(correlation, distance), jnp.zeros_like(distance))
    column_scale = jnp.where(
        earlier == 0,
        jnp.ones_like(distance),
        jnp.sqrt(1.0 - correlation * correlation) * jnp.ones_like(distance),
    )
    return lower * column_scale


def shifted(array, axis, step):
    size = lax.axis_size(axis)
    return lax.ppermute(array, axis, [(k, (k + step) % size) for k in range(size)])


def split_kernel(first_ref, basis_ref, kept_ref, sent_ref):
    source = lax.broadcasted_iota(jnp.int32, (256, 128), 0)
    target = lax.broadcasted_iota(jnp.int32, (256, 128), 1)
    for half, ref in ((first_ref[0], kept_ref), (1 - first_ref[0], sent_ref)):
        match = source == (target // 8) * 16 + half * 8 + lax.rem(target, 8)
        chosen = match.astype(jnp.float32).astype(jnp.bfloat16)
        for block in range(basis_ref.shape[1] // 256):
            moved = jnp.dot(
                basis_ref[:, block * 256 : block * 256 + 256],
                chosen,
                preferred_element_type=jnp.float32,
            )
            ref[:, block * 128 : block * 128 + 128] = moved.astype(jnp.bfloat16)


def split_columns(place, basis):
    rows, columns = basis.shape
    half = jax.ShapeDtypeStruct((rows, columns // 2), basis.dtype)
    return pl.pallas_call(
        split_kernel,
        out_shape=(half, half),
        in_specs=[SMEM, VMEM],
        out_specs=(VMEM, VMEM),
        compiler_params=pltpu.CompilerParams(vmem_limit_bytes=GRANT),
        name="split_columns",
    )(place, basis)


def columns_at(ref, index):
    return pl.ds(pl.multiple_of(index * 128, 128), 128)


def product_of(place_ref, load, steps, pieces, acc_ref):
    y_here, z_here = place_ref[2], place_ref[3]
    for (step, parts), ref in zip(steps, pieces):
        at = lax.rem(z_here + step, 8)
        where = [columns_at(ref, lax.rem(y_here + part, 4) * 8 + at) for part in parts]
        field = jnp.concatenate([load(span) for span in where], axis=1)
        basis = jnp.concatenate([ref[k] for k in range(len(parts))], axis=0)
        acc_ref[...] += jnp.dot(field, basis, preferred_element_type=jnp.float32)


NEAR = tuple((step, (0, 3, 1, 2)) for step in (0, 7, 1, 6, 2, 5, 3))
FAR = ((4, (0, 3)), (4, (1, 2)))


def near_kernel(place_ref, *refs):
    blocks, pieces, acc_ref = refs[:8], refs[8:-1], refs[-1]
    acc_ref[...] = jnp.zeros_like(acc_ref)

    def load(span):
        return jnp.concatenate([ref[:, span] for ref in blocks], axis=0)

    product_of(place_ref, load, NEAR, pieces, acc_ref)


def near_product(place, fields, pieces):
    rows = sum(field.shape[0] for field in fields)
    width = pieces[0].shape[-1]
    return pl.pallas_call(
        near_kernel,
        out_shape=jax.ShapeDtypeStruct((rows, width), jnp.float32),
        in_specs=[SMEM] + [VMEM] * 15,
        out_specs=VMEM,
        compiler_params=pltpu.CompilerParams(vmem_limit_bytes=GRANT),
        cost_estimate=pl.CostEstimate(
            flops=2 * rows * 3584 * width, bytes_accessed=8 << 20, transcendentals=0
        ),
        name="near_product",
    )(place, *fields, *pieces)


def first_kernel(mix_ref, place_ref, *refs):
    blocks, pieces, near_ref, out_ref, acc_ref, tmp_ref = refs[:8], refs[8:10], *refs[10:]
    rows = blocks[0].shape[0]
    lo = place_ref[0]
    acc_ref[...] = near_ref[...]

    def load(span):
        return jnp.concatenate([ref[:, span] for ref in blocks], axis=0)

    product_of(place_ref, load, FAR, pieces, acc_ref)
    for a in range(4):
        for group in range(2):
            mixed = sum(
                mix_ref[group * 4 + t, a]
                * acc_ref[(group * 4 + t) * rows : (group * 4 + t + 1) * rows, :]
                for t in range(4)
            )
            at = lo if group == 0 else 1 - lo
            tmp_ref[pl.ds(pl.multiple_of(at * rows, rows), rows), :] = mixed
        out_ref[:, a * 2 * rows : (a + 1) * 2 * rows] = tmp_ref[...].T.astype(jnp.bfloat16)


def first_product(mix, place, fields, pieces, near):
    rows = fields[0].shape[0]
    width = near.shape[-1]
    return pl.pallas_call(
        first_kernel,
        out_shape=jax.ShapeDtypeStruct((width, 8 * rows), jnp.bfloat16),
        in_specs=[SMEM, SMEM] + [VMEM] * 11,
        out_specs=VMEM,
        scratch_shapes=[
            pltpu.VMEM((8 * rows, width), jnp.float32),
            pltpu.VMEM((2 * rows, width), jnp.float32),
        ],
        compiler_params=pltpu.CompilerParams(vmem_limit_bytes=GRANT),
        cost_estimate=pl.CostEstimate(
            flops=2 * 8 * rows * 512 * width, bytes_accessed=4 << 20, transcendentals=0
        ),
        name="first_product",
    )(mix, place, *fields, *pieces, near)


def load_bands(fields, which, span):
    return jnp.concatenate([ref[which, :, span] for ref in fields], axis=0)


def natural_rows(place_ref, slice_ref, acc_ref, rows_ref):
    times, group = 4, 8
    for b in range(8):
        half_of = place_ref[0] if b < 4 else 1 - place_ref[0]
        to = pl.multiple_of((slice_ref[b] * 2 + half_of) * group, group)
        for a in range(times):
            first = (b * times + a) * group
            rows_ref[a, pl.ds(to, group), :] = acc_ref[first : first + group, :]


def moved_columns(half):
    source = lax.broadcasted_iota(jnp.int32, (128, 256), 0)
    target = lax.broadcasted_iota(jnp.int32, (128, 256), 1)
    return (target == (source // 8) * 16 + half * 8 + lax.rem(source, 8)).astype(jnp.float32)


def sent_kernel(place_ref, slice_ref, *refs):
    fields, pieces, (sent_ref, acc_ref, rows_ref) = refs[:8], refs[8:17], refs[17:]
    acc_ref[...] = jnp.zeros_like(acc_ref)
    which = 1 - place_ref[0]
    product_of(
        place_ref, lambda span: load_bands(fields, which, span), NEAR + FAR, pieces, acc_ref
    )
    natural_rows(place_ref, slice_ref, acc_ref, rows_ref)
    sent_ref[...] = rows_ref[...].astype(jnp.bfloat16)


def kept_kernel(place_ref, slice_ref, *refs):
    fields, pieces, (sx_ref, sy_ref, white_ref) = refs[:8], refs[8:17], refs[17:20]
    kept_ref, acc_ref, rows_ref = refs[20:]
    acc_ref[...] = jnp.zeros_like(acc_ref)
    lo = place_ref[0]
    product_of(place_ref, lambda span: load_bands(fields, lo, span), NEAR + FAR, pieces, acc_ref)
    natural_rows(place_ref, slice_ref, acc_ref, rows_ref)
    chosen = moved_columns(lo)
    for block in range(rows_ref.shape[-1] // 128):
        span = slice(block * 256, block * 256 + 256)
        scale = sy_ref[:, :1] * sx_ref[:, span]
        for a in range(rows_ref.shape[0]):
            moved = jnp.dot(
                rows_ref[a, :, block * 128 : block * 128 + 128],
                chosen,
                precision=lax.Precision.HIGHEST,
            )
            kept_ref[a, :, span] = scale * moved - white_ref[:, a, span]


def band_products(kernel, name, place, slices, fields, pieces, more, out_shape):
    _, rows, total = fields[0].shape
    width = pieces[0].shape[-1]
    count = len(fields) * rows
    return pl.pallas_call(
        kernel,
        out_shape=out_shape,
        in_specs=[SMEM, SMEM] + [VMEM] * (17 + len(more)),
        out_specs=VMEM,
        scratch_shapes=[
            pltpu.VMEM((count, width), jnp.float32),
            pltpu.VMEM((4, count // 4, width), jnp.float32),
        ],
        compiler_params=pltpu.CompilerParams(vmem_limit_bytes=GRANT),
        cost_estimate=pl.CostEstimate(
            flops=2 * count * total * width, bytes_accessed=6 << 20, transcendentals=0
        ),
        name=name,
    )(place, slices, *fields, *pieces, *more)


def gradient_kernel(place_ref, kept_ref, got_ref, sx_ref, sy_ref, out_ref):
    chosen = moved_columns(1 - place_ref[0]).astype(jnp.bfloat16)
    for block in range(got_ref.shape[-1] // 128):
        span = slice(block * 256, block * 256 + 256)
        scale = sy_ref[:, :1] * sx_ref[:, span]
        for a in range(got_ref.shape[0]):
            moved = jnp.dot(
                got_ref[a, :, block * 128 : block * 128 + 128],
                chosen,
                preferred_element_type=jnp.float32,
            )
            out_ref[:, a, span] = kept_ref[a, :, span] + scale * moved


def whitened_gradient(place, kept, got, sx, sy):
    times, rows, width = kept.shape
    return pl.pallas_call(
        gradient_kernel,
        out_shape=jax.ShapeDtypeStruct((rows, times, width), jnp.float32),
        in_specs=[SMEM] + [VMEM] * 4,
        out_specs=VMEM,
        compiler_params=pltpu.CompilerParams(vmem_limit_bytes=GRANT),
        name="whitened_gradient",
    )(place, kept, got, sx, sy)


def with_core(block):
    return block, shifted(block, "core", 1)


def local(event_counts, latent_mean, latent_var, eigen_basis, spectrum, correlation, whitened):
    hi, core = lax.axis_index("hi"), lax.axis_index("core")
    y, z, lo = (lax.axis_index(axis) for axis in ROW)
    time = hi * 2 + core
    ny, nz = lax.axis_size("y"), lax.axis_size("z")
    place = jnp.stack([lo, time, y, z]).astype(jnp.int32)

    kept, sent = split_columns(place, eigen_basis)
    other = shifted(sent, "lo", 1)
    mine = jnp.where(lo == 0, jnp.concatenate([kept, other]), jnp.concatenate([other, kept]))
    pseudo = moments(event_counts, latent_mean, latent_var).astype(jnp.bfloat16)[0]
    mine, pseudo = lax.optimization_barrier((mine, pseudo))
    far, before, after = [shifted(pseudo, RING, step) for step in (2, 1, 3)]
    block = jnp.stack([mine] + [shifted(mine, "y", step) for step in (1, 3, 2)])
    own = with_core(pseudo)

    flips = jnp.array([0, 1, 2, 3], jnp.int32)
    before_flip, after_flip = 2 * (1 - lo), 2 * lo
    crossed = jnp.stack([before_flip, before_flip + 1, after_flip, after_flip + 1])
    slices = lax.bitwise_xor(time, jnp.concatenate([flips, crossed])).astype(jnp.int32)
    factor = time_factor(correlation[0], 4)
    mix = jnp.take(factor, slices, axis=0)
    root = jnp.sqrt(spectrum)
    sx = lax.dynamic_slice_in_dim(root, time * 1024, 1024, 0)[None]
    row = (y * nz + z) * 2 + lo
    sy = lax.dynamic_slice_in_dim(root.reshape(4, lax.axis_size(ROW), -1), row, 1, 1).reshape(-1, 1)
    sy = jnp.broadcast_to(sy, (sy.shape[0], 128))

    right, left = shifted(block, "z", 1), shifted(block, "z", nz - 1)
    pieces = [block, right, left]
    right, left, before, after = lax.optimization_barrier((right, left, before, after))
    before, after = with_core(before), with_core(after)
    right, left = shifted(right, "z", 1), shifted(left, "z", nz - 1)
    pieces += [right, left]
    right, left, far, own, mix, sx, sy = lax.optimization_barrier(
        (right, left, far, own, mix, sx, sy)
    )
    far = with_core(far)
    right, left = shifted(right, "z", 1), shifted(left, "z", nz - 1)
    pieces += [right, left]
    right, left, far, before, after = lax.optimization_barrier((right, left, far, before, after))
    last = [shifted(right[:2], "z", 1), shifted(left[2:], "z", nz - 1)]

    fields = (*own, *far, *before, *after)
    near = near_product(place, fields, pieces)
    partial_y = first_product(mix, place, fields, last, near)
    pieces += last

    modes, width = partial_y.shape
    sent = partial_y.reshape(ny * nz, modes // (ny * nz), width)
    got = lax.all_to_all(sent, ("y", "z"), 0, 0, tiled=True)
    got = got.reshape(ny * nz, 2, modes // (2 * ny * nz), 4, width // 4)
    got = got.transpose(1, 3, 2, 0, 4).reshape(2, 4 * (modes // (2 * ny * nz)), -1)
    far, before, after = [shifted(got, RING, step) for step in (2, 1, 3)]
    bands = tuple(b for block in (got, far, before, after) for b in with_core(block))
    white = whitened.reshape(-1, *whitened.shape[3:])
    part = (4, white.shape[0], pieces[0].shape[-1])
    sent = jax.ShapeDtypeStruct(part, jnp.bfloat16)
    sent = band_products(sent_kernel, "sent_rows", place, slices, bands, pieces, (), sent)
    got = shifted(sent, "lo", 1)
    kept = jax.ShapeDtypeStruct((*part[:2], 2 * part[2]), jnp.float32)
    more = (sx, sy, white)
    kept = band_products(kept_kernel, "kept_rows", place, slices, bands, pieces, more, kept)
    gradient = whitened_gradient(place, kept, got, sx, sy)
    return gradient.reshape(whitened.shape)


def solution(mesh):
    finer = Mesh(mesh.devices.reshape(2, 2, 4, 8, 2), ("hi", "core", "y", "z", "lo"))
    placed = (
        P(TM, ROW, None),
        P(TM, ROW, None),
        P(TM, ROW, None),
        P(ROW, TM),
        P(),
        P(),
        P(None, ROW, None, None, TM),
    )
    return jax.shard_map(
        local,
        mesh=finer,
        in_specs=placed,
        out_specs=P(None, ROW, None, None, TM),
        check_vma=False,
    )
```

```python
import math

import jax
import jax.numpy as jnp
from jax import lax
from jax.experimental import pallas as pl
from jax.experimental.pallas import tpu as pltpu
from jax.sharding import Mesh
from jax.sharding import PartitionSpec as P

TM = ("hi", "core")
ROW = ("y", "z", "lo")
RING = ("hi", "lo")

HERMITE_NODES = (
    -2.0201828704560856,
    -0.9585724646138185,
    0.0,
    0.9585724646138185,
    2.0201828704560856,
)
HERMITE_WEIGHTS = (
    0.019953242059045913,
    0.3936193231522412,
    0.9453087204829419,
    0.3936193231522412,
    0.019953242059045913,
)
GRANT = 20 << 20
VMEM = pl.BlockSpec(memory_space=pltpu.VMEM)
SMEM = pl.BlockSpec(memory_space=pltpu.SMEM)


def moments(event_counts, latent_mean, latent_var):
    spread = jnp.sqrt(2.0 * latent_var)
    normal = 1.0 / math.sqrt(math.pi)
    points = [latent_mean + spread * abscissa for abscissa in HERMITE_NODES]
    rate_points = [jnp.exp(value) for value in points]
    mean_rate = sum(
        (weight * normal * value for weight, value in zip(HERMITE_WEIGHTS, rate_points))
    )
    covariance = sum(
        (
            weight * normal * (node_value - latent_mean) * (value - mean_rate)
            for weight, node_value, value in zip(HERMITE_WEIGHTS, points, rate_points)
        )
    )
    rate_var = sum(
        (
            weight * normal * (value - mean_rate) * (value - mean_rate)
            for weight, value in zip(HERMITE_WEIGHTS, rate_points)
        )
    )
    slope_gain = covariance / latent_var
    noise_var = rate_var - slope_gain * covariance + mean_rate
    return slope_gain * (event_counts.astype(latent_mean.dtype) - mean_rate) / noise_var


def time_factor(correlation, total):
    later = jnp.arange(total)[:, None]
    earlier = jnp.arange(total)[None, :]
    distance = jnp.maximum(later - earlier, 0).astype(correlation.dtype)
    lower = jnp.where(later >= earlier, jnp.power(correlation, distance), jnp.zeros_like(distance))
    column_scale = jnp.where(
        earlier == 0,
        jnp.ones_like(distance),
        jnp.sqrt(1.0 - correlation * correlation) * jnp.ones_like(distance),
    )
    return lower * column_scale


def shifted(array, axis, step):
    size = lax.axis_size(axis)
    return lax.ppermute(array, axis, [(k, (k + step) % size) for k in range(size)])


def split_kernel(first_ref, basis_ref, kept_ref, sent_ref):
    source = lax.broadcasted_iota(jnp.int32, (256, 128), 0)
    target = lax.broadcasted_iota(jnp.int32, (256, 128), 1)
    for half, ref in ((first_ref[0], kept_ref), (1 - first_ref[0], sent_ref)):
        match = source == (target // 8) * 16 + half * 8 + lax.rem(target, 8)
        chosen = match.astype(jnp.float32).astype(jnp.bfloat16)
        for block in range(basis_ref.shape[1] // 256):
            moved = jnp.dot(
                basis_ref[:, block * 256 : block * 256 + 256],
                chosen,
                preferred_element_type=jnp.float32,
            )
            ref[:, block * 128 : block * 128 + 128] = moved.astype(jnp.bfloat16)


def split_columns(place, basis):
    rows, columns = basis.shape
    half = jax.ShapeDtypeStruct((rows, columns // 2), basis.dtype)
    return pl.pallas_call(
        split_kernel,
        out_shape=(half, half),
        in_specs=[SMEM, VMEM],
        out_specs=(VMEM, VMEM),
        compiler_params=pltpu.CompilerParams(vmem_limit_bytes=GRANT),
        name="split_columns",
    )(place, basis)


def columns_at(index):
    return pl.ds(pl.multiple_of(index * 128, 128), 128)


def product_of(place_ref, load, spec, pieces, acc_ref):
    acc_ref[...] = jnp.zeros_like(acc_ref)
    y_here, z_here = place_ref[2], place_ref[3]
    for blocks, ref in zip(spec, pieces):
        where = [
            columns_at(lax.rem(y_here + dy, 4) * 8 + lax.rem(z_here + dz, 8)) for dz, dy in blocks
        ]
        field = jnp.concatenate([load(span) for span in where], axis=1)
        basis = jnp.concatenate([ref[k] for k in range(len(blocks))], axis=0)
        acc_ref[...] += jnp.dot(field, basis, preferred_element_type=jnp.float32)


NEAR = (
    ((0, 0), (0, 1)),
    ((0, 2),),
    ((0, 3),),
    ((7, 0), (7, 1)),
    ((1, 0), (1, 1)),
    ((7, 2), (1, 2)),
    ((7, 3), (1, 3)),
    ((6, 0), (6, 1)),
    ((2, 0), (2, 1)),
    ((6, 2), (2, 2)),
    ((6, 3), (2, 3)),
    ((5, 0), (5, 1)),
    ((3, 0), (3, 1)),
)
FAR = (
    ((5, 2), (3, 2)),
    ((5, 3), (3, 3)),
    ((4, 0),),
    ((4, 1),),
    ((4, 2),),
    ((4, 3),),
)


def near_kernel(place_ref, *refs):
    blocks, pieces, acc_ref = refs[:8], refs[8:-1], refs[-1]

    def load(span):
        return jnp.concatenate([ref[:, span] for ref in blocks], axis=0)

    product_of(place_ref, load, NEAR, pieces, acc_ref)


def near_product(place, fields, pieces):
    rows = sum(field.shape[0] for field in fields)
    width = pieces[0].shape[-1]
    return pl.pallas_call(
        near_kernel,
        out_shape=jax.ShapeDtypeStruct((rows, width), jnp.float32),
        in_specs=[SMEM] + [VMEM] * (8 + len(pieces)),
        out_specs=VMEM,
        compiler_params=pltpu.CompilerParams(vmem_limit_bytes=GRANT),
        cost_estimate=pl.CostEstimate(
            flops=2 * rows * 3072 * width, bytes_accessed=8 << 20, transcendentals=0
        ),
        name="near_product",
    )(place, *fields, *pieces)


def first_kernel(mix_ref, place_ref, *refs):
    blocks, pieces, (near_ref, out_ref, acc_ref, tmp_ref) = refs[:8], refs[8:-4], refs[-4:]
    rows = blocks[0].shape[0]
    lo = place_ref[0]

    def load(span):
        return jnp.concatenate([ref[:, span] for ref in blocks], axis=0)

    product_of(place_ref, load, FAR, pieces, acc_ref)
    acc_ref[...] += near_ref[...]
    for a in range(4):
        for group in range(2):
            mixed = sum(
                mix_ref[group * 4 + t, a]
                * acc_ref[(group * 4 + t) * rows : (group * 4 + t + 1) * rows, :]
                for t in range(4)
            )
            at = lo if group == 0 else 1 - lo
            tmp_ref[pl.ds(pl.multiple_of(at * rows, rows), rows), :] = mixed
        out_ref[:, a * 2 * rows : (a + 1) * 2 * rows] = tmp_ref[...].T.astype(jnp.bfloat16)


def first_product(mix, place, fields, pieces, near):
    rows = fields[0].shape[0]
    width = near.shape[-1]
    return pl.pallas_call(
        first_kernel,
        out_shape=jax.ShapeDtypeStruct((width, 8 * rows), jnp.bfloat16),
        in_specs=[SMEM, SMEM] + [VMEM] * (9 + len(pieces)),
        out_specs=VMEM,
        scratch_shapes=[
            pltpu.VMEM((8 * rows, width), jnp.float32),
            pltpu.VMEM((2 * rows, width), jnp.float32),
        ],
        compiler_params=pltpu.CompilerParams(vmem_limit_bytes=GRANT),
        cost_estimate=pl.CostEstimate(
            flops=2 * 8 * rows * 1024 * width, bytes_accessed=4 << 20, transcendentals=0
        ),
        name="first_product",
    )(mix, place, *fields, *pieces, near)


def load_bands(fields, which, span):
    return jnp.concatenate([ref[which, :, span] for ref in fields], axis=0)


def natural_place(slice_ref, half_of, block):
    return pl.multiple_of((slice_ref[block] * 2 + half_of) * 8, 8)


def moved_columns(half):
    source = lax.broadcasted_iota(jnp.int32, (128, 256), 0)
    target = lax.broadcasted_iota(jnp.int32, (128, 256), 1)
    return (target == (source // 8) * 16 + half * 8 + lax.rem(source, 8)).astype(jnp.float32)


def sent_kernel(place_ref, *refs):
    count = len(refs) - len(NEAR + FAR) - 2
    fields, pieces, (sent_ref, acc_ref) = refs[:count], refs[count:-2], refs[-2:]
    which = 1 - place_ref[0]
    product_of(
        place_ref, lambda span: load_bands(fields, which, span), NEAR + FAR, pieces, acc_ref
    )
    sent_ref[...] = acc_ref[...].astype(jnp.bfloat16)


def sent_rows(place, fields, pieces):
    count = sum(field.shape[1] for field in fields)
    total, width = fields[0].shape[-1], pieces[0].shape[-1]
    return pl.pallas_call(
        sent_kernel,
        out_shape=jax.ShapeDtypeStruct((count, width), jnp.bfloat16),
        in_specs=[SMEM] + [VMEM] * (len(fields) + len(pieces)),
        out_specs=VMEM,
        scratch_shapes=[pltpu.VMEM((count, width), jnp.float32)],
        compiler_params=pltpu.CompilerParams(vmem_limit_bytes=GRANT),
        cost_estimate=pl.CostEstimate(
            flops=2 * count * total * width, bytes_accessed=6 << 20, transcendentals=0
        ),
        name="sent_rows",
    )(place, *fields, *pieces)


def kept_kernel(place_ref, slice_ref, *refs):
    count = len(refs) - len(NEAR + FAR) - 6
    fields, pieces = refs[:count], refs[count:-6]
    sx_ref, sy_ref, white_ref, kept_ref, acc_ref, rows_ref = refs[-6:]
    lo = place_ref[0]
    product_of(place_ref, lambda span: load_bands(fields, lo, span), NEAR + FAR, pieces, acc_ref)
    for b in range(8):
        to = natural_place(slice_ref, lo if b < 4 else 1 - lo, b)
        for a in range(4):
            first = (b * 4 + a) * 8
            rows_ref[a, pl.ds(to, 8), :] = acc_ref[first : first + 8, :]
    chosen = moved_columns(lo)
    for block in range(rows_ref.shape[-1] // 128):
        span = slice(block * 256, block * 256 + 256)
        scale = sy_ref[:, :1] * sx_ref[:, span]
        for a in range(rows_ref.shape[0]):
            moved = jnp.dot(
                rows_ref[a, :, block * 128 : block * 128 + 128],
                chosen,
                precision=lax.Precision.HIGHEST,
            )
            kept_ref[a, :, span] = scale * moved - white_ref[:, a, span]


def kept_rows(place, slices, fields, pieces, sx, sy, white):
    count = sum(field.shape[1] for field in fields)
    total, width = fields[0].shape[-1], pieces[0].shape[-1]
    rows, times, columns = white.shape
    return pl.pallas_call(
        kept_kernel,
        out_shape=jax.ShapeDtypeStruct((times, rows, columns), jnp.float32),
        in_specs=[SMEM, SMEM] + [VMEM] * (len(fields) + len(pieces) + 3),
        out_specs=VMEM,
        scratch_shapes=[
            pltpu.VMEM((count, width), jnp.float32),
            pltpu.VMEM((times, rows, width), jnp.float32),
        ],
        compiler_params=pltpu.CompilerParams(vmem_limit_bytes=GRANT),
        cost_estimate=pl.CostEstimate(
            flops=2 * count * total * width, bytes_accessed=6 << 20, transcendentals=0
        ),
        name="kept_rows",
    )(place, slices, *fields, *pieces, sx, sy, white)


def gradient_kernel(place_ref, slice_ref, kept_ref, early_ref, late_ref, sx_ref, sy_ref, out_ref):
    lo = place_ref[0]
    chosen = moved_columns(1 - lo).astype(jnp.bfloat16)
    for block in range(early_ref.shape[-1] // 128):
        here = slice(block * 128, block * 128 + 128)
        span = slice(block * 256, block * 256 + 256)
        for ref, sources in ((early_ref, (0, 1, 4, 5, 6, 7)), (late_ref, (2, 3))):
            moved = jnp.dot(ref[:, here], chosen, preferred_element_type=jnp.float32)
            for k, b in enumerate(sources):
                to = natural_place(slice_ref, 1 - lo if b < 4 else lo, b)
                scale = sy_ref[pl.ds(to, 8), :1] * sx_ref[:, span]
                for a in range(4):
                    first = (k * 4 + a) * 8
                    out_ref[pl.ds(to, 8), a, span] = (
                        kept_ref[a, pl.ds(to, 8), span] + scale * moved[first : first + 8]
                    )


def whitened_gradient(place, slices, kept, early, late, sx, sy):
    times, rows, width = kept.shape
    return pl.pallas_call(
        gradient_kernel,
        out_shape=jax.ShapeDtypeStruct((rows, times, width), jnp.float32),
        in_specs=[SMEM, SMEM] + [VMEM] * 5,
        out_specs=VMEM,
        compiler_params=pltpu.CompilerParams(vmem_limit_bytes=GRANT),
        name="whitened_gradient",
    )(place, slices, kept, early, late, sx, sy)


def with_core(block):
    return block, shifted(block, "core", 1)


def local(event_counts, latent_mean, latent_var, eigen_basis, spectrum, correlation, whitened):
    hi, core = lax.axis_index("hi"), lax.axis_index("core")
    y, z, lo = (lax.axis_index(axis) for axis in ROW)
    time = hi * 2 + core
    ny, nz = lax.axis_size("y"), lax.axis_size("z")
    place = jnp.stack([lo, time, y, z]).astype(jnp.int32)

    kept, sent = split_columns(place, eigen_basis)
    other = shifted(sent, "lo", 1)
    mine = jnp.where(lo == 0, jnp.concatenate([kept, other]), jnp.concatenate([other, kept]))
    pseudo = moments(event_counts, latent_mean, latent_var).astype(jnp.bfloat16)[0]
    mine, pseudo = lax.optimization_barrier((mine, pseudo))
    next_y = shifted(mine, "y", 3)
    far, before, after = [shifted(pseudo, RING, step) for step in (2, 1, 3)]
    block = jnp.stack([mine, next_y])
    own = with_core(pseudo)

    flips = jnp.array([0, 1, 2, 3], jnp.int32)
    before_flip, after_flip = 2 * (1 - lo), 2 * lo
    crossed = jnp.stack([before_flip, before_flip + 1, after_flip, after_flip + 1])
    slices = lax.bitwise_xor(time, jnp.concatenate([flips, crossed])).astype(jnp.int32)
    swapped = jnp.concatenate([slices[:4], slices[6:], slices[4:6]])
    factor = time_factor(correlation[0], 4)
    mix = jnp.take(factor, slices, axis=0)
    root = jnp.sqrt(spectrum)
    sx = lax.dynamic_slice_in_dim(root, time * 1024, 1024, 0)[None]
    row = (y * nz + z) * 2 + lo
    sy = lax.dynamic_slice_in_dim(root.reshape(4, lax.axis_size(ROW), -1), row, 1, 1).reshape(-1, 1)
    sy = jnp.broadcast_to(sy, (sy.shape[0], 128))

    def from_neighbours(blocks):
        second = jnp.concatenate([b[-1:] for b in blocks])
        first = jnp.concatenate([b[:1] for b in blocks])
        return [shifted(second, "y", 3), shifted(first, "y", 1)]

    right, left = shifted(block, "z", 1), shifted(block, "z", nz - 1)
    beside = from_neighbours([block])
    right, left, before, after = lax.optimization_barrier((right, left, before, after))
    pieces = [block]
    next_right, next_left = shifted(right, "z", 1), shifted(left, "z", nz - 1)
    beside_next = from_neighbours([right, left])
    before, after = with_core(before), with_core(after)
    next_right, next_left, beside, beside_next, far, own, mix, sx, sy = lax.optimization_barrier(
        (next_right, next_left, beside, beside_next, far, own, mix, sx, sy)
    )
    pieces += [*beside, right, left, *beside_next]
    right, left = next_right, next_left
    next_right, next_left = shifted(right, "z", 1), shifted(left, "z", nz - 1)
    beside = from_neighbours([right, left])
    far = with_core(far)
    next_right, next_left, beside, far, before, after = lax.optimization_barrier(
        (next_right, next_left, beside, far, before, after)
    )
    pieces += [right, left, *beside]
    right, left = next_right, next_left
    pieces += [right, left]
    ends = [shifted(right[:1], "z", 1), shifted(left[1:], "z", nz - 1)]
    last = [*from_neighbours([right, left]), *ends]
    last += [shifted(ends[1], "y", 3), shifted(ends[0], "y", 1)]

    fields = (*own, *far, *before, *after)
    near = near_product(place, fields, pieces)
    partial_y = first_product(mix, place, fields, last, near)
    pieces += last

    modes, width = partial_y.shape
    sent = partial_y.reshape(ny * nz, modes // (ny * nz), width)
    got = lax.all_to_all(sent, ("y", "z"), 0, 0, tiled=True)
    got = got.reshape(ny * nz, 2, modes // (2 * ny * nz), 4, width // 4)
    got = got.transpose(1, 3, 2, 0, 4).reshape(2, 4 * (modes // (2 * ny * nz)), -1)
    own, before, after = with_core(got), shifted(got, RING, 1), shifted(got, RING, 3)
    middle = got.shape[1] // 2
    far = [shifted(before[:, :middle], RING, 1), shifted(after[:, middle:], RING, 3)]
    before, after = with_core(before), with_core(after)
    early = sent_rows(place, (*own, *before, *after), pieces)
    far, early = lax.optimization_barrier((far, early))
    got_early = shifted(early, "lo", 1)
    far = (*far, *(shifted(half, "core", 1) for half in far))
    got_late = shifted(sent_rows(place, far, pieces), "lo", 1)
    white = whitened.reshape(-1, *whitened.shape[3:])
    kept = kept_rows(place, slices, (*own, *far, *before, *after), pieces, sx, sy, white)
    gradient = whitened_gradient(place, swapped, kept, got_early, got_late, sx, sy)
    return gradient.reshape(whitened.shape)


def solution(mesh):
    finer = Mesh(mesh.devices.reshape(2, 2, 4, 8, 2), ("hi", "core", "y", "z", "lo"))
    placed = (
        P(TM, ROW, None),
        P(TM, ROW, None),
        P(TM, ROW, None),
        P(ROW, TM),
        P(),
        P(),
        P(None, ROW, None, None, TM),
    )
    return jax.shard_map(
        local,
        mesh=finer,
        in_specs=placed,
        out_specs=P(None, ROW, None, None, TM),
        check_vma=False,
    )
```

```python
import math

import jax
import jax.numpy as jnp
from jax import lax
from jax.experimental import pallas as pl
from jax.experimental.pallas import tpu as pltpu
from jax.sharding import Mesh
from jax.sharding import PartitionSpec as P

TM = ("hi", "core")
ROW = ("y", "z", "lo")
RING = ("hi", "lo")

HERMITE_NODES = (
    -2.0201828704560856,
    -0.9585724646138185,
    0.0,
    0.9585724646138185,
    2.0201828704560856,
)
HERMITE_WEIGHTS = (
    0.019953242059045913,
    0.3936193231522412,
    0.9453087204829419,
    0.3936193231522412,
    0.019953242059045913,
)
GRANT = 20 << 20
VMEM = pl.BlockSpec(memory_space=pltpu.VMEM)
SMEM = pl.BlockSpec(memory_space=pltpu.SMEM)


def moments(event_counts, latent_mean, latent_var):
    spread = jnp.sqrt(2.0 * latent_var)
    normal = 1.0 / math.sqrt(math.pi)
    points = [latent_mean + spread * abscissa for abscissa in HERMITE_NODES]
    rate_points = [jnp.exp(value) for value in points]
    mean_rate = sum(
        (weight * normal * value for weight, value in zip(HERMITE_WEIGHTS, rate_points))
    )
    covariance = sum(
        (
            weight * normal * (node_value - latent_mean) * (value - mean_rate)
            for weight, node_value, value in zip(HERMITE_WEIGHTS, points, rate_points)
        )
    )
    rate_var = sum(
        (
            weight * normal * (value - mean_rate) * (value - mean_rate)
            for weight, value in zip(HERMITE_WEIGHTS, rate_points)
        )
    )
    slope_gain = covariance / latent_var
    noise_var = rate_var - slope_gain * covariance + mean_rate
    return slope_gain * (event_counts.astype(latent_mean.dtype) - mean_rate) / noise_var


def time_factor(correlation, total):
    later = jnp.arange(total)[:, None]
    earlier = jnp.arange(total)[None, :]
    distance = jnp.maximum(later - earlier, 0).astype(correlation.dtype)
    lower = jnp.where(later >= earlier, jnp.power(correlation, distance), jnp.zeros_like(distance))
    column_scale = jnp.where(
        earlier == 0,
        jnp.ones_like(distance),
        jnp.sqrt(1.0 - correlation * correlation) * jnp.ones_like(distance),
    )
    return lower * column_scale


def shifted(array, axis, step):
    size = lax.axis_size(axis)
    return lax.ppermute(array, axis, [(k, (k + step) % size) for k in range(size)])


def copies_along(array, axis):
    size = lax.axis_size(axis)
    return lax.all_to_all(
        jnp.broadcast_to(array[None], (size, *array.shape)), axis, 0, 0, tiled=True
    )


def split_kernel(first_ref, basis_ref, kept_ref, sent_ref):
    source = lax.broadcasted_iota(jnp.int32, (256, 128), 0)
    target = lax.broadcasted_iota(jnp.int32, (256, 128), 1)
    for half, ref in ((first_ref[0], kept_ref), (1 - first_ref[0], sent_ref)):
        match = source == (target // 8) * 16 + half * 8 + lax.rem(target, 8)
        chosen = match.astype(jnp.float32).astype(jnp.bfloat16)
        for block in range(basis_ref.shape[1] // 256):
            moved = jnp.dot(
                basis_ref[:, block * 256 : block * 256 + 256],
                chosen,
                preferred_element_type=jnp.float32,
            )
            ref[:, block * 128 : block * 128 + 128] = moved.astype(jnp.bfloat16)


def split_columns(place, basis):
    rows, columns = basis.shape
    half = jax.ShapeDtypeStruct((rows, columns // 2), basis.dtype)
    return pl.pallas_call(
        split_kernel,
        out_shape=(half, half),
        in_specs=[SMEM, VMEM],
        out_specs=(VMEM, VMEM),
        compiler_params=pltpu.CompilerParams(vmem_limit_bytes=GRANT),
        name="split_columns",
    )(place, basis)


def columns_at(index):
    return pl.ds(pl.multiple_of(index * 128, 128), 128)


def product_of(place_ref, load, spec, pieces, acc_ref):
    acc_ref[...] = jnp.zeros_like(acc_ref)
    y_here, z_here = place_ref[2], place_ref[3]
    for blocks, ref in zip(spec, pieces):
        where = [
            columns_at(lax.rem(y_here + dy, 4) * 8 + lax.rem(z_here + dz, 8)) for dz, dy in blocks
        ]
        field = jnp.concatenate([load(span) for span in where], axis=1)
        basis = jnp.concatenate([ref[k] for k in range(len(blocks))], axis=0)
        acc_ref[...] += jnp.dot(field, basis, preferred_element_type=jnp.float32)


NEAR = tuple(tuple((dz, dy) for dy in (0, 3, 1, 2)) for dz in (0, 7, 1, 6, 2, 5, 3))
FAR = (((4, 0), (4, 3)), ((4, 1), (4, 2)))


def load_fields(refs, span):
    return jnp.concatenate([ref[x, :, span] for ref in refs for x in range(4)], axis=0)


def near_kernel(place_ref, *refs):
    fields, pieces, acc_ref = refs[:2], refs[2:-1], refs[-1]
    product_of(place_ref, lambda span: load_fields(fields, span), NEAR, pieces, acc_ref)


def near_product(place, fields, pieces):
    rows = 8 * fields[0].shape[1]
    width = pieces[0].shape[-1]
    return pl.pallas_call(
        near_kernel,
        out_shape=jax.ShapeDtypeStruct((rows, width), jnp.float32),
        in_specs=[SMEM] + [VMEM] * (2 + len(pieces)),
        out_specs=VMEM,
        compiler_params=pltpu.CompilerParams(vmem_limit_bytes=GRANT),
        cost_estimate=pl.CostEstimate(
            flops=2 * rows * 3584 * width, bytes_accessed=8 << 20, transcendentals=0
        ),
        name="near_product",
    )(place, *fields, *pieces)


def first_kernel(mix_ref, place_ref, *refs):
    fields, pieces, (near_ref, out_ref, acc_ref, tmp_ref) = refs[:2], refs[2:-4], refs[-4:]
    rows = fields[0].shape[1]
    product_of(place_ref, lambda span: load_fields(fields, span), FAR, pieces, acc_ref)
    acc_ref[...] += near_ref[...]
    for a in range(4):
        for lo in range(2):
            blocks = [core * 4 + hi * 2 + lo for core in range(2) for hi in range(2)]
            tmp_ref[lo * rows : (lo + 1) * rows, :] = sum(
                mix_ref[b, a] * acc_ref[b * rows : (b + 1) * rows, :] for b in blocks
            )
        out_ref[:, a * 2 * rows : (a + 1) * 2 * rows] = tmp_ref[...].T.astype(jnp.bfloat16)


def first_product(mix, place, fields, pieces, near):
    rows = fields[0].shape[1]
    width = near.shape[-1]
    return pl.pallas_call(
        first_kernel,
        out_shape=jax.ShapeDtypeStruct((width, 8 * rows), jnp.bfloat16),
        in_specs=[SMEM, SMEM] + [VMEM] * (3 + len(pieces)),
        out_specs=VMEM,
        scratch_shapes=[
            pltpu.VMEM((8 * rows, width), jnp.float32),
            pltpu.VMEM((2 * rows, width), jnp.float32),
        ],
        compiler_params=pltpu.CompilerParams(vmem_limit_bytes=GRANT),
        cost_estimate=pl.CostEstimate(
            flops=2 * 8 * rows * 512 * width, bytes_accessed=4 << 20, transcendentals=0
        ),
        name="first_product",
    )(mix, place, *fields, *pieces, near)


def load_bands(fields, which, span):
    return jnp.concatenate([ref[which, :, span] for ref in fields], axis=0)


def natural_place(slice_ref, half_of, block):
    return pl.multiple_of((slice_ref[block] * 2 + half_of) * 8, 8)


def moved_columns(half):
    source = lax.broadcasted_iota(jnp.int32, (128, 256), 0)
    target = lax.broadcasted_iota(jnp.int32, (128, 256), 1)
    return (target == (source // 8) * 16 + half * 8 + lax.rem(source, 8)).astype(jnp.float32)


def sent_kernel(place_ref, *refs):
    count = len(refs) - len(NEAR + FAR) - 2
    fields, pieces, (sent_ref, acc_ref) = refs[:count], refs[count:-2], refs[-2:]
    which = 1 - place_ref[0]
    product_of(
        place_ref, lambda span: load_bands(fields, which, span), NEAR + FAR, pieces, acc_ref
    )
    sent_ref[...] = acc_ref[...].astype(jnp.bfloat16)


def sent_rows(place, fields, pieces):
    count = sum(field.shape[1] for field in fields)
    total, width = fields[0].shape[-1], pieces[0].shape[-1]
    return pl.pallas_call(
        sent_kernel,
        out_shape=jax.ShapeDtypeStruct((count, width), jnp.bfloat16),
        in_specs=[SMEM] + [VMEM] * (len(fields) + len(pieces)),
        out_specs=VMEM,
        scratch_shapes=[pltpu.VMEM((count, width), jnp.float32)],
        compiler_params=pltpu.CompilerParams(vmem_limit_bytes=GRANT),
        cost_estimate=pl.CostEstimate(
            flops=2 * count * total * width, bytes_accessed=6 << 20, transcendentals=0
        ),
        name="sent_rows",
    )(place, *fields, *pieces)


def kept_kernel(place_ref, slice_ref, *refs):
    count = len(refs) - len(NEAR + FAR) - 6
    fields, pieces = refs[:count], refs[count:-6]
    sx_ref, sy_ref, white_ref, kept_ref, acc_ref, rows_ref = refs[-6:]
    lo = place_ref[0]
    product_of(place_ref, lambda span: load_bands(fields, lo, span), NEAR + FAR, pieces, acc_ref)
    for b in range(8):
        to = natural_place(slice_ref, lo if b < 4 else 1 - lo, b)
        for a in range(4):
            first = (b * 4 + a) * 8
            rows_ref[a, pl.ds(to, 8), :] = acc_ref[first : first + 8, :]
    chosen = moved_columns(lo)
    for block in range(rows_ref.shape[-1] // 128):
        span = slice(block * 256, block * 256 + 256)
        scale = sy_ref[:, :1] * sx_ref[:, span]
        for a in range(rows_ref.shape[0]):
            moved = jnp.dot(
                rows_ref[a, :, block * 128 : block * 128 + 128],
                chosen,
                precision=lax.Precision.HIGHEST,
            )
            kept_ref[a, :, span] = scale * moved - white_ref[:, a, span]


def kept_rows(place, slices, fields, pieces, sx, sy, white):
    count = sum(field.shape[1] for field in fields)
    total, width = fields[0].shape[-1], pieces[0].shape[-1]
    rows, times, columns = white.shape
    return pl.pallas_call(
        kept_kernel,
        out_shape=jax.ShapeDtypeStruct((times, rows, columns), jnp.float32),
        in_specs=[SMEM, SMEM] + [VMEM] * (len(fields) + len(pieces) + 3),
        out_specs=VMEM,
        scratch_shapes=[
            pltpu.VMEM((count, width), jnp.float32),
            pltpu.VMEM((times, rows, width), jnp.float32),
        ],
        compiler_params=pltpu.CompilerParams(vmem_limit_bytes=GRANT),
        cost_estimate=pl.CostEstimate(
            flops=2 * count * total * width, bytes_accessed=6 << 20, transcendentals=0
        ),
        name="kept_rows",
    )(place, slices, *fields, *pieces, sx, sy, white)


def gradient_kernel(place_ref, slice_ref, kept_ref, early_ref, late_ref, sx_ref, sy_ref, out_ref):
    lo = place_ref[0]
    chosen = moved_columns(1 - lo).astype(jnp.bfloat16)
    for block in range(early_ref.shape[-1] // 128):
        here = slice(block * 128, block * 128 + 128)
        span = slice(block * 256, block * 256 + 256)
        for ref, sources in ((early_ref, (0, 1, 4, 5, 6, 7)), (late_ref, (2, 3))):
            moved = jnp.dot(ref[:, here], chosen, preferred_element_type=jnp.float32)
            for k, b in enumerate(sources):
                to = natural_place(slice_ref, 1 - lo if b < 4 else lo, b)
                scale = sy_ref[pl.ds(to, 8), :1] * sx_ref[:, span]
                for a in range(4):
                    first = (k * 4 + a) * 8
                    out_ref[pl.ds(to, 8), a, span] = (
                        kept_ref[a, pl.ds(to, 8), span] + scale * moved[first : first + 8]
                    )


def whitened_gradient(place, slices, kept, early, late, sx, sy):
    times, rows, width = kept.shape
    return pl.pallas_call(
        gradient_kernel,
        out_shape=jax.ShapeDtypeStruct((rows, times, width), jnp.float32),
        in_specs=[SMEM, SMEM] + [VMEM] * 5,
        out_specs=VMEM,
        compiler_params=pltpu.CompilerParams(vmem_limit_bytes=GRANT),
        name="whitened_gradient",
    )(place, slices, kept, early, late, sx, sy)


def with_core(block):
    return block, shifted(block, "core", 1)


def local(event_counts, latent_mean, latent_var, eigen_basis, spectrum, correlation, whitened):
    hi, core = lax.axis_index("hi"), lax.axis_index("core")
    y, z, lo = (lax.axis_index(axis) for axis in ROW)
    time = hi * 2 + core
    ny, nz = lax.axis_size("y"), lax.axis_size("z")
    place = jnp.stack([lo, time, y, z]).astype(jnp.int32)

    kept, sent = split_columns(place, eigen_basis)
    other = shifted(sent, "lo", 1)
    mine = jnp.where(lo == 0, jnp.concatenate([kept, other]), jnp.concatenate([other, kept]))
    pseudo = moments(event_counts, latent_mean, latent_var).astype(jnp.bfloat16)[0]
    mine, pseudo = lax.optimization_barrier((mine, pseudo))
    block = jnp.stack([mine] + [shifted(mine, "y", step) for step in (1, 3, 2)])
    field = copies_along(pseudo, RING).reshape(4, *pseudo.shape)

    flips = jnp.array([0, 1, 2, 3], jnp.int32)
    before_flip, after_flip = 2 * (1 - lo), 2 * lo
    crossed = jnp.stack([before_flip, before_flip + 1, after_flip, after_flip + 1])
    slices = lax.bitwise_xor(time, jnp.concatenate([flips, crossed])).astype(jnp.int32)
    swapped = jnp.concatenate([slices[:4], slices[6:], slices[4:6]])
    factor = time_factor(correlation[0], 4)
    early_slices = jnp.arange(4) // 2 * 2
    mix = jnp.take(factor, jnp.concatenate([early_slices + core, early_slices + 1 - core]), axis=0)
    root = jnp.sqrt(spectrum)
    sx = lax.dynamic_slice_in_dim(root, time * 1024, 1024, 0)[None]
    row = (y * nz + z) * 2 + lo
    sy = lax.dynamic_slice_in_dim(root.reshape(4, lax.axis_size(ROW), -1), row, 1, 1).reshape(-1, 1)
    sy = jnp.broadcast_to(sy, (sy.shape[0], 128))

    right, left = shifted(block, "z", 1), shifted(block, "z", nz - 1)
    pieces = [block, right, left]
    right, left = shifted(right, "z", 1), shifted(left, "z", nz - 1)
    pieces += [right, left]
    right, left, field, mix, sx, sy = lax.optimization_barrier((right, left, field, mix, sx, sy))
    fields = with_core(field)
    right, left = shifted(right, "z", 1), shifted(left, "z", nz - 1)
    pieces += [right, left]
    right, left, fields = lax.optimization_barrier((right, left, fields))
    last = [shifted(right[:2], "z", 1), shifted(left[2:], "z", nz - 1)]

    near = near_product(place, fields, pieces)
    partial_y = first_product(mix, place, fields, last, near)
    pieces += last

    modes, width = partial_y.shape
    sent = partial_y.reshape(ny * nz, modes // (ny * nz), width)
    got = lax.all_to_all(sent, ("y", "z"), 0, 0, tiled=True)
    got = got.reshape(ny * nz, 2, modes // (2 * ny * nz), 4, width // 4)
    got = got.transpose(1, 3, 2, 0, 4).reshape(2, 4 * (modes // (2 * ny * nz)), -1)
    own, before, after = with_core(got), shifted(got, RING, 1), shifted(got, RING, 3)
    middle = got.shape[1] // 2
    far = [shifted(before[:, :middle], RING, 1), shifted(after[:, middle:], RING, 3)]
    before, after = with_core(before), with_core(after)
    early = sent_rows(place, (*own, *before, *after), pieces)
    far, early = lax.optimization_barrier((far, early))
    got_early = shifted(early, "lo", 1)
    far = (*far, *(shifted(half, "core", 1) for half in far))
    got_late = shifted(sent_rows(place, far, pieces), "lo", 1)
    white = whitened.reshape(-1, *whitened.shape[3:])
    kept = kept_rows(place, slices, (*own, *far, *before, *after), pieces, sx, sy, white)
    gradient = whitened_gradient(place, swapped, kept, got_early, got_late, sx, sy)
    return gradient.reshape(whitened.shape)


def solution(mesh):
    finer = Mesh(mesh.devices.reshape(2, 2, 4, 8, 2), ("hi", "core", "y", "z", "lo"))
    placed = (
        P(TM, ROW, None),
        P(TM, ROW, None),
        P(TM, ROW, None),
        P(ROW, TM),
        P(),
        P(),
        P(None, ROW, None, None, TM),
    )
    return jax.shard_map(
        local,
        mesh=finer,
        in_specs=placed,
        out_specs=P(None, ROW, None, None, TM),
        check_vma=False,
    )
```

```python
import math

import jax
import jax.numpy as jnp
from jax import lax
from jax.experimental import pallas as pl
from jax.experimental.pallas import tpu as pltpu
from jax.sharding import Mesh
from jax.sharding import PartitionSpec as P

TM = ("hi", "core")
ROW = ("y", "z", "lo")
RING = ("hi", "lo")

HERMITE_NODES = (
    -2.0201828704560856,
    -0.9585724646138185,
    0.0,
    0.9585724646138185,
    2.0201828704560856,
)
HERMITE_WEIGHTS = (
    0.019953242059045913,
    0.3936193231522412,
    0.9453087204829419,
    0.3936193231522412,
    0.019953242059045913,
)
GRANT = 20 << 20
VMEM = pl.BlockSpec(memory_space=pltpu.VMEM)
SMEM = pl.BlockSpec(memory_space=pltpu.SMEM)


def moments(event_counts, latent_mean, latent_var):
    spread = jnp.sqrt(2.0 * latent_var)
    normal = 1.0 / math.sqrt(math.pi)
    points = [latent_mean + spread * abscissa for abscissa in HERMITE_NODES]
    rate_points = [jnp.exp(value) for value in points]
    mean_rate = sum(
        (weight * normal * value for weight, value in zip(HERMITE_WEIGHTS, rate_points))
    )
    covariance = sum(
        (
            weight * normal * (node_value - latent_mean) * (value - mean_rate)
            for weight, node_value, value in zip(HERMITE_WEIGHTS, points, rate_points)
        )
    )
    rate_var = sum(
        (
            weight * normal * (value - mean_rate) * (value - mean_rate)
            for weight, value in zip(HERMITE_WEIGHTS, rate_points)
        )
    )
    slope_gain = covariance / latent_var
    noise_var = rate_var - slope_gain * covariance + mean_rate
    return slope_gain * (event_counts.astype(latent_mean.dtype) - mean_rate) / noise_var


def time_factor(correlation, total):
    later = jnp.arange(total)[:, None]
    earlier = jnp.arange(total)[None, :]
    distance = jnp.maximum(later - earlier, 0).astype(correlation.dtype)
    lower = jnp.where(later >= earlier, jnp.power(correlation, distance), jnp.zeros_like(distance))
    column_scale = jnp.where(
        earlier == 0,
        jnp.ones_like(distance),
        jnp.sqrt(1.0 - correlation * correlation) * jnp.ones_like(distance),
    )
    return lower * column_scale


def shifted(array, axis, step):
    size = lax.axis_size(axis)
    return lax.ppermute(array, axis, [(k, (k + step) % size) for k in range(size)])


def split_kernel(first_ref, basis_ref, kept_ref, sent_ref):
    source = lax.broadcasted_iota(jnp.int32, (256, 128), 0)
    target = lax.broadcasted_iota(jnp.int32, (256, 128), 1)
    for half, ref in ((first_ref[0], kept_ref), (1 - first_ref[0], sent_ref)):
        match = source == (target // 8) * 16 + half * 8 + lax.rem(target, 8)
        chosen = match.astype(jnp.float32).astype(jnp.bfloat16)
        for block in range(basis_ref.shape[1] // 256):
            moved = jnp.dot(
                basis_ref[:, block * 256 : block * 256 + 256],
                chosen,
                preferred_element_type=jnp.float32,
            )
            ref[:, block * 128 : block * 128 + 128] = moved.astype(jnp.bfloat16)


def split_columns(place, basis):
    rows, columns = basis.shape
    half = jax.ShapeDtypeStruct((rows, columns // 2), basis.dtype)
    return pl.pallas_call(
        split_kernel,
        out_shape=(half, half),
        in_specs=[SMEM, VMEM],
        out_specs=(VMEM, VMEM),
        compiler_params=pltpu.CompilerParams(vmem_limit_bytes=GRANT),
        name="split_columns",
    )(place, basis)


def columns_at(index):
    return pl.ds(pl.multiple_of(index * 128, 128), 128)


def product_of(place_ref, load, spec, pieces, acc_ref):
    acc_ref[...] = jnp.zeros_like(acc_ref)
    y_here, z_here = place_ref[2], place_ref[3]
    for blocks, ref in zip(spec, pieces):
        where = [
            columns_at(lax.rem(y_here + dy, 4) * 8 + lax.rem(z_here + dz, 8)) for dz, dy in blocks
        ]
        field = jnp.concatenate([load(span) for span in where], axis=1)
        basis = jnp.concatenate([ref[k] for k in range(len(blocks))], axis=0)
        acc_ref[...] += jnp.dot(field, basis, preferred_element_type=jnp.float32)


NEAR = tuple(tuple((dz, dy) for dy in (0, 3, 1, 2)) for dz in (0, 7, 1, 6, 2, 5, 3))
FAR = (((4, 0), (4, 3)), ((4, 1), (4, 2)))


def near_kernel(place_ref, *refs):
    blocks, pieces, acc_ref = refs[:8], refs[8:-1], refs[-1]

    def load(span):
        return jnp.concatenate([ref[:, span] for ref in blocks], axis=0)

    product_of(place_ref, load, NEAR, pieces, acc_ref)


def near_product(place, fields, pieces):
    rows = sum(field.shape[0] for field in fields)
    width = pieces[0].shape[-1]
    return pl.pallas_call(
        near_kernel,
        out_shape=jax.ShapeDtypeStruct((rows, width), jnp.float32),
        in_specs=[SMEM] + [VMEM] * (8 + len(pieces)),
        out_specs=VMEM,
        compiler_params=pltpu.CompilerParams(vmem_limit_bytes=GRANT),
        cost_estimate=pl.CostEstimate(
            flops=2 * rows * 3072 * width, bytes_accessed=8 << 20, transcendentals=0
        ),
        name="near_product",
    )(place, *fields, *pieces)


def first_kernel(mix_ref, place_ref, *refs):
    blocks, pieces, (near_ref, out_ref, acc_ref, tmp_ref) = refs[:8], refs[8:-4], refs[-4:]
    rows = blocks[0].shape[0]
    lo = place_ref[0]

    def load(span):
        return jnp.concatenate([ref[:, span] for ref in blocks], axis=0)

    product_of(place_ref, load, FAR, pieces, acc_ref)
    acc_ref[...] += near_ref[...]
    for a in range(4):
        for group in range(2):
            mixed = sum(
                mix_ref[group * 4 + t, a]
                * acc_ref[(group * 4 + t) * rows : (group * 4 + t + 1) * rows, :]
                for t in range(4)
            )
            at = lo if group == 0 else 1 - lo
            tmp_ref[pl.ds(pl.multiple_of(at * rows, rows), rows), :] = mixed
        out_ref[:, a * 2 * rows : (a + 1) * 2 * rows] = tmp_ref[...].T.astype(jnp.bfloat16)


def first_product(mix, place, fields, pieces, near):
    rows = fields[0].shape[0]
    width = near.shape[-1]
    return pl.pallas_call(
        first_kernel,
        out_shape=jax.ShapeDtypeStruct((width, 8 * rows), jnp.bfloat16),
        in_specs=[SMEM, SMEM] + [VMEM] * (9 + len(pieces)),
        out_specs=VMEM,
        scratch_shapes=[
            pltpu.VMEM((8 * rows, width), jnp.float32),
            pltpu.VMEM((2 * rows, width), jnp.float32),
        ],
        compiler_params=pltpu.CompilerParams(vmem_limit_bytes=GRANT),
        cost_estimate=pl.CostEstimate(
            flops=2 * 8 * rows * 1024 * width, bytes_accessed=4 << 20, transcendentals=0
        ),
        name="first_product",
    )(mix, place, *fields, *pieces, near)


def load_bands(fields, which, span):
    return jnp.concatenate(
        [ref[part, which, :, span] for ref in fields for part in range(ref.shape[0])], axis=0
    )


def natural_place(slice_ref, half_of, block):
    return pl.multiple_of((slice_ref[block] * 2 + half_of) * 8, 8)


def moved_columns(half):
    source = lax.broadcasted_iota(jnp.int32, (128, 256), 0)
    target = lax.broadcasted_iota(jnp.int32, (128, 256), 1)
    return (target == (source // 8) * 16 + half * 8 + lax.rem(source, 8)).astype(jnp.float32)


def sent_kernel(place_ref, *refs):
    count = len(refs) - len(NEAR + FAR) - 2
    fields, pieces, (sent_ref, acc_ref) = refs[:count], refs[count:-2], refs[-2:]
    which = 1 - place_ref[0]
    product_of(
        place_ref, lambda span: load_bands(fields, which, span), NEAR + FAR, pieces, acc_ref
    )
    sent_ref[...] = acc_ref[...].astype(jnp.bfloat16)


def sent_rows(place, fields, pieces):
    count = sum(field.shape[0] * field.shape[2] for field in fields)
    total, width = fields[0].shape[-1], pieces[0].shape[-1]
    return pl.pallas_call(
        sent_kernel,
        out_shape=jax.ShapeDtypeStruct((count, width), jnp.bfloat16),
        in_specs=[SMEM] + [VMEM] * (len(fields) + len(pieces)),
        out_specs=VMEM,
        scratch_shapes=[pltpu.VMEM((count, width), jnp.float32)],
        compiler_params=pltpu.CompilerParams(vmem_limit_bytes=GRANT),
        cost_estimate=pl.CostEstimate(
            flops=2 * count * total * width, bytes_accessed=6 << 20, transcendentals=0
        ),
        name="sent_rows",
    )(place, *fields, *pieces)


def kept_kernel(place_ref, slice_ref, *refs):
    count = len(refs) - len(NEAR + FAR) - 6
    fields, pieces = refs[:count], refs[count:-6]
    sx_ref, sy_ref, white_ref, kept_ref, acc_ref, rows_ref = refs[-6:]
    lo = place_ref[0]
    product_of(place_ref, lambda span: load_bands(fields, lo, span), NEAR + FAR, pieces, acc_ref)
    for b in range(8):
        to = natural_place(slice_ref, lo if b < 4 else 1 - lo, b)
        for a in range(4):
            first = (b * 4 + a) * 8
            rows_ref[a, pl.ds(to, 8), :] = acc_ref[first : first + 8, :]
    chosen = moved_columns(lo)
    for block in range(rows_ref.shape[-1] // 128):
        span = slice(block * 256, block * 256 + 256)
        scale = sy_ref[:, :1] * sx_ref[:, span]
        for a in range(rows_ref.shape[0]):
            moved = jnp.dot(
                rows_ref[a, :, block * 128 : block * 128 + 128],
                chosen,
                precision=lax.Precision.HIGHEST,
            )
            kept_ref[a, :, span] = scale * moved - white_ref[:, a, span]


def kept_rows(place, slices, fields, pieces, sx, sy, white):
    count = sum(field.shape[0] * field.shape[2] for field in fields)
    total, width = fields[0].shape[-1], pieces[0].shape[-1]
    rows, times, columns = white.shape
    return pl.pallas_call(
        kept_kernel,
        out_shape=jax.ShapeDtypeStruct((times, rows, columns), jnp.float32),
        in_specs=[SMEM, SMEM] + [VMEM] * (len(fields) + len(pieces) + 3),
        out_specs=VMEM,
        scratch_shapes=[
            pltpu.VMEM((count, width), jnp.float32),
            pltpu.VMEM((times, rows, width), jnp.float32),
        ],
        compiler_params=pltpu.CompilerParams(vmem_limit_bytes=GRANT),
        cost_estimate=pl.CostEstimate(
            flops=2 * count * total * width, bytes_accessed=6 << 20, transcendentals=0
        ),
        name="kept_rows",
    )(place, slices, *fields, *pieces, sx, sy, white)


def gradient_kernel(place_ref, slice_ref, kept_ref, early_ref, late_ref, sx_ref, sy_ref, out_ref):
    lo = place_ref[0]
    chosen = moved_columns(1 - lo).astype(jnp.bfloat16)
    for block in range(early_ref.shape[-1] // 128):
        here = slice(block * 128, block * 128 + 128)
        span = slice(block * 256, block * 256 + 256)
        for ref, sources in ((early_ref, (0, 1, 4, 5, 6, 7)), (late_ref, (2, 3))):
            moved = jnp.dot(ref[:, here], chosen, preferred_element_type=jnp.float32)
            for k, b in enumerate(sources):
                to = natural_place(slice_ref, 1 - lo if b < 4 else lo, b)
                scale = sy_ref[pl.ds(to, 8), :1] * sx_ref[:, span]
                for a in range(4):
                    first = (k * 4 + a) * 8
                    out_ref[pl.ds(to, 8), a, span] = (
                        kept_ref[a, pl.ds(to, 8), span] + scale * moved[first : first + 8]
                    )


def whitened_gradient(place, slices, kept, early, late, sx, sy):
    times, rows, width = kept.shape
    return pl.pallas_call(
        gradient_kernel,
        out_shape=jax.ShapeDtypeStruct((rows, times, width), jnp.float32),
        in_specs=[SMEM, SMEM] + [VMEM] * 5,
        out_specs=VMEM,
        compiler_params=pltpu.CompilerParams(vmem_limit_bytes=GRANT),
        name="whitened_gradient",
    )(place, slices, kept, early, late, sx, sy)


def with_core(block):
    return block, shifted(block, "core", 1)


def local(event_counts, latent_mean, latent_var, eigen_basis, spectrum, correlation, whitened):
    hi, core = lax.axis_index("hi"), lax.axis_index("core")
    y, z, lo = (lax.axis_index(axis) for axis in ROW)
    time = hi * 2 + core
    ny, nz = lax.axis_size("y"), lax.axis_size("z")
    place = jnp.stack([lo, time, y, z]).astype(jnp.int32)

    kept, sent = split_columns(place, eigen_basis)
    other = shifted(sent, "lo", 1)
    mine = jnp.where(lo == 0, jnp.concatenate([kept, other]), jnp.concatenate([other, kept]))
    pseudo = moments(event_counts, latent_mean, latent_var).astype(jnp.bfloat16)[0]
    mine, pseudo = lax.optimization_barrier((mine, pseudo))
    far, before, after = [shifted(pseudo, RING, step) for step in (2, 1, 3)]
    block = jnp.stack([mine] + [shifted(mine, "y", step) for step in (1, 3, 2)])
    own = with_core(pseudo)

    flips = jnp.array([0, 1, 2, 3], jnp.int32)
    before_flip, after_flip = 2 * (1 - lo), 2 * lo
    crossed = jnp.stack([before_flip, before_flip + 1, after_flip, after_flip + 1])
    slices = lax.bitwise_xor(time, jnp.concatenate([flips, crossed])).astype(jnp.int32)
    swapped = jnp.concatenate([slices[:4], slices[6:], slices[4:6]])
    factor = time_factor(correlation[0], 4)
    mix = jnp.take(factor, slices, axis=0)
    root = jnp.sqrt(spectrum)
    sx = lax.dynamic_slice_in_dim(root, time * 1024, 1024, 0)[None]
    row = (y * nz + z) * 2 + lo
    sy = lax.dynamic_slice_in_dim(root.reshape(4, lax.axis_size(ROW), -1), row, 1, 1).reshape(-1, 1)
    sy = jnp.broadcast_to(sy, (sy.shape[0], 128))

    right, left = shifted(block, "z", 1), shifted(block, "z", nz - 1)
    pieces = [block, right, left]
    right, left, before, after = lax.optimization_barrier((right, left, before, after))
    before, after = with_core(before), with_core(after)
    right, left = shifted(right, "z", 1), shifted(left, "z", nz - 1)
    pieces += [right, left]
    right, left, far, own, mix, sx, sy = lax.optimization_barrier(
        (right, left, far, own, mix, sx, sy)
    )
    far = with_core(far)
    right, left = shifted(right, "z", 1), shifted(left, "z", nz - 1)
    pieces += [right, left]
    right, left, far, before, after = lax.optimization_barrier((right, left, far, before, after))
    last = [shifted(right[:2], "z", 1), shifted(left[2:], "z", nz - 1)]

    fields = (*own, *far, *before, *after)
    near = near_product(place, fields, pieces)
    partial_y = first_product(mix, place, fields, last, near)
    pieces += last

    modes, width = partial_y.shape
    sent = partial_y.reshape(ny * nz, modes // (ny * nz), width)
    got = lax.all_to_all(sent, ("y", "z"), 0, 0, tiled=True)
    group = modes // (2 * ny * nz)
    got = got.reshape(ny * nz, 2, group, 2, 2, width // 4)
    got = got.transpose(3, 1, 4, 2, 0, 5).reshape(2, 2, 2 * group, -1)
    own, before, after = with_core(got), shifted(got, RING, 1), shifted(got, RING, 3)
    before, after, far = lax.optimization_barrier((before, after, (before[:1], after[1:])))
    far = [shifted(far[0], RING, 1), shifted(far[1], RING, 3)]
    own, before, after = lax.optimization_barrier((own, before, after))
    before, after = with_core(before), with_core(after)
    early = sent_rows(place, (*own, *before, *after), pieces)
    far, early = lax.optimization_barrier((far, early))
    got_early = shifted(early, "lo", 1)
    far = (*far, *(shifted(half, "core", 1) for half in far))
    got_late = shifted(sent_rows(place, far, pieces), "lo", 1)
    white = whitened.reshape(-1, *whitened.shape[3:])
    kept = kept_rows(place, slices, (*own, *far, *before, *after), pieces, sx, sy, white)
    gradient = whitened_gradient(place, swapped, kept, got_early, got_late, sx, sy)
    return gradient.reshape(whitened.shape)


def solution(mesh):
    finer = Mesh(mesh.devices.reshape(2, 2, 4, 8, 2), ("hi", "core", "y", "z", "lo"))
    placed = (
        P(TM, ROW, None),
        P(TM, ROW, None),
        P(TM, ROW, None),
        P(ROW, TM),
        P(),
        P(),
        P(None, ROW, None, None, TM),
    )
    return jax.shard_map(
        local,
        mesh=finer,
        in_specs=placed,
        out_specs=P(None, ROW, None, None, TM),
        check_vma=False,
    )
```

```python
import math

import jax
import jax.numpy as jnp
from jax import lax
from jax.experimental import pallas as pl
from jax.experimental.pallas import tpu as pltpu
from jax.sharding import Mesh
from jax.sharding import PartitionSpec as P

TM = ("hi", "core")
ROW = ("y", "z", "lo")
RING = ("hi", "lo")

HERMITE_NODES = (
    -2.0201828704560856,
    -0.9585724646138185,
    0.0,
    0.9585724646138185,
    2.0201828704560856,
)
HERMITE_WEIGHTS = (
    0.019953242059045913,
    0.3936193231522412,
    0.9453087204829419,
    0.3936193231522412,
    0.019953242059045913,
)
GRANT = 20 << 20
VMEM = pl.BlockSpec(memory_space=pltpu.VMEM)
SMEM = pl.BlockSpec(memory_space=pltpu.SMEM)


def moments(event_counts, latent_mean, latent_var):
    spread = jnp.sqrt(2.0 * latent_var)
    normal = 1.0 / math.sqrt(math.pi)
    points = [latent_mean + spread * abscissa for abscissa in HERMITE_NODES]
    rate_points = [jnp.exp(value) for value in points]
    mean_rate = sum(
        (weight * normal * value for weight, value in zip(HERMITE_WEIGHTS, rate_points))
    )
    covariance = sum(
        (
            weight * normal * (node_value - latent_mean) * (value - mean_rate)
            for weight, node_value, value in zip(HERMITE_WEIGHTS, points, rate_points)
        )
    )
    rate_var = sum(
        (
            weight * normal * (value - mean_rate) * (value - mean_rate)
            for weight, value in zip(HERMITE_WEIGHTS, rate_points)
        )
    )
    slope_gain = covariance / latent_var
    noise_var = rate_var - slope_gain * covariance + mean_rate
    return slope_gain * (event_counts.astype(latent_mean.dtype) - mean_rate) / noise_var


def time_factor(correlation, total):
    later = jnp.arange(total)[:, None]
    earlier = jnp.arange(total)[None, :]
    distance = jnp.maximum(later - earlier, 0).astype(correlation.dtype)
    lower = jnp.where(later >= earlier, jnp.power(correlation, distance), jnp.zeros_like(distance))
    column_scale = jnp.where(
        earlier == 0,
        jnp.ones_like(distance),
        jnp.sqrt(1.0 - correlation * correlation) * jnp.ones_like(distance),
    )
    return lower * column_scale


def shifted(array, axis, step):
    size = lax.axis_size(axis)
    return lax.ppermute(array, axis, [(k, (k + step) % size) for k in range(size)])


def split_kernel(first_ref, basis_ref, kept_ref, sent_ref):
    source = lax.broadcasted_iota(jnp.int32, (256, 128), 0)
    target = lax.broadcasted_iota(jnp.int32, (256, 128), 1)
    for half, ref in ((first_ref[0], kept_ref), (1 - first_ref[0], sent_ref)):
        match = source == (target // 8) * 16 + half * 8 + lax.rem(target, 8)
        chosen = match.astype(jnp.float32).astype(jnp.bfloat16)
        for block in range(basis_ref.shape[1] // 256):
            moved = jnp.dot(
                basis_ref[:, block * 256 : block * 256 + 256],
                chosen,
                preferred_element_type=jnp.float32,
            )
            ref[:, block * 128 : block * 128 + 128] = moved.astype(jnp.bfloat16)


def split_columns(place, basis):
    rows, columns = basis.shape
    half = jax.ShapeDtypeStruct((rows, columns // 2), basis.dtype)
    return pl.pallas_call(
        split_kernel,
        out_shape=(half, half),
        in_specs=[SMEM, VMEM],
        out_specs=(VMEM, VMEM),
        compiler_params=pltpu.CompilerParams(vmem_limit_bytes=GRANT),
        name="split_columns",
    )(place, basis)


def columns_at(index):
    return pl.ds(pl.multiple_of(index * 128, 128), 128)


def product_of(place_ref, load, spec, pieces, acc_ref):
    acc_ref[...] = jnp.zeros_like(acc_ref)
    y_here, z_here = place_ref[2], place_ref[3]
    for blocks, ref in zip(spec, pieces):
        where = [
            columns_at(lax.rem(y_here + dy, 4) * 8 + lax.rem(z_here + dz, 8)) for dz, dy in blocks
        ]
        field = jnp.concatenate([load(span) for span in where], axis=1)
        basis = jnp.concatenate([ref[k] for k in range(len(blocks))], axis=0)
        acc_ref[...] += jnp.dot(field, basis, preferred_element_type=jnp.float32)


NEAR = tuple(tuple((dz, dy) for dy in (0, 3, 1, 2)) for dz in (0, 7, 1, 6, 2, 5, 3))
FAR = (((4, 0), (4, 3)), ((4, 1), (4, 2)))


def near_kernel(place_ref, *refs):
    blocks, pieces, acc_ref = refs[:8], refs[8:-1], refs[-1]

    def load(span):
        return jnp.concatenate([ref[:, span] for ref in blocks], axis=0)

    product_of(place_ref, load, NEAR, pieces, acc_ref)


def near_product(place, fields, pieces):
    rows = sum(field.shape[0] for field in fields)
    width = pieces[0].shape[-1]
    return pl.pallas_call(
        near_kernel,
        out_shape=jax.ShapeDtypeStruct((rows, width), jnp.float32),
        in_specs=[SMEM] + [VMEM] * (8 + len(pieces)),
        out_specs=VMEM,
        compiler_params=pltpu.CompilerParams(vmem_limit_bytes=GRANT),
        cost_estimate=pl.CostEstimate(
            flops=2 * rows * 3072 * width, bytes_accessed=8 << 20, transcendentals=0
        ),
        name="near_product",
    )(place, *fields, *pieces)


def first_kernel(mix_ref, place_ref, *refs):
    blocks, pieces, (near_ref, out_ref, acc_ref, tmp_ref) = refs[:8], refs[8:-4], refs[-4:]
    rows = blocks[0].shape[0]
    lo = place_ref[0]

    def load(span):
        return jnp.concatenate([ref[:, span] for ref in blocks], axis=0)

    product_of(place_ref, load, FAR, pieces, acc_ref)
    acc_ref[...] += near_ref[...]
    for a in range(4):
        for group in range(2):
            mixed = sum(
                mix_ref[group * 4 + t, a]
                * acc_ref[(group * 4 + t) * rows : (group * 4 + t + 1) * rows, :]
                for t in range(4)
            )
            at = lo if group == 0 else 1 - lo
            tmp_ref[pl.ds(pl.multiple_of(at * rows, rows), rows), :] = mixed
        out_ref[:, a * 2 * rows : (a + 1) * 2 * rows] = tmp_ref[...].T.astype(jnp.bfloat16)


def first_product(mix, place, fields, pieces, near):
    rows = fields[0].shape[0]
    width = near.shape[-1]
    return pl.pallas_call(
        first_kernel,
        out_shape=jax.ShapeDtypeStruct((width, 8 * rows), jnp.bfloat16),
        in_specs=[SMEM, SMEM] + [VMEM] * (9 + len(pieces)),
        out_specs=VMEM,
        scratch_shapes=[
            pltpu.VMEM((8 * rows, width), jnp.float32),
            pltpu.VMEM((2 * rows, width), jnp.float32),
        ],
        compiler_params=pltpu.CompilerParams(vmem_limit_bytes=GRANT),
        cost_estimate=pl.CostEstimate(
            flops=2 * 8 * rows * 1024 * width, bytes_accessed=4 << 20, transcendentals=0
        ),
        name="first_product",
    )(mix, place, *fields, *pieces, near)


def load_bands(fields, which, span):
    return jnp.concatenate(
        [ref[part, which, :, span] for ref in fields for part in range(ref.shape[0])], axis=0
    )


def natural_place(slice_ref, half_of, block):
    return pl.multiple_of((slice_ref[block] * 2 + half_of) * 8, 8)


def moved_columns(half):
    source = lax.broadcasted_iota(jnp.int32, (128, 256), 0)
    target = lax.broadcasted_iota(jnp.int32, (128, 256), 1)
    return (target == (source // 8) * 16 + half * 8 + lax.rem(source, 8)).astype(jnp.float32)


def sent_kernel(place_ref, *refs):
    count = len(refs) - len(NEAR + FAR) - 2
    fields, pieces, (sent_ref, acc_ref) = refs[:count], refs[count:-2], refs[-2:]
    which = 1 - place_ref[0]
    product_of(
        place_ref, lambda span: load_bands(fields, which, span), NEAR + FAR, pieces, acc_ref
    )
    sent_ref[...] = acc_ref[...].astype(jnp.bfloat16)


def sent_rows(place, fields, pieces):
    count = sum(field.shape[0] * field.shape[2] for field in fields)
    total, width = fields[0].shape[-1], pieces[0].shape[-1]
    return pl.pallas_call(
        sent_kernel,
        out_shape=jax.ShapeDtypeStruct((count, width), jnp.bfloat16),
        in_specs=[SMEM] + [VMEM] * (len(fields) + len(pieces)),
        out_specs=VMEM,
        scratch_shapes=[pltpu.VMEM((count, width), jnp.float32)],
        compiler_params=pltpu.CompilerParams(vmem_limit_bytes=GRANT),
        cost_estimate=pl.CostEstimate(
            flops=2 * count * total * width, bytes_accessed=6 << 20, transcendentals=0
        ),
        name="sent_rows",
    )(place, *fields, *pieces)


def kept_kernel(place_ref, slice_ref, *refs):
    count = len(refs) - len(NEAR + FAR) - 6
    fields, pieces = refs[:count], refs[count:-6]
    sx_ref, sy_ref, white_ref, kept_ref, acc_ref, rows_ref = refs[-6:]
    lo = place_ref[0]
    product_of(place_ref, lambda span: load_bands(fields, lo, span), NEAR + FAR, pieces, acc_ref)
    for b in range(8):
        to = natural_place(slice_ref, lo if b < 4 else 1 - lo, b)
        for a in range(4):
            first = (b * 4 + a) * 8
            rows_ref[a, pl.ds(to, 8), :] = acc_ref[first : first + 8, :]
    chosen = moved_columns(lo)
    for block in range(rows_ref.shape[-1] // 128):
        span = slice(block * 256, block * 256 + 256)
        scale = sy_ref[:, :1] * sx_ref[:, span]
        for a in range(rows_ref.shape[0]):
            moved = jnp.dot(
                rows_ref[a, :, block * 128 : block * 128 + 128],
                chosen,
                precision=lax.Precision.HIGHEST,
            )
            kept_ref[a, :, span] = scale * moved - white_ref[:, a, span]


def kept_rows(place, slices, fields, pieces, sx, sy, white):
    count = sum(field.shape[0] * field.shape[2] for field in fields)
    total, width = fields[0].shape[-1], pieces[0].shape[-1]
    rows, times, columns = white.shape
    return pl.pallas_call(
        kept_kernel,
        out_shape=jax.ShapeDtypeStruct((times, rows, columns), jnp.float32),
        in_specs=[SMEM, SMEM] + [VMEM] * (len(fields) + len(pieces) + 3),
        out_specs=VMEM,
        scratch_shapes=[
            pltpu.VMEM((count, width), jnp.float32),
            pltpu.VMEM((times, rows, width), jnp.float32),
        ],
        compiler_params=pltpu.CompilerParams(vmem_limit_bytes=GRANT),
        cost_estimate=pl.CostEstimate(
            flops=2 * count * total * width, bytes_accessed=6 << 20, transcendentals=0
        ),
        name="kept_rows",
    )(place, slices, *fields, *pieces, sx, sy, white)


def gradient_kernel(place_ref, slice_ref, kept_ref, early_ref, late_ref, sx_ref, sy_ref, out_ref):
    lo = place_ref[0]
    chosen = moved_columns(1 - lo).astype(jnp.bfloat16)
    for block in range(early_ref.shape[-1] // 128):
        here = slice(block * 128, block * 128 + 128)
        span = slice(block * 256, block * 256 + 256)
        for ref, sources in ((early_ref, (0, 1, 4, 5, 6, 7)), (late_ref, (2, 3))):
            moved = jnp.dot(ref[:, here], chosen, preferred_element_type=jnp.float32)
            for k, b in enumerate(sources):
                to = natural_place(slice_ref, 1 - lo if b < 4 else lo, b)
                scale = sy_ref[pl.ds(to, 8), :1] * sx_ref[:, span]
                for a in range(4):
                    first = (k * 4 + a) * 8
                    out_ref[pl.ds(to, 8), a, span] = (
                        kept_ref[a, pl.ds(to, 8), span] + scale * moved[first : first + 8]
                    )


def whitened_gradient(place, slices, kept, early, late, sx, sy):
    times, rows, width = kept.shape
    return pl.pallas_call(
        gradient_kernel,
        out_shape=jax.ShapeDtypeStruct((rows, times, width), jnp.float32),
        in_specs=[SMEM, SMEM] + [VMEM] * 5,
        out_specs=VMEM,
        compiler_params=pltpu.CompilerParams(vmem_limit_bytes=GRANT),
        name="whitened_gradient",
    )(place, slices, kept, early, late, sx, sy)


def with_core(block):
    return block, shifted(block, "core", 1)


def local(event_counts, latent_mean, latent_var, eigen_basis, spectrum, correlation, whitened):
    hi, core = lax.axis_index("hi"), lax.axis_index("core")
    y, z, lo = (lax.axis_index(axis) for axis in ROW)
    time = hi * 2 + core
    ny, nz = lax.axis_size("y"), lax.axis_size("z")
    place = jnp.stack([lo, time, y, z]).astype(jnp.int32)

    kept, sent = split_columns(place, eigen_basis)
    other = shifted(sent, "lo", 1)
    mine = jnp.where(lo == 0, jnp.concatenate([kept, other]), jnp.concatenate([other, kept]))
    pseudo = moments(event_counts, latent_mean, latent_var).astype(jnp.bfloat16)[0]
    mine, pseudo = lax.optimization_barrier((mine, pseudo))
    before, after = shifted(pseudo, RING, 1), shifted(pseudo, RING, 3)
    block = jnp.stack([mine] + [shifted(mine, "y", step) for step in (1, 3, 2)])
    block, pseudo = lax.optimization_barrier((block, pseudo))
    own = lax.optimization_barrier(with_core(pseudo))
    far = shifted(own[0], RING, 2)

    flips = jnp.array([0, 1, 2, 3], jnp.int32)
    before_flip, after_flip = 2 * (1 - lo), 2 * lo
    crossed = jnp.stack([before_flip, before_flip + 1, after_flip, after_flip + 1])
    slices = lax.bitwise_xor(time, jnp.concatenate([flips, crossed])).astype(jnp.int32)
    swapped = jnp.concatenate([slices[:4], slices[6:], slices[4:6]])
    factor = time_factor(correlation[0], 4)
    mix = jnp.take(factor, slices, axis=0)
    root = jnp.sqrt(spectrum)
    sx = lax.dynamic_slice_in_dim(root, time * 1024, 1024, 0)[None]
    row = (y * nz + z) * 2 + lo
    sy = lax.dynamic_slice_in_dim(root.reshape(4, lax.axis_size(ROW), -1), row, 1, 1).reshape(-1, 1)
    sy = jnp.broadcast_to(sy, (sy.shape[0], 128))

    right, left = shifted(block, "z", 1), shifted(block, "z", nz - 1)
    pieces = [block, right, left]
    right, left, before, after = lax.optimization_barrier((right, left, before, after))
    before, after = with_core(before), with_core(after)
    right, left = shifted(right, "z", 1), shifted(left, "z", nz - 1)
    pieces += [right, left]
    right, left, far, own, mix, sx, sy = lax.optimization_barrier(
        (right, left, far, own, mix, sx, sy)
    )
    far = with_core(far)
    right, left = shifted(right, "z", 1), shifted(left, "z", nz - 1)
    pieces += [right, left]
    right, left, far, before, after = lax.optimization_barrier((right, left, far, before, after))
    last = [shifted(right[:2], "z", 1), shifted(left[2:], "z", nz - 1)]

    fields = (*own, *far, *before, *after)
    near = near_product(place, fields, pieces)
    partial_y = first_product(mix, place, fields, last, near)
    pieces += last

    modes, width = partial_y.shape
    sent = partial_y.reshape(ny * nz, modes // (ny * nz), width)
    got = lax.all_to_all(sent, ("y", "z"), 0, 0, tiled=True)
    group = modes // (2 * ny * nz)
    got = got.reshape(ny * nz, 2, group, 2, 2, width // 4)
    got = got.transpose(3, 1, 4, 2, 0, 5).reshape(2, 2, 2 * group, -1)
    own, before, after = with_core(got), shifted(got, RING, 1), shifted(got, RING, 3)
    before, after, far = lax.optimization_barrier((before, after, (before[:1], after[1:])))
    far = [shifted(far[0], RING, 1), shifted(far[1], RING, 3)]
    own, before, after = lax.optimization_barrier((own, before, after))
    before, after = with_core(before), with_core(after)
    early = sent_rows(place, (*own, *before, *after), pieces)
    far, early = lax.optimization_barrier((far, early))
    got_early = shifted(early, "lo", 1)
    far = (*far, *(shifted(half, "core", 1) for half in far))
    got_late = shifted(sent_rows(place, far, pieces), "lo", 1)
    white = whitened.reshape(-1, *whitened.shape[3:])
    kept = kept_rows(place, slices, (*own, *far, *before, *after), pieces, sx, sy, white)
    gradient = whitened_gradient(place, swapped, kept, got_early, got_late, sx, sy)
    return gradient.reshape(whitened.shape)


def solution(mesh):
    finer = Mesh(mesh.devices.reshape(2, 2, 4, 8, 2), ("hi", "core", "y", "z", "lo"))
    placed = (
        P(TM, ROW, None),
        P(TM, ROW, None),
        P(TM, ROW, None),
        P(ROW, TM),
        P(),
        P(),
        P(None, ROW, None, None, TM),
    )
    return jax.shard_map(
        local,
        mesh=finer,
        in_specs=placed,
        out_specs=P(None, ROW, None, None, TM),
        check_vma=False,
    )
```

```python
import math

import jax
import jax.numpy as jnp
from jax import lax
from jax.experimental import pallas as pl
from jax.experimental.pallas import tpu as pltpu
from jax.sharding import Mesh
from jax.sharding import PartitionSpec as P

TM = ("hi", "core")
ROW = ("y", "z", "lo")
RING = ("hi", "lo")

HERMITE_NODES = (
    -2.0201828704560856,
    -0.9585724646138185,
    0.0,
    0.9585724646138185,
    2.0201828704560856,
)
HERMITE_WEIGHTS = (
    0.019953242059045913,
    0.3936193231522412,
    0.9453087204829419,
    0.3936193231522412,
    0.019953242059045913,
)
GRANT = 20 << 20
VMEM = pl.BlockSpec(memory_space=pltpu.VMEM)
SMEM = pl.BlockSpec(memory_space=pltpu.SMEM)


def moments(event_counts, latent_mean, latent_var):
    spread = jnp.sqrt(2.0 * latent_var)
    normal = 1.0 / math.sqrt(math.pi)
    points = [latent_mean + spread * abscissa for abscissa in HERMITE_NODES]
    rate_points = [jnp.exp(value) for value in points]
    mean_rate = sum(
        (weight * normal * value for weight, value in zip(HERMITE_WEIGHTS, rate_points))
    )
    covariance = sum(
        (
            weight * normal * (node_value - latent_mean) * (value - mean_rate)
            for weight, node_value, value in zip(HERMITE_WEIGHTS, points, rate_points)
        )
    )
    rate_var = sum(
        (
            weight * normal * (value - mean_rate) * (value - mean_rate)
            for weight, value in zip(HERMITE_WEIGHTS, rate_points)
        )
    )
    slope_gain = covariance / latent_var
    noise_var = rate_var - slope_gain * covariance + mean_rate
    return slope_gain * (event_counts.astype(latent_mean.dtype) - mean_rate) / noise_var


def time_factor(correlation, total):
    later = jnp.arange(total)[:, None]
    earlier = jnp.arange(total)[None, :]
    distance = jnp.maximum(later - earlier, 0).astype(correlation.dtype)
    lower = jnp.where(later >= earlier, jnp.power(correlation, distance), jnp.zeros_like(distance))
    column_scale = jnp.where(
        earlier == 0,
        jnp.ones_like(distance),
        jnp.sqrt(1.0 - correlation * correlation) * jnp.ones_like(distance),
    )
    return lower * column_scale


def shifted(array, axis, step):
    size = lax.axis_size(axis)
    return lax.ppermute(array, axis, [(k, (k + step) % size) for k in range(size)])


def split_kernel(first_ref, basis_ref, kept_ref, sent_ref):
    source = lax.broadcasted_iota(jnp.int32, (256, 128), 0)
    target = lax.broadcasted_iota(jnp.int32, (256, 128), 1)
    for half, ref in ((first_ref[0], kept_ref), (1 - first_ref[0], sent_ref)):
        match = source == (target // 8) * 16 + half * 8 + lax.rem(target, 8)
        chosen = match.astype(jnp.float32).astype(jnp.bfloat16)
        for block in range(basis_ref.shape[1] // 256):
            moved = jnp.dot(
                basis_ref[:, block * 256 : block * 256 + 256],
                chosen,
                preferred_element_type=jnp.float32,
            )
            ref[:, block * 128 : block * 128 + 128] = moved.astype(jnp.bfloat16)


def split_columns(place, basis):
    rows, columns = basis.shape
    half = jax.ShapeDtypeStruct((rows, columns // 2), basis.dtype)
    return pl.pallas_call(
        split_kernel,
        out_shape=(half, half),
        in_specs=[SMEM, VMEM],
        out_specs=(VMEM, VMEM),
        compiler_params=pltpu.CompilerParams(vmem_limit_bytes=GRANT),
        name="split_columns",
    )(place, basis)


def columns_at(index):
    return pl.ds(pl.multiple_of(index * 128, 128), 128)


def product_of(place_ref, load, spec, pieces, acc_ref):
    acc_ref[...] = jnp.zeros_like(acc_ref)
    y_here, z_here = place_ref[2], place_ref[3]
    for blocks, ref in zip(spec, pieces):
        where = [
            columns_at(lax.rem(y_here + dy, 4) * 8 + lax.rem(z_here + dz, 8)) for dz, dy in blocks
        ]
        field = jnp.concatenate([load(span) for span in where], axis=1)
        basis = jnp.concatenate([ref[k] for k in range(len(blocks))], axis=0)
        acc_ref[...] += jnp.dot(field, basis, preferred_element_type=jnp.float32)


NEAR = (
    *((((dz, 0), (dz, 1))) for dz in (0, 7, 1, 6, 2, 5, 3)),
    tuple((dz, 2) for dz in (0, 7, 1, 6, 2)),
    tuple((dz, 3) for dz in (0, 7, 1, 6, 2)),
)
FAR = (
    ((5, 2), (3, 2)),
    ((5, 3), (3, 3)),
    ((4, 0),),
    ((4, 1),),
    ((4, 2),),
    ((4, 3),),
)


def near_kernel(place_ref, *refs):
    blocks, pieces, acc_ref = refs[:8], refs[8:-1], refs[-1]

    def load(span):
        return jnp.concatenate([ref[:, span] for ref in blocks], axis=0)

    product_of(place_ref, load, NEAR, pieces, acc_ref)


def near_product(place, fields, pieces):
    rows = sum(field.shape[0] for field in fields)
    width = pieces[0].shape[-1]
    return pl.pallas_call(
        near_kernel,
        out_shape=jax.ShapeDtypeStruct((rows, width), jnp.float32),
        in_specs=[SMEM] + [VMEM] * (8 + len(pieces)),
        out_specs=VMEM,
        compiler_params=pltpu.CompilerParams(vmem_limit_bytes=GRANT),
        cost_estimate=pl.CostEstimate(
            flops=2 * rows * 3072 * width, bytes_accessed=8 << 20, transcendentals=0
        ),
        name="near_product",
    )(place, *fields, *pieces)


def first_kernel(mix_ref, place_ref, *refs):
    blocks, pieces, (near_ref, out_ref, acc_ref, tmp_ref) = refs[:8], refs[8:-4], refs[-4:]
    rows = blocks[0].shape[0]
    lo = place_ref[0]

    def load(span):
        return jnp.concatenate([ref[:, span] for ref in blocks], axis=0)

    product_of(place_ref, load, FAR, pieces, acc_ref)
    acc_ref[...] += near_ref[...]
    for a in range(4):
        for group in range(2):
            mixed = sum(
                mix_ref[group * 4 + t, a]
                * acc_ref[(group * 4 + t) * rows : (group * 4 + t + 1) * rows, :]
                for t in range(4)
            )
            at = lo if group == 0 else 1 - lo
            tmp_ref[pl.ds(pl.multiple_of(at * rows, rows), rows), :] = mixed
        out_ref[:, a * 2 * rows : (a + 1) * 2 * rows] = tmp_ref[...].T.astype(jnp.bfloat16)


def first_product(mix, place, fields, pieces, near):
    rows = fields[0].shape[0]
    width = near.shape[-1]
    return pl.pallas_call(
        first_kernel,
        out_shape=jax.ShapeDtypeStruct((width, 8 * rows), jnp.bfloat16),
        in_specs=[SMEM, SMEM] + [VMEM] * (9 + len(pieces)),
        out_specs=VMEM,
        scratch_shapes=[
            pltpu.VMEM((8 * rows, width), jnp.float32),
            pltpu.VMEM((2 * rows, width), jnp.float32),
        ],
        compiler_params=pltpu.CompilerParams(vmem_limit_bytes=GRANT),
        cost_estimate=pl.CostEstimate(
            flops=2 * 8 * rows * 1024 * width, bytes_accessed=4 << 20, transcendentals=0
        ),
        name="first_product",
    )(mix, place, *fields, *pieces, near)


def load_bands(fields, which, span):
    return jnp.concatenate(
        [ref[part, which, :, span] for ref in fields for part in range(ref.shape[0])], axis=0
    )


def natural_place(slice_ref, half_of, block):
    return pl.multiple_of((slice_ref[block] * 2 + half_of) * 8, 8)


def moved_columns(half):
    source = lax.broadcasted_iota(jnp.int32, (128, 256), 0)
    target = lax.broadcasted_iota(jnp.int32, (128, 256), 1)
    return (target == (source // 8) * 16 + half * 8 + lax.rem(source, 8)).astype(jnp.float32)


def sent_kernel(place_ref, *refs):
    count = len(refs) - len(NEAR + FAR) - 2
    fields, pieces, (sent_ref, acc_ref) = refs[:count], refs[count:-2], refs[-2:]
    which = 1 - place_ref[0]
    product_of(
        place_ref, lambda span: load_bands(fields, which, span), NEAR + FAR, pieces, acc_ref
    )
    sent_ref[...] = acc_ref[...].astype(jnp.bfloat16)


def sent_rows(place, fields, pieces):
    count = sum(field.shape[0] * field.shape[2] for field in fields)
    total, width = fields[0].shape[-1], pieces[0].shape[-1]
    return pl.pallas_call(
        sent_kernel,
        out_shape=jax.ShapeDtypeStruct((count, width), jnp.bfloat16),
        in_specs=[SMEM] + [VMEM] * (len(fields) + len(pieces)),
        out_specs=VMEM,
        scratch_shapes=[pltpu.VMEM((count, width), jnp.float32)],
        compiler_params=pltpu.CompilerParams(vmem_limit_bytes=GRANT),
        cost_estimate=pl.CostEstimate(
            flops=2 * count * total * width, bytes_accessed=6 << 20, transcendentals=0
        ),
        name="sent_rows",
    )(place, *fields, *pieces)


def kept_kernel(place_ref, slice_ref, *refs):
    count = len(refs) - len(NEAR + FAR) - 6
    fields, pieces = refs[:count], refs[count:-6]
    sx_ref, sy_ref, white_ref, kept_ref, acc_ref, rows_ref = refs[-6:]
    lo = place_ref[0]
    product_of(place_ref, lambda span: load_bands(fields, lo, span), NEAR + FAR, pieces, acc_ref)
    for b in range(8):
        to = natural_place(slice_ref, lo if b < 4 else 1 - lo, b)
        for a in range(4):
            first = (b * 4 + a) * 8
            rows_ref[a, pl.ds(to, 8), :] = acc_ref[first : first + 8, :]
    chosen = moved_columns(lo)
    for block in range(rows_ref.shape[-1] // 128):
        span = slice(block * 256, block * 256 + 256)
        scale = sy_ref[:, :1] * sx_ref[:, span]
        for a in range(rows_ref.shape[0]):
            moved = jnp.dot(
                rows_ref[a, :, block * 128 : block * 128 + 128],
                chosen,
                precision=lax.Precision.HIGHEST,
            )
            kept_ref[a, :, span] = scale * moved - white_ref[:, a, span]


def kept_rows(place, slices, fields, pieces, sx, sy, white):
    count = sum(field.shape[0] * field.shape[2] for field in fields)
    total, width = fields[0].shape[-1], pieces[0].shape[-1]
    rows, times, columns = white.shape
    return pl.pallas_call(
        kept_kernel,
        out_shape=jax.ShapeDtypeStruct((times, rows, columns), jnp.float32),
        in_specs=[SMEM, SMEM] + [VMEM] * (len(fields) + len(pieces) + 3),
        out_specs=VMEM,
        scratch_shapes=[
            pltpu.VMEM((count, width), jnp.float32),
            pltpu.VMEM((times, rows, width), jnp.float32),
        ],
        compiler_params=pltpu.CompilerParams(vmem_limit_bytes=GRANT),
        cost_estimate=pl.CostEstimate(
            flops=2 * count * total * width, bytes_accessed=6 << 20, transcendentals=0
        ),
        name="kept_rows",
    )(place, slices, *fields, *pieces, sx, sy, white)


def gradient_kernel(place_ref, slice_ref, kept_ref, early_ref, late_ref, sx_ref, sy_ref, out_ref):
    lo = place_ref[0]
    chosen = moved_columns(1 - lo).astype(jnp.bfloat16)
    for block in range(early_ref.shape[-1] // 128):
        here = slice(block * 128, block * 128 + 128)
        span = slice(block * 256, block * 256 + 256)
        for ref, sources in ((early_ref, (0, 1, 4, 5, 6, 7)), (late_ref, (2, 3))):
            moved = jnp.dot(ref[:, here], chosen, preferred_element_type=jnp.float32)
            for k, b in enumerate(sources):
                to = natural_place(slice_ref, 1 - lo if b < 4 else lo, b)
                scale = sy_ref[pl.ds(to, 8), :1] * sx_ref[:, span]
                for a in range(4):
                    first = (k * 4 + a) * 8
                    out_ref[pl.ds(to, 8), a, span] = (
                        kept_ref[a, pl.ds(to, 8), span] + scale * moved[first : first + 8]
                    )


def whitened_gradient(place, slices, kept, early, late, sx, sy):
    times, rows, width = kept.shape
    return pl.pallas_call(
        gradient_kernel,
        out_shape=jax.ShapeDtypeStruct((rows, times, width), jnp.float32),
        in_specs=[SMEM, SMEM] + [VMEM] * 5,
        out_specs=VMEM,
        compiler_params=pltpu.CompilerParams(vmem_limit_bytes=GRANT),
        name="whitened_gradient",
    )(place, slices, kept, early, late, sx, sy)


def with_core(block):
    return block, shifted(block, "core", 1)


def local(event_counts, latent_mean, latent_var, eigen_basis, spectrum, correlation, whitened):
    hi, core = lax.axis_index("hi"), lax.axis_index("core")
    y, z, lo = (lax.axis_index(axis) for axis in ROW)
    time = hi * 2 + core
    ny, nz = lax.axis_size("y"), lax.axis_size("z")
    place = jnp.stack([lo, time, y, z]).astype(jnp.int32)

    kept, sent = split_columns(place, eigen_basis)
    other = shifted(sent, "lo", 1)
    mine = jnp.where(lo == 0, jnp.concatenate([kept, other]), jnp.concatenate([other, kept]))
    pseudo = moments(event_counts, latent_mean, latent_var).astype(jnp.bfloat16)[0]
    mine, pseudo = lax.optimization_barrier((mine, pseudo))
    block = jnp.stack([mine, shifted(mine, "y", 3)])
    block, pseudo = lax.optimization_barrier((block, pseudo))
    own = with_core(pseudo)

    flips = jnp.array([0, 1, 2, 3], jnp.int32)
    before_flip, after_flip = 2 * (1 - lo), 2 * lo
    crossed = jnp.stack([before_flip, before_flip + 1, after_flip, after_flip + 1])
    slices = lax.bitwise_xor(time, jnp.concatenate([flips, crossed])).astype(jnp.int32)
    swapped = jnp.concatenate([slices[:4], slices[6:], slices[4:6]])
    factor = time_factor(correlation[0], 4)
    mix = jnp.take(factor, slices, axis=0)
    root = jnp.sqrt(spectrum)
    sx = lax.dynamic_slice_in_dim(root, time * 1024, 1024, 0)[None]
    row = (y * nz + z) * 2 + lo
    sy = lax.dynamic_slice_in_dim(root.reshape(4, lax.axis_size(ROW), -1), row, 1, 1).reshape(-1, 1)
    sy = jnp.broadcast_to(sy, (sy.shape[0], 128))

    def from_neighbours(blocks):
        second = jnp.concatenate([b[-1:] for b in blocks])
        first = jnp.concatenate([b[:1] for b in blocks])
        return [shifted(second, "y", 3), shifted(first, "y", 1)]

    def step(right, left):
        return shifted(right, "z", 1), shifted(left, "z", nz - 1)

    one = step(block, block)
    one, own = lax.optimization_barrier((one, own))
    two = step(*one)
    before, after = shifted(own[0], RING, 1), shifted(own[0], RING, 3)
    two, own, mix, sx, sy = lax.optimization_barrier((two, own, mix, sx, sy))
    three = step(*two)
    far = shifted(own[0], RING, 2)
    beside_two = from_neighbours([block, *one, *two])
    three, before, after = lax.optimization_barrier((three, before, after))
    before, after, far = with_core(before), with_core(after), with_core(far)
    ends = step(three[0][:1], three[1][1:])
    pieces = [block, *one, *two, *three, *beside_two]
    last = [*from_neighbours(three), *ends]
    last += [shifted(ends[1], "y", 3), shifted(ends[0], "y", 1)]

    fields = (*own, *far, *before, *after)
    near = near_product(place, fields, pieces)
    partial_y = first_product(mix, place, fields, last, near)
    pieces += last

    modes, width = partial_y.shape
    sent = partial_y.reshape(ny * nz, modes // (ny * nz), width)
    got = lax.all_to_all(sent, ("y", "z"), 0, 0, tiled=True)
    group = modes // (2 * ny * nz)
    got = got.reshape(ny * nz, 2, group, 2, 2, width // 4)
    got = got.transpose(3, 1, 4, 2, 0, 5).reshape(2, 2, 2 * group, -1)
    own, before, after = with_core(got), shifted(got, RING, 1), shifted(got, RING, 3)
    before, after, far = lax.optimization_barrier((before, after, (before[:1], after[1:])))
    far = [shifted(far[0], RING, 1), shifted(far[1], RING, 3)]
    own, before, after = lax.optimization_barrier((own, before, after))
    before, after = with_core(before), with_core(after)
    early = sent_rows(place, (*own, *before, *after), pieces)
    far, early = lax.optimization_barrier((far, early))
    got_early = shifted(early, "lo", 1)
    far = (*far, *(shifted(half, "core", 1) for half in far))
    got_late = shifted(sent_rows(place, far, pieces), "lo", 1)
    white = whitened.reshape(-1, *whitened.shape[3:])
    kept = kept_rows(place, slices, (*own, *far, *before, *after), pieces, sx, sy, white)
    gradient = whitened_gradient(place, swapped, kept, got_early, got_late, sx, sy)
    return gradient.reshape(whitened.shape)


def solution(mesh):
    finer = Mesh(mesh.devices.reshape(2, 2, 4, 8, 2), ("hi", "core", "y", "z", "lo"))
    placed = (
        P(TM, ROW, None),
        P(TM, ROW, None),
        P(TM, ROW, None),
        P(ROW, TM),
        P(),
        P(),
        P(None, ROW, None, None, TM),
    )
    return jax.shard_map(
        local,
        mesh=finer,
        in_specs=placed,
        out_specs=P(None, ROW, None, None, TM),
        check_vma=False,
    )
```

```python
import math

import jax
import jax.numpy as jnp
from jax import lax
from jax.experimental import pallas as pl
from jax.experimental.pallas import tpu as pltpu
from jax.sharding import Mesh
from jax.sharding import PartitionSpec as P

TM = ("hi", "core")
ROW = ("y", "z", "lo")
RING = ("hi", "lo")

HERMITE_NODES = (
    -2.0201828704560856,
    -0.9585724646138185,
    0.0,
    0.9585724646138185,
    2.0201828704560856,
)
HERMITE_WEIGHTS = (
    0.019953242059045913,
    0.3936193231522412,
    0.9453087204829419,
    0.3936193231522412,
    0.019953242059045913,
)
GRANT = 20 << 20
VMEM = pl.BlockSpec(memory_space=pltpu.VMEM)
SMEM = pl.BlockSpec(memory_space=pltpu.SMEM)


def moments(event_counts, latent_mean, latent_var):
    spread = jnp.sqrt(2.0 * latent_var)
    normal = 1.0 / math.sqrt(math.pi)
    points = [latent_mean + spread * abscissa for abscissa in HERMITE_NODES]
    rate_points = [jnp.exp(value) for value in points]
    mean_rate = sum(
        (weight * normal * value for weight, value in zip(HERMITE_WEIGHTS, rate_points))
    )
    covariance = sum(
        (
            weight * normal * (node_value - latent_mean) * (value - mean_rate)
            for weight, node_value, value in zip(HERMITE_WEIGHTS, points, rate_points)
        )
    )
    rate_var = sum(
        (
            weight * normal * (value - mean_rate) * (value - mean_rate)
            for weight, value in zip(HERMITE_WEIGHTS, rate_points)
        )
    )
    slope_gain = covariance / latent_var
    noise_var = rate_var - slope_gain * covariance + mean_rate
    return slope_gain * (event_counts.astype(latent_mean.dtype) - mean_rate) / noise_var


def time_factor(correlation, total):
    later = jnp.arange(total)[:, None]
    earlier = jnp.arange(total)[None, :]
    distance = jnp.maximum(later - earlier, 0).astype(correlation.dtype)
    lower = jnp.where(later >= earlier, jnp.power(correlation, distance), jnp.zeros_like(distance))
    column_scale = jnp.where(
        earlier == 0,
        jnp.ones_like(distance),
        jnp.sqrt(1.0 - correlation * correlation) * jnp.ones_like(distance),
    )
    return lower * column_scale


def shifted(array, axis, step):
    size = lax.axis_size(axis)
    return lax.ppermute(array, axis, [(k, (k + step) % size) for k in range(size)])


def split_kernel(first_ref, basis_ref, kept_ref, sent_ref):
    source = lax.broadcasted_iota(jnp.int32, (256, 128), 0)
    target = lax.broadcasted_iota(jnp.int32, (256, 128), 1)
    for half, ref in ((first_ref[0], kept_ref), (1 - first_ref[0], sent_ref)):
        match = source == (target // 8) * 16 + half * 8 + lax.rem(target, 8)
        chosen = match.astype(jnp.float32).astype(jnp.bfloat16)
        for block in range(basis_ref.shape[1] // 256):
            moved = jnp.dot(
                basis_ref[:, block * 256 : block * 256 + 256],
                chosen,
                preferred_element_type=jnp.float32,
            )
            ref[:, block * 128 : block * 128 + 128] = moved.astype(jnp.bfloat16)


def split_columns(place, basis):
    rows, columns = basis.shape
    half = jax.ShapeDtypeStruct((rows, columns // 2), basis.dtype)
    return pl.pallas_call(
        split_kernel,
        out_shape=(half, half),
        in_specs=[SMEM, VMEM],
        out_specs=(VMEM, VMEM),
        compiler_params=pltpu.CompilerParams(vmem_limit_bytes=GRANT),
        name="split_columns",
    )(place, basis)


def columns_at(index):
    return pl.ds(pl.multiple_of(index * 128, 128), 128)


def product_of(place_ref, load, spec, pieces, acc_ref):
    acc_ref[...] = jnp.zeros_like(acc_ref)
    y_here, z_here = place_ref[2], place_ref[3]
    for blocks, ref in zip(spec, pieces):
        where = [
            columns_at(lax.rem(y_here + dy, 4) * 8 + lax.rem(z_here + dz, 8)) for dz, dy in blocks
        ]
        field = jnp.concatenate([load(span) for span in where], axis=1)
        basis = jnp.concatenate([ref[k] for k in range(len(blocks))], axis=0)
        acc_ref[...] += jnp.dot(field, basis, preferred_element_type=jnp.float32)


NEAR = tuple(tuple((dz, dy) for dy in (0, 3, 1, 2)) for dz in (0, 7, 1, 6, 2, 5, 3))
FAR = (((4, 0), (4, 3)), ((4, 1), (4, 2)))


def near_kernel(place_ref, *refs):
    blocks, pieces, acc_ref = refs[:8], refs[8:-1], refs[-1]

    def load(span):
        return jnp.concatenate([ref[:, span] for ref in blocks], axis=0)

    product_of(place_ref, load, NEAR, pieces, acc_ref)


def near_product(place, fields, pieces):
    rows = sum(field.shape[0] for field in fields)
    width = pieces[0].shape[-1]
    return pl.pallas_call(
        near_kernel,
        out_shape=jax.ShapeDtypeStruct((rows, width), jnp.float32),
        in_specs=[SMEM] + [VMEM] * (8 + len(pieces)),
        out_specs=VMEM,
        compiler_params=pltpu.CompilerParams(vmem_limit_bytes=GRANT),
        cost_estimate=pl.CostEstimate(
            flops=2 * rows * 3072 * width, bytes_accessed=8 << 20, transcendentals=0
        ),
        name="near_product",
    )(place, *fields, *pieces)


def first_kernel(mix_ref, place_ref, *refs):
    blocks, pieces, (near_ref, out_ref, acc_ref, tmp_ref) = refs[:8], refs[8:-4], refs[-4:]
    rows = blocks[0].shape[0]
    lo = place_ref[0]

    def load(span):
        return jnp.concatenate([ref[:, span] for ref in blocks], axis=0)

    product_of(place_ref, load, FAR, pieces, acc_ref)
    acc_ref[...] += near_ref[...]
    for a in range(4):
        for group in range(2):
            mixed = sum(
                mix_ref[group * 4 + t, a]
                * acc_ref[(group * 4 + t) * rows : (group * 4 + t + 1) * rows, :]
                for t in range(4)
            )
            at = lo if group == 0 else 1 - lo
            tmp_ref[pl.ds(pl.multiple_of(at * rows, rows), rows), :] = mixed
        out_ref[:, a * 2 * rows : (a + 1) * 2 * rows] = tmp_ref[...].T.astype(jnp.bfloat16)


def first_product(mix, place, fields, pieces, near):
    rows = fields[0].shape[0]
    width = near.shape[-1]
    return pl.pallas_call(
        first_kernel,
        out_shape=jax.ShapeDtypeStruct((width, 8 * rows), jnp.bfloat16),
        in_specs=[SMEM, SMEM] + [VMEM] * (9 + len(pieces)),
        out_specs=VMEM,
        scratch_shapes=[
            pltpu.VMEM((8 * rows, width), jnp.float32),
            pltpu.VMEM((2 * rows, width), jnp.float32),
        ],
        compiler_params=pltpu.CompilerParams(vmem_limit_bytes=GRANT),
        cost_estimate=pl.CostEstimate(
            flops=2 * 8 * rows * 1024 * width, bytes_accessed=4 << 20, transcendentals=0
        ),
        name="first_product",
    )(mix, place, *fields, *pieces, near)


def load_bands(fields, which, span):
    return jnp.concatenate(
        [ref[part, which, :, span] for ref in fields for part in range(ref.shape[0])], axis=0
    )


def natural_place(slice_ref, half_of, block):
    return pl.multiple_of((slice_ref[block] * 2 + half_of) * 8, 8)


def moved_columns(half):
    source = lax.broadcasted_iota(jnp.int32, (128, 256), 0)
    target = lax.broadcasted_iota(jnp.int32, (128, 256), 1)
    return (target == (source // 8) * 16 + half * 8 + lax.rem(source, 8)).astype(jnp.float32)


def sent_kernel(place_ref, *refs):
    count = len(refs) - len(NEAR + FAR) - 2
    fields, pieces, (sent_ref, acc_ref) = refs[:count], refs[count:-2], refs[-2:]
    which = 1 - place_ref[0]
    product_of(
        place_ref, lambda span: load_bands(fields, which, span), NEAR + FAR, pieces, acc_ref
    )
    sent_ref[...] = acc_ref[...].astype(jnp.bfloat16)


def sent_rows(place, fields, pieces):
    count = sum(field.shape[0] * field.shape[2] for field in fields)
    total, width = fields[0].shape[-1], pieces[0].shape[-1]
    return pl.pallas_call(
        sent_kernel,
        out_shape=jax.ShapeDtypeStruct((count, width), jnp.bfloat16),
        in_specs=[SMEM] + [VMEM] * (len(fields) + len(pieces)),
        out_specs=VMEM,
        scratch_shapes=[pltpu.VMEM((count, width), jnp.float32)],
        compiler_params=pltpu.CompilerParams(vmem_limit_bytes=GRANT),
        cost_estimate=pl.CostEstimate(
            flops=2 * count * total * width, bytes_accessed=6 << 20, transcendentals=0
        ),
        name="sent_rows",
    )(place, *fields, *pieces)


def kept_kernel(place_ref, slice_ref, *refs):
    count = len(refs) - len(NEAR + FAR) - 6
    fields, pieces = refs[:count], refs[count:-6]
    sx_ref, sy_ref, white_ref, kept_ref, acc_ref, rows_ref = refs[-6:]
    lo = place_ref[0]
    product_of(place_ref, lambda span: load_bands(fields, lo, span), NEAR + FAR, pieces, acc_ref)
    for b in range(8):
        to = natural_place(slice_ref, lo if b < 4 else 1 - lo, b)
        for a in range(4):
            first = (b * 4 + a) * 8
            rows_ref[a, pl.ds(to, 8), :] = acc_ref[first : first + 8, :]
    chosen = moved_columns(lo)
    for block in range(rows_ref.shape[-1] // 128):
        span = slice(block * 256, block * 256 + 256)
        scale = sy_ref[:, :1] * sx_ref[:, span]
        for a in range(rows_ref.shape[0]):
            moved = jnp.dot(
                rows_ref[a, :, block * 128 : block * 128 + 128],
                chosen,
                precision=lax.Precision.HIGHEST,
            )
            kept_ref[a, :, span] = scale * moved - white_ref[:, a, span]


def kept_rows(place, slices, fields, pieces, sx, sy, white):
    count = sum(field.shape[0] * field.shape[2] for field in fields)
    total, width = fields[0].shape[-1], pieces[0].shape[-1]
    rows, times, columns = white.shape
    return pl.pallas_call(
        kept_kernel,
        out_shape=jax.ShapeDtypeStruct((times, rows, columns), jnp.float32),
        in_specs=[SMEM, SMEM] + [VMEM] * (len(fields) + len(pieces) + 3),
        out_specs=VMEM,
        scratch_shapes=[
            pltpu.VMEM((count, width), jnp.float32),
            pltpu.VMEM((times, rows, width), jnp.float32),
        ],
        compiler_params=pltpu.CompilerParams(vmem_limit_bytes=GRANT),
        cost_estimate=pl.CostEstimate(
            flops=2 * count * total * width, bytes_accessed=6 << 20, transcendentals=0
        ),
        name="kept_rows",
    )(place, slices, *fields, *pieces, sx, sy, white)


def gradient_kernel(place_ref, slice_ref, kept_ref, early_ref, late_ref, sx_ref, sy_ref, out_ref):
    lo = place_ref[0]
    chosen = moved_columns(1 - lo).astype(jnp.bfloat16)
    for block in range(early_ref.shape[-1] // 128):
        here = slice(block * 128, block * 128 + 128)
        span = slice(block * 256, block * 256 + 256)
        for ref, sources in ((early_ref, (0, 1, 4, 5, 6, 7)), (late_ref, (2, 3))):
            moved = jnp.dot(ref[:, here], chosen, preferred_element_type=jnp.float32)
            for k, b in enumerate(sources):
                to = natural_place(slice_ref, 1 - lo if b < 4 else lo, b)
                scale = sy_ref[pl.ds(to, 8), :1] * sx_ref[:, span]
                for a in range(4):
                    first = (k * 4 + a) * 8
                    out_ref[pl.ds(to, 8), a, span] = (
                        kept_ref[a, pl.ds(to, 8), span] + scale * moved[first : first + 8]
                    )


def whitened_gradient(place, slices, kept, early, late, sx, sy):
    times, rows, width = kept.shape
    return pl.pallas_call(
        gradient_kernel,
        out_shape=jax.ShapeDtypeStruct((rows, times, width), jnp.float32),
        in_specs=[SMEM, SMEM] + [VMEM] * 5,
        out_specs=VMEM,
        compiler_params=pltpu.CompilerParams(vmem_limit_bytes=GRANT),
        name="whitened_gradient",
    )(place, slices, kept, early, late, sx, sy)


def with_core(block):
    return block, shifted(block, "core", 1)


def local(event_counts, latent_mean, latent_var, eigen_basis, spectrum, correlation, whitened):
    hi, core = lax.axis_index("hi"), lax.axis_index("core")
    y, z, lo = (lax.axis_index(axis) for axis in ROW)
    time = hi * 2 + core
    ny, nz = lax.axis_size("y"), lax.axis_size("z")
    place = jnp.stack([lo, time, y, z]).astype(jnp.int32)

    kept, sent = split_columns(place, eigen_basis)
    other = shifted(sent, "lo", 1)
    mine = jnp.where(lo == 0, jnp.concatenate([kept, other]), jnp.concatenate([other, kept]))
    pseudo = moments(event_counts, latent_mean, latent_var).astype(jnp.bfloat16)[0]
    mine, pseudo = lax.optimization_barrier((mine, pseudo))
    before, after = shifted(pseudo, RING, 1), shifted(pseudo, RING, 3)
    block = jnp.stack([mine] + [shifted(mine, "y", step) for step in (1, 3, 2)])
    block, pseudo = lax.optimization_barrier((block, pseudo))
    own = with_core(pseudo)

    flips = jnp.array([0, 1, 2, 3], jnp.int32)
    before_flip, after_flip = 2 * (1 - lo), 2 * lo
    crossed = jnp.stack([before_flip, before_flip + 1, after_flip, after_flip + 1])
    slices = lax.bitwise_xor(time, jnp.concatenate([flips, crossed])).astype(jnp.int32)
    swapped = jnp.concatenate([slices[:4], slices[6:], slices[4:6]])
    factor = time_factor(correlation[0], 4)
    mix = jnp.take(factor, slices, axis=0)
    root = jnp.sqrt(spectrum)
    sx = lax.dynamic_slice_in_dim(root, time * 1024, 1024, 0)[None]
    row = (y * nz + z) * 2 + lo
    sy = lax.dynamic_slice_in_dim(root.reshape(4, lax.axis_size(ROW), -1), row, 1, 1).reshape(-1, 1)
    sy = jnp.broadcast_to(sy, (sy.shape[0], 128))

    def step(right, left):
        return shifted(right, "z", 1), shifted(left, "z", nz - 1)

    one = step(block, block)
    one, own = lax.optimization_barrier((one, own))
    two = step(*one)
    far = shifted(own[0], RING, 2)
    two, own, before, after, mix, sx, sy = lax.optimization_barrier(
        (two, own, before, after, mix, sx, sy)
    )
    three = step(*two)
    before, after = with_core(before), with_core(after)
    three, far, before, after = lax.optimization_barrier((three, far, before, after))
    last = step(three[0][:2], three[1][2:])
    far = with_core(far)
    pieces = [block, *one, *two, *three]

    fields = (*own, *far, *before, *after)
    near = near_product(place, fields, pieces)
    partial_y = first_product(mix, place, fields, last, near)
    pieces += last

    modes, width = partial_y.shape
    sent = partial_y.reshape(ny * nz, modes // (ny * nz), width)
    got = lax.all_to_all(sent, ("y", "z"), 0, 0, tiled=True)
    group = modes // (2 * ny * nz)
    got = got.reshape(ny * nz, 2, group, 2, 2, width // 4)
    got = got.transpose(3, 1, 4, 2, 0, 5).reshape(2, 2, 2 * group, -1)
    own, before, after = with_core(got), shifted(got, RING, 1), shifted(got, RING, 3)
    before, after, far = lax.optimization_barrier((before, after, (before[:1], after[1:])))
    far = [shifted(far[0], RING, 1), shifted(far[1], RING, 3)]
    own, before, after = lax.optimization_barrier((own, before, after))
    before, after = with_core(before), with_core(after)
    early = sent_rows(place, (*own, *before, *after), pieces)
    far, early = lax.optimization_barrier((far, early))
    got_early = shifted(early, "lo", 1)
    far = (*far, *(shifted(half, "core", 1) for half in far))
    got_late = shifted(sent_rows(place, far, pieces), "lo", 1)
    white = whitened.reshape(-1, *whitened.shape[3:])
    kept = kept_rows(place, slices, (*own, *far, *before, *after), pieces, sx, sy, white)
    gradient = whitened_gradient(place, swapped, kept, got_early, got_late, sx, sy)
    return gradient.reshape(whitened.shape)


def solution(mesh):
    finer = Mesh(mesh.devices.reshape(2, 2, 4, 8, 2), ("hi", "core", "y", "z", "lo"))
    placed = (
        P(TM, ROW, None),
        P(TM, ROW, None),
        P(TM, ROW, None),
        P(ROW, TM),
        P(),
        P(),
        P(None, ROW, None, None, TM),
    )
    return jax.shard_map(
        local,
        mesh=finer,
        in_specs=placed,
        out_specs=P(None, ROW, None, None, TM),
        check_vma=False,
    )
```

```python
import math

import jax
import jax.numpy as jnp
from jax import lax
from jax.experimental import pallas as pl
from jax.experimental.pallas import tpu as pltpu
from jax.sharding import Mesh
from jax.sharding import PartitionSpec as P

TM = ("hi", "core")
ROW = ("y", "z", "lo")
RING = ("hi", "lo")

HERMITE_NODES = (
    -2.0201828704560856,
    -0.9585724646138185,
    0.0,
    0.9585724646138185,
    2.0201828704560856,
)
HERMITE_WEIGHTS = (
    0.019953242059045913,
    0.3936193231522412,
    0.9453087204829419,
    0.3936193231522412,
    0.019953242059045913,
)
GRANT = 20 << 20
VMEM = pl.BlockSpec(memory_space=pltpu.VMEM)
SMEM = pl.BlockSpec(memory_space=pltpu.SMEM)


def moments(event_counts, latent_mean, latent_var):
    spread = jnp.sqrt(2.0 * latent_var)
    normal = 1.0 / math.sqrt(math.pi)
    points = [latent_mean + spread * abscissa for abscissa in HERMITE_NODES]
    rate_points = [jnp.exp(value) for value in points]
    mean_rate = sum(
        (weight * normal * value for weight, value in zip(HERMITE_WEIGHTS, rate_points))
    )
    covariance = sum(
        (
            weight * normal * (node_value - latent_mean) * (value - mean_rate)
            for weight, node_value, value in zip(HERMITE_WEIGHTS, points, rate_points)
        )
    )
    rate_var = sum(
        (
            weight * normal * (value - mean_rate) * (value - mean_rate)
            for weight, value in zip(HERMITE_WEIGHTS, rate_points)
        )
    )
    slope_gain = covariance / latent_var
    noise_var = rate_var - slope_gain * covariance + mean_rate
    return slope_gain * (event_counts.astype(latent_mean.dtype) - mean_rate) / noise_var


def time_factor(correlation, total):
    later = jnp.arange(total)[:, None]
    earlier = jnp.arange(total)[None, :]
    distance = jnp.maximum(later - earlier, 0).astype(correlation.dtype)
    lower = jnp.where(later >= earlier, jnp.power(correlation, distance), jnp.zeros_like(distance))
    column_scale = jnp.where(
        earlier == 0,
        jnp.ones_like(distance),
        jnp.sqrt(1.0 - correlation * correlation) * jnp.ones_like(distance),
    )
    return lower * column_scale


def shifted(array, axis, step):
    size = lax.axis_size(axis)
    return lax.ppermute(array, axis, [(k, (k + step) % size) for k in range(size)])


def split_kernel(first_ref, basis_ref, kept_ref, sent_ref):
    source = lax.broadcasted_iota(jnp.int32, (256, 128), 0)
    target = lax.broadcasted_iota(jnp.int32, (256, 128), 1)
    for half, ref in ((first_ref[0], kept_ref), (1 - first_ref[0], sent_ref)):
        match = source == (target // 8) * 16 + half * 8 + lax.rem(target, 8)
        chosen = match.astype(jnp.float32).astype(jnp.bfloat16)
        for block in range(basis_ref.shape[1] // 256):
            moved = jnp.dot(
                basis_ref[:, block * 256 : block * 256 + 256],
                chosen,
                preferred_element_type=jnp.float32,
            )
            ref[:, block * 128 : block * 128 + 128] = moved.astype(jnp.bfloat16)


def split_columns(place, basis):
    rows, columns = basis.shape
    half = jax.ShapeDtypeStruct((rows, columns // 2), basis.dtype)
    return pl.pallas_call(
        split_kernel,
        out_shape=(half, half),
        in_specs=[SMEM, VMEM],
        out_specs=(VMEM, VMEM),
        compiler_params=pltpu.CompilerParams(vmem_limit_bytes=GRANT),
        name="split_columns",
    )(place, basis)


def columns_at(index):
    return pl.ds(pl.multiple_of(index * 128, 128), 128)


def product_of(place_ref, load, spec, pieces, acc_ref):
    acc_ref[...] = jnp.zeros_like(acc_ref)
    y_here, z_here = place_ref[2], place_ref[3]
    for blocks, ref in zip(spec, pieces):
        where = [
            columns_at(lax.rem(y_here + dy, 4) * 8 + lax.rem(z_here + dz, 8)) for dz, dy in blocks
        ]
        field = jnp.concatenate([load(span) for span in where], axis=1)
        basis = jnp.concatenate([ref[k] for k in range(len(blocks))], axis=0)
        acc_ref[...] += jnp.dot(field, basis, preferred_element_type=jnp.float32)


NEAR = tuple(tuple((dz, dy) for dy in (0, 3, 1, 2)) for dz in (0, 7, 1, 6, 2, 5, 3))
FAR = (((4, 0), (4, 3)), ((4, 1), (4, 2)))


def near_kernel(place_ref, *refs):
    blocks, pieces, acc_ref = refs[:8], refs[8:-1], refs[-1]

    def load(span):
        return jnp.concatenate([ref[:, span] for ref in blocks], axis=0)

    product_of(place_ref, load, NEAR, pieces, acc_ref)


def near_product(place, fields, pieces):
    rows = sum(field.shape[0] for field in fields)
    width = pieces[0].shape[-1]
    return pl.pallas_call(
        near_kernel,
        out_shape=jax.ShapeDtypeStruct((rows, width), jnp.float32),
        in_specs=[SMEM] + [VMEM] * (8 + len(pieces)),
        out_specs=VMEM,
        compiler_params=pltpu.CompilerParams(vmem_limit_bytes=GRANT),
        cost_estimate=pl.CostEstimate(
            flops=2 * rows * 3072 * width, bytes_accessed=8 << 20, transcendentals=0
        ),
        name="near_product",
    )(place, *fields, *pieces)


def first_kernel(mix_ref, place_ref, *refs):
    blocks, pieces, (near_ref, out_ref, acc_ref, tmp_ref) = refs[:8], refs[8:-4], refs[-4:]
    rows = blocks[0].shape[0]
    lo = place_ref[0]

    def load(span):
        return jnp.concatenate([ref[:, span] for ref in blocks], axis=0)

    product_of(place_ref, load, FAR, pieces, acc_ref)
    acc_ref[...] += near_ref[...]
    for a in range(4):
        for group in range(2):
            mixed = sum(
                mix_ref[group * 4 + t, a]
                * acc_ref[(group * 4 + t) * rows : (group * 4 + t + 1) * rows, :]
                for t in range(4)
            )
            at = lo if group == 0 else 1 - lo
            tmp_ref[pl.ds(pl.multiple_of(at * rows, rows), rows), :] = mixed
        out_ref[:, a * 2 * rows : (a + 1) * 2 * rows] = tmp_ref[...].T.astype(jnp.bfloat16)


def first_product(mix, place, fields, pieces, near):
    rows = fields[0].shape[0]
    width = near.shape[-1]
    return pl.pallas_call(
        first_kernel,
        out_shape=jax.ShapeDtypeStruct((width, 8 * rows), jnp.bfloat16),
        in_specs=[SMEM, SMEM] + [VMEM] * (9 + len(pieces)),
        out_specs=VMEM,
        scratch_shapes=[
            pltpu.VMEM((8 * rows, width), jnp.float32),
            pltpu.VMEM((2 * rows, width), jnp.float32),
        ],
        compiler_params=pltpu.CompilerParams(vmem_limit_bytes=GRANT),
        cost_estimate=pl.CostEstimate(
            flops=2 * 8 * rows * 1024 * width, bytes_accessed=4 << 20, transcendentals=0
        ),
        name="first_product",
    )(mix, place, *fields, *pieces, near)


def load_bands(fields, which, span):
    return jnp.concatenate(
        [ref[part, which, :, span] for ref in fields for part in range(ref.shape[0])], axis=0
    )


def natural_place(slice_ref, half_of, block):
    return pl.multiple_of((slice_ref[block] * 2 + half_of) * 8, 8)


def moved_columns(half):
    source = lax.broadcasted_iota(jnp.int32, (128, 256), 0)
    target = lax.broadcasted_iota(jnp.int32, (128, 256), 1)
    return (target == (source // 8) * 16 + half * 8 + lax.rem(source, 8)).astype(jnp.float32)


def sent_kernel(place_ref, *refs):
    count = len(refs) - len(NEAR + FAR) - 2
    fields, pieces, (sent_ref, acc_ref) = refs[:count], refs[count:-2], refs[-2:]
    which = 1 - place_ref[0]
    product_of(
        place_ref, lambda span: load_bands(fields, which, span), NEAR + FAR, pieces, acc_ref
    )
    sent_ref[...] = acc_ref[...].astype(jnp.bfloat16)


def sent_rows(place, fields, pieces):
    count = sum(field.shape[0] * field.shape[2] for field in fields)
    total, width = fields[0].shape[-1], pieces[0].shape[-1]
    return pl.pallas_call(
        sent_kernel,
        out_shape=jax.ShapeDtypeStruct((count, width), jnp.bfloat16),
        in_specs=[SMEM] + [VMEM] * (len(fields) + len(pieces)),
        out_specs=VMEM,
        scratch_shapes=[pltpu.VMEM((count, width), jnp.float32)],
        compiler_params=pltpu.CompilerParams(vmem_limit_bytes=GRANT),
        cost_estimate=pl.CostEstimate(
            flops=2 * count * total * width, bytes_accessed=6 << 20, transcendentals=0
        ),
        name="sent_rows",
    )(place, *fields, *pieces)


def kept_kernel(place_ref, slice_ref, *refs):
    count = len(refs) - len(NEAR + FAR) - 6
    fields, pieces = refs[:count], refs[count:-6]
    sx_ref, sy_ref, white_ref, kept_ref, acc_ref, rows_ref = refs[-6:]
    lo = place_ref[0]
    product_of(place_ref, lambda span: load_bands(fields, lo, span), NEAR + FAR, pieces, acc_ref)
    for b in range(8):
        to = natural_place(slice_ref, lo if b < 4 else 1 - lo, b)
        for a in range(4):
            first = (b * 4 + a) * 8
            rows_ref[a, pl.ds(to, 8), :] = acc_ref[first : first + 8, :]
    chosen = moved_columns(lo)
    for block in range(rows_ref.shape[-1] // 128):
        span = slice(block * 256, block * 256 + 256)
        scale = sy_ref[:, :1] * sx_ref[:, span]
        for a in range(rows_ref.shape[0]):
            moved = jnp.dot(
                rows_ref[a, :, block * 128 : block * 128 + 128],
                chosen,
                precision=lax.Precision.HIGHEST,
            )
            kept_ref[a, :, span] = scale * moved - white_ref[:, a, span]


def kept_rows(place, slices, fields, pieces, sx, sy, white):
    count = sum(field.shape[0] * field.shape[2] for field in fields)
    total, width = fields[0].shape[-1], pieces[0].shape[-1]
    rows, times, columns = white.shape
    return pl.pallas_call(
        kept_kernel,
        out_shape=jax.ShapeDtypeStruct((times, rows, columns), jnp.float32),
        in_specs=[SMEM, SMEM] + [VMEM] * (len(fields) + len(pieces) + 3),
        out_specs=VMEM,
        scratch_shapes=[
            pltpu.VMEM((count, width), jnp.float32),
            pltpu.VMEM((times, rows, width), jnp.float32),
        ],
        compiler_params=pltpu.CompilerParams(vmem_limit_bytes=GRANT),
        cost_estimate=pl.CostEstimate(
            flops=2 * count * total * width, bytes_accessed=6 << 20, transcendentals=0
        ),
        name="kept_rows",
    )(place, slices, *fields, *pieces, sx, sy, white)


def gradient_kernel(place_ref, slice_ref, kept_ref, early_ref, late_ref, sx_ref, sy_ref, out_ref):
    lo = place_ref[0]
    chosen = moved_columns(1 - lo).astype(jnp.bfloat16)
    for block in range(early_ref.shape[-1] // 128):
        here = slice(block * 128, block * 128 + 128)
        span = slice(block * 256, block * 256 + 256)
        for ref, sources in ((early_ref, (0, 1, 4, 5, 6, 7)), (late_ref, (2, 3))):
            moved = jnp.dot(ref[:, here], chosen, preferred_element_type=jnp.float32)
            for k, b in enumerate(sources):
                to = natural_place(slice_ref, 1 - lo if b < 4 else lo, b)
                scale = sy_ref[pl.ds(to, 8), :1] * sx_ref[:, span]
                for a in range(4):
                    first = (k * 4 + a) * 8
                    out_ref[pl.ds(to, 8), a, span] = (
                        kept_ref[a, pl.ds(to, 8), span] + scale * moved[first : first + 8]
                    )


def whitened_gradient(place, slices, kept, early, late, sx, sy):
    times, rows, width = kept.shape
    return pl.pallas_call(
        gradient_kernel,
        out_shape=jax.ShapeDtypeStruct((rows, times, width), jnp.float32),
        in_specs=[SMEM, SMEM] + [VMEM] * 5,
        out_specs=VMEM,
        compiler_params=pltpu.CompilerParams(vmem_limit_bytes=GRANT),
        name="whitened_gradient",
    )(place, slices, kept, early, late, sx, sy)


def with_core(block):
    return block, shifted(block, "core", 1)


def local(event_counts, latent_mean, latent_var, eigen_basis, spectrum, correlation, whitened):
    hi, core = lax.axis_index("hi"), lax.axis_index("core")
    y, z, lo = (lax.axis_index(axis) for axis in ROW)
    time = hi * 2 + core
    ny, nz = lax.axis_size("y"), lax.axis_size("z")
    place = jnp.stack([lo, time, y, z]).astype(jnp.int32)

    kept, sent = split_columns(place, eigen_basis)
    other = shifted(sent, "lo", 1)
    mine = jnp.where(lo == 0, jnp.concatenate([kept, other]), jnp.concatenate([other, kept]))
    pseudo = moments(event_counts, latent_mean, latent_var).astype(jnp.bfloat16)[0]
    mine, pseudo = lax.optimization_barrier((mine, pseudo))
    before, after = shifted(pseudo, RING, 1), shifted(pseudo, RING, 3)
    block = jnp.stack([mine] + [shifted(mine, "y", step) for step in (1, 3, 2)])
    block, pseudo = lax.optimization_barrier((block, pseudo))
    own = with_core(pseudo)

    flips = jnp.array([0, 1, 2, 3], jnp.int32)
    before_flip, after_flip = 2 * (1 - lo), 2 * lo
    crossed = jnp.stack([before_flip, before_flip + 1, after_flip, after_flip + 1])
    slices = lax.bitwise_xor(time, jnp.concatenate([flips, crossed])).astype(jnp.int32)
    swapped = jnp.concatenate([slices[:4], slices[6:], slices[4:6]])
    factor = time_factor(correlation[0], 4)
    mix = jnp.take(factor, slices, axis=0)
    root = jnp.sqrt(spectrum)
    sx = lax.dynamic_slice_in_dim(root, time * 1024, 1024, 0)[None]
    row = (y * nz + z) * 2 + lo
    sy = lax.dynamic_slice_in_dim(root.reshape(4, lax.axis_size(ROW), -1), row, 1, 1).reshape(-1, 1)
    sy = jnp.broadcast_to(sy, (sy.shape[0], 128))

    def step(right, left):
        return shifted(right, "z", 1), shifted(left, "z", nz - 1)

    one = step(block, block)
    one, own, before = lax.optimization_barrier((one, own, before))
    two = step(*one)
    far = shifted(own[0], RING, 2)
    before = with_core(before)
    two, after, mix, sx, sy = lax.optimization_barrier((two, after, mix, sx, sy))
    three = step(*two)
    after = with_core(after)
    three, far, before, after = lax.optimization_barrier((three, far, before, after))
    last = step(three[0][:2], three[1][2:])
    far = with_core(far)
    pieces = [block, *one, *two, *three]

    fields = (*own, *far, *before, *after)
    near = near_product(place, fields, pieces)
    partial_y = first_product(mix, place, fields, last, near)
    pieces += last

    modes, width = partial_y.shape
    sent = partial_y.reshape(ny * nz, modes // (ny * nz), width)
    got = lax.all_to_all(sent, ("y", "z"), 0, 0, tiled=True)
    group = modes // (2 * ny * nz)
    got = got.reshape(ny * nz, 2, group, 2, 2, width // 4)
    got = got.transpose(3, 1, 4, 2, 0, 5).reshape(2, 2, 2 * group, -1)
    own, before, after = with_core(got), shifted(got, RING, 1), shifted(got, RING, 3)
    before, after, far = lax.optimization_barrier((before, after, (before[:1], after[1:])))
    far = [shifted(far[0], RING, 1), shifted(far[1], RING, 3)]
    own, before, after = lax.optimization_barrier((own, before, after))
    before, after = with_core(before), with_core(after)
    early = sent_rows(place, (*own, *before, *after), pieces)
    far, early = lax.optimization_barrier((far, early))
    got_early = shifted(early, "lo", 1)
    far = (*far, *(shifted(half, "core", 1) for half in far))
    got_late = shifted(sent_rows(place, far, pieces), "lo", 1)
    white = whitened.reshape(-1, *whitened.shape[3:])
    kept = kept_rows(place, slices, (*own, *far, *before, *after), pieces, sx, sy, white)
    gradient = whitened_gradient(place, swapped, kept, got_early, got_late, sx, sy)
    return gradient.reshape(whitened.shape)


def solution(mesh):
    finer = Mesh(mesh.devices.reshape(2, 2, 4, 8, 2), ("hi", "core", "y", "z", "lo"))
    placed = (
        P(TM, ROW, None),
        P(TM, ROW, None),
        P(TM, ROW, None),
        P(ROW, TM),
        P(),
        P(),
        P(None, ROW, None, None, TM),
    )
    return jax.shard_map(
        local,
        mesh=finer,
        in_specs=placed,
        out_specs=P(None, ROW, None, None, TM),
        check_vma=False,
    )
```

```python
import math

import jax
import jax.numpy as jnp
from jax import lax
from jax.experimental import pallas as pl
from jax.experimental.pallas import tpu as pltpu
from jax.sharding import Mesh
from jax.sharding import PartitionSpec as P

TM = ("hi", "core")
ROW = ("y", "z", "lo")
RING = ("hi", "lo")

HERMITE_NODES = (
    -2.0201828704560856,
    -0.9585724646138185,
    0.0,
    0.9585724646138185,
    2.0201828704560856,
)
HERMITE_WEIGHTS = (
    0.019953242059045913,
    0.3936193231522412,
    0.9453087204829419,
    0.3936193231522412,
    0.019953242059045913,
)
GRANT = 20 << 20
VMEM = pl.BlockSpec(memory_space=pltpu.VMEM)
SMEM = pl.BlockSpec(memory_space=pltpu.SMEM)


def moments(event_counts, latent_mean, latent_var):
    spread = jnp.sqrt(2.0 * latent_var)
    normal = 1.0 / math.sqrt(math.pi)
    points = [latent_mean + spread * abscissa for abscissa in HERMITE_NODES]
    rate_points = [jnp.exp(value) for value in points]
    mean_rate = sum(
        (weight * normal * value for weight, value in zip(HERMITE_WEIGHTS, rate_points))
    )
    covariance = sum(
        (
            weight * normal * (node_value - latent_mean) * (value - mean_rate)
            for weight, node_value, value in zip(HERMITE_WEIGHTS, points, rate_points)
        )
    )
    rate_var = sum(
        (
            weight * normal * (value - mean_rate) * (value - mean_rate)
            for weight, value in zip(HERMITE_WEIGHTS, rate_points)
        )
    )
    slope_gain = covariance / latent_var
    noise_var = rate_var - slope_gain * covariance + mean_rate
    return slope_gain * (event_counts.astype(latent_mean.dtype) - mean_rate) / noise_var


def time_factor(correlation, total):
    later = jnp.arange(total)[:, None]
    earlier = jnp.arange(total)[None, :]
    distance = jnp.maximum(later - earlier, 0).astype(correlation.dtype)
    lower = jnp.where(later >= earlier, jnp.power(correlation, distance), jnp.zeros_like(distance))
    column_scale = jnp.where(
        earlier == 0,
        jnp.ones_like(distance),
        jnp.sqrt(1.0 - correlation * correlation) * jnp.ones_like(distance),
    )
    return lower * column_scale


def shifted(array, axis, step):
    size = lax.axis_size(axis)
    return lax.ppermute(array, axis, [(k, (k + step) % size) for k in range(size)])


def split_kernel(place_ref, basis_ref, kept_ref):
    source = lax.broadcasted_iota(jnp.int32, (256, 128), 0)
    target = lax.broadcasted_iota(jnp.int32, (256, 128), 1)
    match = source == (target // 8) * 16 + place_ref[0] * 8 + lax.rem(target, 8)
    chosen = match.astype(jnp.float32).astype(jnp.bfloat16)
    for block in range(basis_ref.shape[1] // 256):
        moved = jnp.dot(
            basis_ref[:, block * 256 : block * 256 + 256],
            chosen,
            preferred_element_type=jnp.float32,
        )
        kept_ref[:, block * 128 : block * 128 + 128] = moved.astype(jnp.bfloat16)


def split_columns(place, basis):
    rows, columns = basis.shape
    return pl.pallas_call(
        split_kernel,
        out_shape=jax.ShapeDtypeStruct((rows, columns // 2), basis.dtype),
        in_specs=[SMEM, VMEM],
        out_specs=VMEM,
        compiler_params=pltpu.CompilerParams(vmem_limit_bytes=GRANT),
        name="split_columns",
    )(place, basis)


def columns_at(index):
    return pl.ds(pl.multiple_of(index * 128, 128), 128)


def product_of(place_ref, load, spec, pieces, acc_ref):
    acc_ref[...] = jnp.zeros_like(acc_ref)
    y_here, z_here = place_ref[2], place_ref[3]
    for blocks, ref in zip(spec, pieces):
        where = [
            columns_at(lax.rem(y_here + dy, 4) * 8 + lax.rem(z_here + dz, 8)) for dz, dy in blocks
        ]
        field = jnp.concatenate([load(span) for span in where], axis=1)
        basis = jnp.concatenate([ref[k] for k in range(len(blocks))], axis=0)
        acc_ref[...] += jnp.dot(field, basis, preferred_element_type=jnp.float32)


NEAR = tuple(tuple((dz, dy) for dy in (0, 3, 1, 2)) for dz in (0, 7, 1, 6, 2, 5, 3))
FAR = (((4, 0), (4, 3)), ((4, 1), (4, 2)))


def near_kernel(place_ref, *refs):
    blocks, pieces, acc_ref = refs[:8], refs[8:-1], refs[-1]

    def load(span):
        return jnp.concatenate([ref[:, span] for ref in blocks], axis=0)

    product_of(place_ref, load, NEAR, pieces, acc_ref)


def near_product(place, fields, pieces):
    rows = sum(field.shape[0] for field in fields)
    width = pieces[0].shape[-1]
    return pl.pallas_call(
        near_kernel,
        out_shape=jax.ShapeDtypeStruct((rows, width), jnp.float32),
        in_specs=[SMEM] + [VMEM] * (8 + len(pieces)),
        out_specs=VMEM,
        compiler_params=pltpu.CompilerParams(vmem_limit_bytes=GRANT),
        cost_estimate=pl.CostEstimate(
            flops=2 * rows * 3072 * width, bytes_accessed=8 << 20, transcendentals=0
        ),
        name="near_product",
    )(place, *fields, *pieces)


def first_kernel(mix_ref, place_ref, *refs):
    blocks, pieces, (near_ref, out_ref, acc_ref, tmp_ref) = refs[:8], refs[8:-4], refs[-4:]
    rows = blocks[0].shape[0]
    lo = place_ref[0]

    def load(span):
        return jnp.concatenate([ref[:, span] for ref in blocks], axis=0)

    product_of(place_ref, load, FAR, pieces, acc_ref)
    acc_ref[...] += near_ref[...]
    for a in range(4):
        for group in range(2):
            mixed = sum(
                mix_ref[group * 4 + t, a]
                * acc_ref[(group * 4 + t) * rows : (group * 4 + t + 1) * rows, :]
                for t in range(4)
            )
            at = lo if group == 0 else 1 - lo
            tmp_ref[pl.ds(pl.multiple_of(at * rows, rows), rows), :] = mixed
        out_ref[:, a * 2 * rows : (a + 1) * 2 * rows] = tmp_ref[...].T.astype(jnp.bfloat16)


def first_product(mix, place, fields, pieces, near):
    rows = fields[0].shape[0]
    width = near.shape[-1]
    return pl.pallas_call(
        first_kernel,
        out_shape=jax.ShapeDtypeStruct((width, 8 * rows), jnp.bfloat16),
        in_specs=[SMEM, SMEM] + [VMEM] * (9 + len(pieces)),
        out_specs=VMEM,
        scratch_shapes=[
            pltpu.VMEM((8 * rows, width), jnp.float32),
            pltpu.VMEM((2 * rows, width), jnp.float32),
        ],
        compiler_params=pltpu.CompilerParams(vmem_limit_bytes=GRANT),
        cost_estimate=pl.CostEstimate(
            flops=2 * 8 * rows * 1024 * width, bytes_accessed=4 << 20, transcendentals=0
        ),
        name="first_product",
    )(mix, place, *fields, *pieces, near)


def load_bands(fields, which, span):
    return jnp.concatenate(
        [ref[part, which, :, span] for ref in fields for part in range(ref.shape[0])], axis=0
    )


def natural_place(slice_ref, half_of, block):
    return pl.multiple_of((slice_ref[block] * 2 + half_of) * 8, 8)


def moved_columns(half):
    source = lax.broadcasted_iota(jnp.int32, (128, 256), 0)
    target = lax.broadcasted_iota(jnp.int32, (128, 256), 1)
    return (target == (source // 8) * 16 + half * 8 + lax.rem(source, 8)).astype(jnp.float32)


def sent_kernel(place_ref, *refs):
    count = len(refs) - len(NEAR + FAR) - 2
    fields, pieces, (sent_ref, acc_ref) = refs[:count], refs[count:-2], refs[-2:]
    which = 1 - place_ref[0]
    product_of(
        place_ref, lambda span: load_bands(fields, which, span), NEAR + FAR, pieces, acc_ref
    )
    sent_ref[...] = acc_ref[...].astype(jnp.bfloat16)


def sent_rows(place, fields, pieces):
    count = sum(field.shape[0] * field.shape[2] for field in fields)
    total, width = fields[0].shape[-1], pieces[0].shape[-1]
    return pl.pallas_call(
        sent_kernel,
        out_shape=jax.ShapeDtypeStruct((count, width), jnp.bfloat16),
        in_specs=[SMEM] + [VMEM] * (len(fields) + len(pieces)),
        out_specs=VMEM,
        scratch_shapes=[pltpu.VMEM((count, width), jnp.float32)],
        compiler_params=pltpu.CompilerParams(vmem_limit_bytes=GRANT),
        cost_estimate=pl.CostEstimate(
            flops=2 * count * total * width, bytes_accessed=6 << 20, transcendentals=0
        ),
        name="sent_rows",
    )(place, *fields, *pieces)


def kept_kernel(place_ref, slice_ref, *refs):
    count = len(refs) - len(NEAR + FAR) - 6
    fields, pieces = refs[:count], refs[count:-6]
    sx_ref, sy_ref, white_ref, kept_ref, acc_ref, rows_ref = refs[-6:]
    lo = place_ref[0]
    product_of(place_ref, lambda span: load_bands(fields, lo, span), NEAR + FAR, pieces, acc_ref)
    for b in range(8):
        to = natural_place(slice_ref, lo if b < 4 else 1 - lo, b)
        for a in range(4):
            first = (b * 4 + a) * 8
            rows_ref[a, pl.ds(to, 8), :] = acc_ref[first : first + 8, :]
    chosen = moved_columns(lo)
    for block in range(rows_ref.shape[-1] // 128):
        span = slice(block * 256, block * 256 + 256)
        scale = sy_ref[:, :1] * sx_ref[:, span]
        for a in range(rows_ref.shape[0]):
            moved = jnp.dot(
                rows_ref[a, :, block * 128 : block * 128 + 128],
                chosen,
                precision=lax.Precision.HIGHEST,
            )
            kept_ref[a, :, span] = scale * moved - white_ref[:, a, span]


def kept_rows(place, slices, fields, pieces, sx, sy, white):
    count = sum(field.shape[0] * field.shape[2] for field in fields)
    total, width = fields[0].shape[-1], pieces[0].shape[-1]
    rows, times, columns = white.shape
    return pl.pallas_call(
        kept_kernel,
        out_shape=jax.ShapeDtypeStruct((times, rows, columns), jnp.float32),
        in_specs=[SMEM, SMEM] + [VMEM] * (len(fields) + len(pieces) + 3),
        out_specs=VMEM,
        scratch_shapes=[
            pltpu.VMEM((count, width), jnp.float32),
            pltpu.VMEM((times, rows, width), jnp.float32),
        ],
        compiler_params=pltpu.CompilerParams(vmem_limit_bytes=GRANT),
        cost_estimate=pl.CostEstimate(
            flops=2 * count * total * width, bytes_accessed=6 << 20, transcendentals=0
        ),
        name="kept_rows",
    )(place, slices, *fields, *pieces, sx, sy, white)


def gradient_kernel(place_ref, slice_ref, kept_ref, early_ref, late_ref, sx_ref, sy_ref, out_ref):
    lo = place_ref[0]
    chosen = moved_columns(1 - lo).astype(jnp.bfloat16)
    for block in range(early_ref.shape[-1] // 128):
        here = slice(block * 128, block * 128 + 128)
        span = slice(block * 256, block * 256 + 256)
        for ref, sources in ((early_ref, (0, 1, 4, 5, 6, 7)), (late_ref, (2, 3))):
            moved = jnp.dot(ref[:, here], chosen, preferred_element_type=jnp.float32)
            for k, b in enumerate(sources):
                to = natural_place(slice_ref, 1 - lo if b < 4 else lo, b)
                scale = sy_ref[pl.ds(to, 8), :1] * sx_ref[:, span]
                for a in range(4):
                    first = (k * 4 + a) * 8
                    out_ref[pl.ds(to, 8), a, span] = (
                        kept_ref[a, pl.ds(to, 8), span] + scale * moved[first : first + 8]
                    )


def whitened_gradient(place, slices, kept, early, late, sx, sy):
    times, rows, width = kept.shape
    return pl.pallas_call(
        gradient_kernel,
        out_shape=jax.ShapeDtypeStruct((rows, times, width), jnp.float32),
        in_specs=[SMEM, SMEM] + [VMEM] * 5,
        out_specs=VMEM,
        compiler_params=pltpu.CompilerParams(vmem_limit_bytes=GRANT),
        name="whitened_gradient",
    )(place, slices, kept, early, late, sx, sy)


def with_core(block):
    return block, shifted(block, "core", 1)


def local(event_counts, latent_mean, latent_var, eigen_basis, spectrum, correlation, whitened):
    hi, core = lax.axis_index("hi"), lax.axis_index("core")
    y, z, lo = (lax.axis_index(axis) for axis in ROW)
    time = hi * 2 + core
    ny, nz = lax.axis_size("y"), lax.axis_size("z")
    place = jnp.stack([lo, time, y, z]).astype(jnp.int32)

    other = shifted(eigen_basis, "lo", 1)
    pair = jnp.where(
        lo == 0,
        jnp.concatenate([eigen_basis, other]),
        jnp.concatenate([other, eigen_basis]),
    )
    mine = split_columns(place, pair)
    pseudo = moments(event_counts, latent_mean, latent_var).astype(jnp.bfloat16)[0]
    mine, pseudo = lax.optimization_barrier((mine, pseudo))
    before, after = shifted(pseudo, RING, 1), shifted(pseudo, RING, 3)
    block = jnp.stack([mine] + [shifted(mine, "y", step) for step in (1, 3, 2)])
    block, pseudo = lax.optimization_barrier((block, pseudo))
    own = lax.optimization_barrier(with_core(pseudo))
    far = shifted(own[0], RING, 2)

    flips = jnp.array([0, 1, 2, 3], jnp.int32)
    before_flip, after_flip = 2 * (1 - lo), 2 * lo
    crossed = jnp.stack([before_flip, before_flip + 1, after_flip, after_flip + 1])
    slices = lax.bitwise_xor(time, jnp.concatenate([flips, crossed])).astype(jnp.int32)
    swapped = jnp.concatenate([slices[:4], slices[6:], slices[4:6]])
    factor = time_factor(correlation[0], 4)
    mix = jnp.take(factor, slices, axis=0)
    root = jnp.sqrt(spectrum)
    sx = lax.dynamic_slice_in_dim(root, time * 1024, 1024, 0)[None]
    row = (y * nz + z) * 2 + lo
    sy = lax.dynamic_slice_in_dim(root.reshape(4, lax.axis_size(ROW), -1), row, 1, 1).reshape(-1, 1)
    sy = jnp.broadcast_to(sy, (sy.shape[0], 128))

    right, left = shifted(block, "z", 1), shifted(block, "z", nz - 1)
    pieces = [block, right, left]
    right, left, before, after = lax.optimization_barrier((right, left, before, after))
    before, after = with_core(before), with_core(after)
    right, left = shifted(right, "z", 1), shifted(left, "z", nz - 1)
    pieces += [right, left]
    right, left, far, own, mix, sx, sy = lax.optimization_barrier(
        (right, left, far, own, mix, sx, sy)
    )
    far = with_core(far)
    right, left = shifted(right, "z", 1), shifted(left, "z", nz - 1)
    pieces += [right, left]
    right, left, far, before, after = lax.optimization_barrier((right, left, far, before, after))
    last = [shifted(right[:2], "z", 1), shifted(left[2:], "z", nz - 1)]

    fields = (*own, *far, *before, *after)
    near = near_product(place, fields, pieces)
    partial_y = first_product(mix, place, fields, last, near)
    pieces += last

    modes, width = partial_y.shape
    sent = partial_y.reshape(ny * nz, modes // (ny * nz), width)
    got = lax.all_to_all(sent, ("y", "z"), 0, 0, tiled=True)
    group = modes // (2 * ny * nz)
    got = got.reshape(ny * nz, 2, group, 2, 2, width // 4)
    got = got.transpose(3, 1, 4, 2, 0, 5).reshape(2, 2, 2 * group, -1)
    own, before, after = with_core(got), shifted(got, RING, 1), shifted(got, RING, 3)
    before, after, far = lax.optimization_barrier((before, after, (before[:1], after[1:])))
    far = [shifted(far[0], RING, 1), shifted(far[1], RING, 3)]
    own, before, after = lax.optimization_barrier((own, before, after))
    before, after = with_core(before), with_core(after)
    early = sent_rows(place, (*own, *before, *after), pieces)
    far, early = lax.optimization_barrier((far, early))
    got_early = shifted(early, "lo", 1)
    far = (*far, *(shifted(half, "core", 1) for half in far))
    got_late = shifted(sent_rows(place, far, pieces), "lo", 1)
    white = whitened.reshape(-1, *whitened.shape[3:])
    kept = kept_rows(place, slices, (*own, *far, *before, *after), pieces, sx, sy, white)
    gradient = whitened_gradient(place, swapped, kept, got_early, got_late, sx, sy)
    return gradient.reshape(whitened.shape)


def solution(mesh):
    finer = Mesh(mesh.devices.reshape(2, 2, 4, 8, 2), ("hi", "core", "y", "z", "lo"))
    placed = (
        P(TM, ROW, None),
        P(TM, ROW, None),
        P(TM, ROW, None),
        P(ROW, TM),
        P(),
        P(),
        P(None, ROW, None, None, TM),
    )
    return jax.shard_map(
        local,
        mesh=finer,
        in_specs=placed,
        out_specs=P(None, ROW, None, None, TM),
        check_vma=False,
    )
```

```python
import math

import jax
import jax.numpy as jnp
from jax import lax
from jax.experimental import pallas as pl
from jax.experimental.pallas import tpu as pltpu
from jax.sharding import Mesh
from jax.sharding import PartitionSpec as P

TM = ("hi", "core")
ROW = ("y", "z", "lo")
RING = ("hi", "lo")

HERMITE_NODES = (
    -2.0201828704560856,
    -0.9585724646138185,
    0.0,
    0.9585724646138185,
    2.0201828704560856,
)
HERMITE_WEIGHTS = (
    0.019953242059045913,
    0.3936193231522412,
    0.9453087204829419,
    0.3936193231522412,
    0.019953242059045913,
)
GRANT = 20 << 20
VMEM = pl.BlockSpec(memory_space=pltpu.VMEM)
SMEM = pl.BlockSpec(memory_space=pltpu.SMEM)


def moments(event_counts, latent_mean, latent_var):
    spread = jnp.sqrt(2.0 * latent_var)
    normal = 1.0 / math.sqrt(math.pi)
    points = [latent_mean + spread * abscissa for abscissa in HERMITE_NODES]
    rate_points = [jnp.exp(value) for value in points]
    mean_rate = sum(
        (weight * normal * value for weight, value in zip(HERMITE_WEIGHTS, rate_points))
    )
    covariance = sum(
        (
            weight * normal * (node_value - latent_mean) * (value - mean_rate)
            for weight, node_value, value in zip(HERMITE_WEIGHTS, points, rate_points)
        )
    )
    rate_var = sum(
        (
            weight * normal * (value - mean_rate) * (value - mean_rate)
            for weight, value in zip(HERMITE_WEIGHTS, rate_points)
        )
    )
    slope_gain = covariance / latent_var
    noise_var = rate_var - slope_gain * covariance + mean_rate
    return slope_gain * (event_counts.astype(latent_mean.dtype) - mean_rate) / noise_var


def time_factor(correlation, total):
    later = jnp.arange(total)[:, None]
    earlier = jnp.arange(total)[None, :]
    distance = jnp.maximum(later - earlier, 0).astype(correlation.dtype)
    lower = jnp.where(later >= earlier, jnp.power(correlation, distance), jnp.zeros_like(distance))
    column_scale = jnp.where(
        earlier == 0,
        jnp.ones_like(distance),
        jnp.sqrt(1.0 - correlation * correlation) * jnp.ones_like(distance),
    )
    return lower * column_scale


def shifted(array, axis, step):
    size = lax.axis_size(axis)
    return lax.ppermute(array, axis, [(k, (k + step) % size) for k in range(size)])


def split_kernel(place_ref, basis_ref, kept_ref):
    source = lax.broadcasted_iota(jnp.int32, (256, 128), 0)
    target = lax.broadcasted_iota(jnp.int32, (256, 128), 1)
    match = source == (target // 8) * 16 + place_ref[0] * 8 + lax.rem(target, 8)
    chosen = match.astype(jnp.float32).astype(jnp.bfloat16)
    for block in range(basis_ref.shape[1] // 256):
        moved = jnp.dot(
            basis_ref[:, block * 256 : block * 256 + 256],
            chosen,
            preferred_element_type=jnp.float32,
        )
        kept_ref[:, block * 128 : block * 128 + 128] = moved.astype(jnp.bfloat16)


def split_columns(place, basis):
    rows, columns = basis.shape
    return pl.pallas_call(
        split_kernel,
        out_shape=jax.ShapeDtypeStruct((rows, columns // 2), basis.dtype),
        in_specs=[SMEM, VMEM],
        out_specs=VMEM,
        compiler_params=pltpu.CompilerParams(vmem_limit_bytes=GRANT),
        name="split_columns",
    )(place, basis)


def columns_at(index):
    return pl.ds(pl.multiple_of(index * 128, 128), 128)


def product_of(place_ref, load, spec, pieces, acc_ref):
    acc_ref[...] = jnp.zeros_like(acc_ref)
    y_here, z_here = place_ref[2], place_ref[3]
    for blocks, ref in zip(spec, pieces):
        where = [
            columns_at(lax.rem(y_here + dy, 4) * 8 + lax.rem(z_here + dz, 8)) for dz, dy in blocks
        ]
        field = jnp.concatenate([load(span) for span in where], axis=1)
        basis = jnp.concatenate([ref[k] for k in range(len(blocks))], axis=0)
        acc_ref[...] += jnp.dot(field, basis, preferred_element_type=jnp.float32)


NEAR = tuple(tuple((dz, dy) for dy in (0, 3, 1, 2)) for dz in (0, 7, 1, 6, 2, 5, 3))
FAR = (((4, 0), (4, 3)), ((4, 1), (4, 2)))


def near_kernel(place_ref, *refs):
    blocks, pieces, acc_ref = refs[:8], refs[8:-1], refs[-1]

    def load(span):
        return jnp.concatenate([ref[:, span] for ref in blocks], axis=0)

    product_of(place_ref, load, NEAR, pieces, acc_ref)


def near_product(place, fields, pieces):
    rows = sum(field.shape[0] for field in fields)
    width = pieces[0].shape[-1]
    return pl.pallas_call(
        near_kernel,
        out_shape=jax.ShapeDtypeStruct((rows, width), jnp.float32),
        in_specs=[SMEM] + [VMEM] * (8 + len(pieces)),
        out_specs=VMEM,
        compiler_params=pltpu.CompilerParams(vmem_limit_bytes=GRANT),
        cost_estimate=pl.CostEstimate(
            flops=2 * rows * 3072 * width, bytes_accessed=8 << 20, transcendentals=0
        ),
        name="near_product",
    )(place, *fields, *pieces)


def first_kernel(mix_ref, place_ref, *refs):
    blocks, pieces, (near_ref, out_ref, acc_ref, tmp_ref) = refs[:8], refs[8:-4], refs[-4:]
    rows = blocks[0].shape[0]
    lo = place_ref[0]

    def load(span):
        return jnp.concatenate([ref[:, span] for ref in blocks], axis=0)

    product_of(place_ref, load, FAR, pieces, acc_ref)
    acc_ref[...] += near_ref[...]
    for a in range(4):
        for group in range(2):
            mixed = sum(
                mix_ref[group * 4 + t, a]
                * acc_ref[(group * 4 + t) * rows : (group * 4 + t + 1) * rows, :]
                for t in range(4)
            )
            at = lo if group == 0 else 1 - lo
            tmp_ref[pl.ds(pl.multiple_of(at * rows, rows), rows), :] = mixed
        out_ref[:, a * 2 * rows : (a + 1) * 2 * rows] = tmp_ref[...].T.astype(jnp.bfloat16)


def first_product(mix, place, fields, pieces, near):
    rows = fields[0].shape[0]
    width = near.shape[-1]
    return pl.pallas_call(
        first_kernel,
        out_shape=jax.ShapeDtypeStruct((width, 8 * rows), jnp.bfloat16),
        in_specs=[SMEM, SMEM] + [VMEM] * (9 + len(pieces)),
        out_specs=VMEM,
        scratch_shapes=[
            pltpu.VMEM((8 * rows, width), jnp.float32),
            pltpu.VMEM((2 * rows, width), jnp.float32),
        ],
        compiler_params=pltpu.CompilerParams(vmem_limit_bytes=GRANT),
        cost_estimate=pl.CostEstimate(
            flops=2 * 8 * rows * 1024 * width, bytes_accessed=4 << 20, transcendentals=0
        ),
        name="first_product",
    )(mix, place, *fields, *pieces, near)


def load_bands(fields, which, span):
    return jnp.concatenate(
        [ref[part, which, :, span] for ref in fields for part in range(ref.shape[0])], axis=0
    )


def natural_place(slice_ref, half_of, block):
    return pl.multiple_of((slice_ref[block] * 2 + half_of) * 8, 8)


def moved_columns(half):
    source = lax.broadcasted_iota(jnp.int32, (128, 256), 0)
    target = lax.broadcasted_iota(jnp.int32, (128, 256), 1)
    return (target == (source // 8) * 16 + half * 8 + lax.rem(source, 8)).astype(jnp.float32)


def sent_kernel(place_ref, *refs):
    count = len(refs) - len(NEAR + FAR) - 2
    fields, pieces, (sent_ref, acc_ref) = refs[:count], refs[count:-2], refs[-2:]
    which = 1 - place_ref[0]
    product_of(
        place_ref, lambda span: load_bands(fields, which, span), NEAR + FAR, pieces, acc_ref
    )
    sent_ref[...] = acc_ref[...].astype(jnp.bfloat16)


def sent_rows(place, fields, pieces):
    count = sum(field.shape[0] * field.shape[2] for field in fields)
    total, width = fields[0].shape[-1], pieces[0].shape[-1]
    return pl.pallas_call(
        sent_kernel,
        out_shape=jax.ShapeDtypeStruct((count, width), jnp.bfloat16),
        in_specs=[SMEM] + [VMEM] * (len(fields) + len(pieces)),
        out_specs=VMEM,
        scratch_shapes=[pltpu.VMEM((count, width), jnp.float32)],
        compiler_params=pltpu.CompilerParams(vmem_limit_bytes=GRANT),
        cost_estimate=pl.CostEstimate(
            flops=2 * count * total * width, bytes_accessed=6 << 20, transcendentals=0
        ),
        name="sent_rows",
    )(place, *fields, *pieces)


def kept_kernel(place_ref, slice_ref, *refs):
    count = len(refs) - len(NEAR + FAR) - 6
    fields, pieces = refs[:count], refs[count:-6]
    sx_ref, sy_ref, white_ref, kept_ref, acc_ref, rows_ref = refs[-6:]
    lo = place_ref[0]
    product_of(place_ref, lambda span: load_bands(fields, lo, span), NEAR + FAR, pieces, acc_ref)
    for b in range(8):
        to = natural_place(slice_ref, lo if b < 4 else 1 - lo, b)
        for a in range(4):
            first = (b * 4 + a) * 8
            rows_ref[a, pl.ds(to, 8), :] = acc_ref[first : first + 8, :]
    chosen = moved_columns(lo)
    for block in range(rows_ref.shape[-1] // 128):
        span = slice(block * 256, block * 256 + 256)
        scale = sy_ref[:, :1] * sx_ref[:, span]
        for a in range(rows_ref.shape[0]):
            moved = jnp.dot(
                rows_ref[a, :, block * 128 : block * 128 + 128],
                chosen,
                precision=lax.Precision.HIGHEST,
            )
            kept_ref[a, :, span] = scale * moved - white_ref[:, a, span]


def kept_rows(place, slices, fields, pieces, sx, sy, white):
    count = sum(field.shape[0] * field.shape[2] for field in fields)
    total, width = fields[0].shape[-1], pieces[0].shape[-1]
    rows, times, columns = white.shape
    return pl.pallas_call(
        kept_kernel,
        out_shape=jax.ShapeDtypeStruct((times, rows, columns), jnp.float32),
        in_specs=[SMEM, SMEM] + [VMEM] * (len(fields) + len(pieces) + 3),
        out_specs=VMEM,
        scratch_shapes=[
            pltpu.VMEM((count, width), jnp.float32),
            pltpu.VMEM((times, rows, width), jnp.float32),
        ],
        compiler_params=pltpu.CompilerParams(vmem_limit_bytes=GRANT),
        cost_estimate=pl.CostEstimate(
            flops=2 * count * total * width, bytes_accessed=6 << 20, transcendentals=0
        ),
        name="kept_rows",
    )(place, slices, *fields, *pieces, sx, sy, white)


def gradient_kernel(place_ref, slice_ref, kept_ref, early_ref, late_ref, sx_ref, sy_ref, out_ref):
    lo = place_ref[0]
    chosen = moved_columns(1 - lo).astype(jnp.bfloat16)
    for block in range(early_ref.shape[-1] // 128):
        here = slice(block * 128, block * 128 + 128)
        span = slice(block * 256, block * 256 + 256)
        for ref, sources in ((early_ref, (0, 1, 4, 5, 6, 7)), (late_ref, (2, 3))):
            moved = jnp.dot(ref[:, here], chosen, preferred_element_type=jnp.float32)
            for k, b in enumerate(sources):
                to = natural_place(slice_ref, 1 - lo if b < 4 else lo, b)
                scale = sy_ref[pl.ds(to, 8), :1] * sx_ref[:, span]
                for a in range(4):
                    first = (k * 4 + a) * 8
                    out_ref[pl.ds(to, 8), a, span] = (
                        kept_ref[a, pl.ds(to, 8), span] + scale * moved[first : first + 8]
                    )


def whitened_gradient(place, slices, kept, early, late, sx, sy):
    times, rows, width = kept.shape
    return pl.pallas_call(
        gradient_kernel,
        out_shape=jax.ShapeDtypeStruct((rows, times, width), jnp.float32),
        in_specs=[SMEM, SMEM] + [VMEM] * 5,
        out_specs=VMEM,
        compiler_params=pltpu.CompilerParams(vmem_limit_bytes=GRANT),
        name="whitened_gradient",
    )(place, slices, kept, early, late, sx, sy)


def with_core(block):
    return block, shifted(block, "core", 1)


def local(event_counts, latent_mean, latent_var, eigen_basis, spectrum, correlation, whitened):
    hi, core = lax.axis_index("hi"), lax.axis_index("core")
    y, z, lo = (lax.axis_index(axis) for axis in ROW)
    time = hi * 2 + core
    ny, nz = lax.axis_size("y"), lax.axis_size("z")
    place = jnp.stack([lo, time, y, z]).astype(jnp.int32)

    other = shifted(eigen_basis, "lo", 1)
    pair = jnp.where(
        lo == 0,
        jnp.concatenate([eigen_basis, other]),
        jnp.concatenate([other, eigen_basis]),
    )
    mine = split_columns(place, pair)
    pseudo = moments(event_counts, latent_mean, latent_var).astype(jnp.bfloat16)[0]
    mine, pseudo = lax.optimization_barrier((mine, pseudo))
    before, after = shifted(pseudo, RING, 1), shifted(pseudo, RING, 3)
    block = jnp.stack([mine] + [shifted(mine, "y", step) for step in (1, 3, 2)])
    block, pseudo = lax.optimization_barrier((block, pseudo))
    own = lax.optimization_barrier(with_core(pseudo))
    far = shifted(own[0], RING, 2)

    flips = jnp.array([0, 1, 2, 3], jnp.int32)
    before_flip, after_flip = 2 * (1 - lo), 2 * lo
    crossed = jnp.stack([before_flip, before_flip + 1, after_flip, after_flip + 1])
    slices = lax.bitwise_xor(time, jnp.concatenate([flips, crossed])).astype(jnp.int32)
    swapped = jnp.concatenate([slices[:4], slices[6:], slices[4:6]])
    factor = time_factor(correlation[0], 4)
    mix = jnp.take(factor, slices, axis=0)
    root = jnp.sqrt(spectrum)
    sx = lax.dynamic_slice_in_dim(root, time * 1024, 1024, 0)[None]
    row = (y * nz + z) * 2 + lo
    sy = lax.dynamic_slice_in_dim(root.reshape(4, lax.axis_size(ROW), -1), row, 1, 1).reshape(-1, 1)
    sy = jnp.broadcast_to(sy, (sy.shape[0], 128))

    right, left = shifted(block, "z", 1), shifted(block, "z", nz - 1)
    pieces = [block, right, left]
    right, left, before, after = lax.optimization_barrier((right, left, before, after))
    before, after = with_core(before), with_core(after)
    right, left = shifted(right, "z", 1), shifted(left, "z", nz - 1)
    pieces += [right, left]
    right, left, far, own, mix, sx, sy = lax.optimization_barrier(
        (right, left, far, own, mix, sx, sy)
    )
    far = with_core(far)
    right, left = shifted(right, "z", 1), shifted(left, "z", nz - 1)
    pieces += [right, left]
    right, left, far, before, after = lax.optimization_barrier((right, left, far, before, after))
    last = [shifted(right[:2], "z", 1), shifted(left[2:], "z", nz - 1)]

    fields = (*own, *far, *before, *after)
    near = near_product(place, fields, pieces)
    partial_y = first_product(mix, place, fields, last, near)
    pieces += last

    modes, width = partial_y.shape
    sent = partial_y.reshape(ny * nz, modes // (ny * nz), width)
    got = lax.all_to_all(sent, ("y", "z"), 0, 0, tiled=True)
    group = modes // (2 * ny * nz)
    got = got.reshape(ny * nz, 2, group, 2, 2, width // 4)
    got = got.transpose(3, 1, 4, 2, 0, 5).reshape(2, 2, 2 * group, -1)
    own, before, after = with_core(got), shifted(got, RING, 1), shifted(got, RING, 3)
    before, after, far = lax.optimization_barrier((before, after, (before[:1], after[1:])))
    far = [shifted(far[0], RING, 1), shifted(far[1], RING, 3)]
    own, before, after = lax.optimization_barrier((own, before, after))
    before, after = with_core(before), with_core(after)
    early = sent_rows(place, (*own, *before, *after), pieces)
    far, early = lax.optimization_barrier((far, early))
    far = (*far, *(shifted(half, "core", 1) for half in far))
    late, early = lax.optimization_barrier((sent_rows(place, far, pieces), early))
    got_late, got_early = shifted(late, "lo", 1), shifted(early, "lo", 1)
    white = whitened.reshape(-1, *whitened.shape[3:])
    kept = kept_rows(place, slices, (*own, *far, *before, *after), pieces, sx, sy, white)
    gradient = whitened_gradient(place, swapped, kept, got_early, got_late, sx, sy)
    return gradient.reshape(whitened.shape)


def solution(mesh):
    finer = Mesh(mesh.devices.reshape(2, 2, 4, 8, 2), ("hi", "core", "y", "z", "lo"))
    placed = (
        P(TM, ROW, None),
        P(TM, ROW, None),
        P(TM, ROW, None),
        P(ROW, TM),
        P(),
        P(),
        P(None, ROW, None, None, TM),
    )
    return jax.shard_map(
        local,
        mesh=finer,
        in_specs=placed,
        out_specs=P(None, ROW, None, None, TM),
        check_vma=False,
    )
```
